32 devices in a mesh: seq: 2 (over x), tensor: 16 (over z, y, core).
Axes of the slice: x: 2, y: 2, z: 4, core: 2. Of those that a mesh axis runs over, the one named last changes fastest.
Arguments:
- tokens: bfloat16 [512, 4096], P(('seq', 'tensor')), may hold values from -6 to 6
- lengths: int32 [6], replicated, may hold values from 1 to 256, 512 in all
- proj_zx: bfloat16 [4096, 2, 8192], P(None, None, 'tensor'), may hold values from -0.09375 to 0.09375
- proj_bc: bfloat16 [4096, 2, 1024], P(None, None, 'tensor'), may hold values from -0.09375 to 0.09375
- proj_dt: bfloat16 [4096, 128], P(None, 'tensor'), may hold values from -0.09375 to 0.09375
- conv_x: float32 [4, 8192], P(None, 'tensor'), may hold values from -3 to 3
- conv_bc: float32 [4, 2, 1024], P(None, None, 'tensor'), may hold values from -3 to 3
- bias_x: float32 [8192], P('tensor'), may hold values from -0.5 to 0.5
- bias_bc: float32 [2, 1024], P(None, 'tensor'), may hold values from -0.5 to 0.5
- dt_bias: float32 [128], P('tensor'), may hold values from -7 to -3
- decay_rate: float32 [128], P('tensor'), may hold values from 0.02 to 1
- skip_gain: float32 [128], P('tensor'), may hold values from 0.5 to 1.5
- proj_out: bfloat16 [8192, 4096], P('tensor'), may hold values from -0.0625 to 0.0625
Outputs:
- mixed: bfloat16 [512, 4096], P(('seq', 'tensor'))
- final_states: float32 [6, 128, 64, 128], P(None, 'tensor')
The draws below stay inside these ranges and needn't reach their ends.
Inputs may be any that keep to these rules, and one draw needn't show every extreme that they name: `lengths`: the 6 requests lie back to back in the stream in this order and fill it exactly; the longest has exactly 256 tokens.
All inputs are finite; a program needn't handle non-finite values.
Results may differ from the reference program's by a relative error of at most 0.0074.
Values may be sent and summed in bfloat16 or wider, within the bound.
A program may use at most 128 MiB of HBM per device.

```python
import math
import jax
import jax.numpy as jnp
import numpy as np
from jax import lax

D = 4096
HEADS = 128
HEAD = 64
GROUPS = 8
STATE = 128
KCONV = 4
INNER = 8192
NSEG = 6
TOKENS = 512


def levels(own_key, shape, split, low, top_value):
    factor_of = 1.0
    for position, parts in split:
        draws = jax.random.uniform(jax.random.fold_in(jax.random.fold_in(own_key, 6), position), (parts,), jnp.float32, low / len(split), top_value / len(split))
        factor_of = factor_of * jnp.repeat(jnp.exp(draws), shape[position] // parts).reshape((-1,) + (1,) * (len(shape) - 1 - position))
    return factor_of


def profile(amount, total, reach, slope):
    loads = [(1 << 20) // math.isqrt(grade ** slope) + 1 for grade in range(2, amount + 1)]
    surplus, holding = total - reach - (amount - 1), [1] * (amount - 1)
    while surplus > 0:
        movable = [i for i in range(amount - 1) if holding[i] < reach]
        mass, remaining = sum([loads[i] for i in movable]), surplus
        for i in movable:
            extra = min(reach - holding[i], max(1, remaining * loads[i] // mass), surplus)
            holding[i] = holding[i] + extra
            surplus = surplus - extra
    return np.array([reach] + holding)


def ragged_sizes(rng, amount, total, reach, lean):
    if amount == 2:
        one = jax.random.randint(rng, (), max(1, total - reach), min(reach, total - 1) + 1)
        return jnp.stack([one, total - one])
    sizes = jnp.asarray(profile(amount, total, reach, lean), jnp.int32)
    twos = (amount - 1) // 2
    source_of, taker = sizes[1:1 + 2 * twos:2], sizes[2:2 + 2 * twos:2]
    slack = jnp.minimum(source_of - 1, reach - taker)
    moved = jax.random.randint(jax.random.fold_in(rng, 1), (twos,), 0, 1 << 20) % (slack + 1)
    sizes = sizes.at[1:1 + 2 * twos:2].set(source_of - moved).at[2:2 + 2 * twos:2].set(taker + moved)
    return sizes[jax.random.permutation(jax.random.fold_in(rng, 2), amount)]


def normal_values(own_key, shape, width, most, cuts=(), held_as=jnp.bfloat16):
    entries = jax.random.normal(own_key, shape, jnp.float32) * width
    if len(cuts) > 0:
        entries = levels(own_key, shape, cuts, -0.22, 0.18) * entries
    return jnp.clip(entries, min=-most, max=most).astype(held_as)


def setup_inputs(seed: int = 0) -> dict:
    splits = jax.random.split(jax.random.key(seed), 14)
    tokens = normal_values(splits[0], (TOKENS, D), 1.0, 6.0, ((0, 32),))
    lengths = ragged_sizes(splits[1], NSEG, TOKENS, TOKENS // 2, 2).astype(jnp.int32)
    proj_zx = normal_values(splits[2], (D, 2, INNER), D ** -0.5, 0.09375, ((2, 16),))
    proj_bc = normal_values(splits[3], (D, 2, GROUPS * STATE), D ** -0.5, 0.09375, ((2, 16),))
    proj_dt = normal_values(splits[4], (D, HEADS), D ** -0.5, 0.09375, ((1, 16),))
    conv_x = normal_values(splits[5], (KCONV, INNER), KCONV ** -0.5, 3.0, ((1, 16),), jnp.float32)
    conv_bc = normal_values(splits[6], (KCONV, 2, GROUPS * STATE), KCONV ** -0.5, 3.0, ((2, 16),), jnp.float32)
    bias_x = jnp.clip(jax.random.uniform(splits[7], (INNER,), jnp.float32, -0.5, 0.5) * levels(splits[7], (INNER,), ((0, 16),), -0.4, 0.0), -0.5, 0.5)
    bias_bc = jnp.clip(jax.random.uniform(splits[8], (2, GROUPS * STATE), jnp.float32, -0.5, 0.5) * levels(splits[8], (2, GROUPS * STATE), ((1, 16),), -0.4, 0.0), -0.5, 0.5)
    dt_bias = jnp.clip(-7.0 + 4.0 * jax.random.uniform(splits[9], (HEADS,), jnp.float32) ** levels(splits[9], (HEADS,), ((0, 16),), -0.2, 0.2), -7.0, -3.0)
    decay_rate = jnp.clip(jnp.exp(math.log(1.0) - 3.912023 * jax.random.uniform(splits[10], (HEADS,), jnp.float32) ** levels(splits[10], (HEADS,), ((0, 16),), -0.2, 0.2)), 0.02, 1.0)
    skip_gain = jnp.clip(0.5 + 1.0 * jax.random.uniform(splits[11], (HEADS,), jnp.float32) ** levels(splits[11], (HEADS,), ((0, 16),), -0.2, 0.2), 0.5, 1.5)
    proj_out = normal_values(splits[12], (INNER, D), INNER ** -0.5, 0.0625, ((0, 16),))
    return {"tokens": tokens, "lengths": lengths, "proj_zx": proj_zx, "proj_bc": proj_bc, "proj_dt": proj_dt, "conv_x": conv_x, "conv_bc": conv_bc, "bias_x": bias_x, "bias_bc": bias_bc, "dt_bias": dt_bias, "decay_rate": decay_rate, "skip_gain": skip_gain, "proj_out": proj_out}


def conv_segment(pre_conv, taps, offset, positions, seg_start):
    values = pre_conv.astype(jnp.float32)
    count = values.shape[0]
    result = jnp.zeros_like(values) + offset[None, :]
    for lag_index in range(taps.shape[0]):
        shifted = jnp.pad(values, ((lag_index, 0), (0, 0)))[:count]
        keep_mask = (positions - lag_index >= seg_start).astype(jnp.float32)
        result = result + taps[lag_index][None, :] * shifted * keep_mask[:, None]
    return result


def reference(tokens, lengths, proj_zx, proj_bc, proj_dt, conv_x, conv_bc, bias_x, bias_bc, dt_bias, decay_rate, skip_gain, proj_out):
    total = tokens.shape[0]
    zx_all = jnp.dot(tokens, proj_zx.reshape(D, 2 * INNER), preferred_element_type=jnp.float32)
    gate_in = zx_all[:, :INNER].astype(jnp.bfloat16)
    x_in = zx_all[:, INNER:].astype(jnp.bfloat16)
    bc_in = jnp.dot(tokens, proj_bc.reshape(D, 2 * GROUPS * STATE), preferred_element_type=jnp.float32).astype(jnp.bfloat16)
    step_size = jax.nn.softplus(jnp.dot(tokens, proj_dt, preferred_element_type=jnp.float32) + dt_bias[None, :])
    positions = jnp.arange(total, dtype=jnp.int32)
    bounds = jnp.cumsum(lengths).astype(jnp.int32)
    reached = bounds[None, :] <= positions[:, None]
    segment = jnp.sum(reached.astype(jnp.int32), axis=1).astype(jnp.int32)
    seg_start = jnp.max(jnp.where(reached, bounds[None, :], 0), axis=1).astype(jnp.int32)
    x_conv = jax.nn.silu(conv_segment(x_in, conv_x, bias_x, positions, seg_start)).astype(jnp.bfloat16)
    bc_conv = jax.nn.silu(conv_segment(bc_in, conv_bc.reshape(KCONV, 2 * GROUPS * STATE), bias_bc.reshape(2 * GROUPS * STATE), positions, seg_start)).astype(jnp.bfloat16)
    bc_float = bc_conv.astype(jnp.float32).reshape(total, 2, GROUPS, STATE)
    x_heads = x_conv.astype(jnp.float32).reshape(total, HEADS, HEAD)
    per_group = HEADS // GROUPS
    is_start = positions == seg_start
    last_pos = jnp.take(bounds, segment) - 1
    is_end = positions == last_pos

    def advance(carry, item):
        state, finals = carry
        step_now, x_now, b_now, c_now, start_now, end_now, seg_now = item
        keep = jnp.where(start_now, 0.0, 1.0).astype(jnp.float32)
        decay = jnp.exp(-decay_rate * step_now) * keep
        b_rep = jnp.repeat(b_now, per_group, axis=0)
        c_rep = jnp.repeat(c_now, per_group, axis=0)
        state = state * decay[:, None, None] + (step_now[:, None] * x_now)[:, :, None] * b_rep[:, None, :]
        y_now = jnp.einsum('hpn,hn->hp', state, c_rep, precision=lax.Precision.HIGHEST) + skip_gain[:, None] * x_now
        current = lax.dynamic_index_in_dim(finals, seg_now, 0, keepdims=False)
        finals = lax.dynamic_update_index_in_dim(finals, jnp.where(end_now, state, current), seg_now, 0)
        return (state, finals), y_now

    init = (jnp.zeros((HEADS, HEAD, STATE), jnp.float32), jnp.zeros((NSEG, HEADS, HEAD, STATE), jnp.float32))
    items = (step_size, x_heads, bc_float[:, 0], bc_float[:, 1], is_start, is_end, segment)
    (state_last, final_states), y_all = lax.scan(advance, init, items)
    gate_values = jax.nn.silu(gate_in.astype(jnp.float32)).reshape(total, HEADS, HEAD)
    gated = (y_all * gate_values).reshape(total, INNER).astype(jnp.bfloat16)
    mixed = jnp.dot(gated, proj_out, preferred_element_type=jnp.float32).astype(jnp.bfloat16)
    return mixed, final_states
```

```python
import jax
import jax.numpy as jnp
from jax import lax
from jax.experimental import pallas as pl
from jax.experimental.pallas import tpu as pltpu
from jax.sharding import PartitionSpec as P

GROUPS = 8


def partner_2(value, axis, bit):
    mask = 2**bit
    pairs = [(source, source ^ mask) for source in range(lax.axis_size(axis))]
    return lax.ppermute(value, axis, pairs)


def passed_along(block, axis, distance):
    devices = range(lax.axis_size(axis))
    route = [(i - distance, i) for i in devices if i - distance in devices]
    return lax.ppermute(block, axis, route)


def group_columns(bc_own, tensor_index, steps_count):
    collected = bc_own
    for bit_number in range(steps_count):
        partner = partner_2(collected, "tensor", bit_number)
        upper = tensor_index // 2**bit_number % 2
        low_first = jnp.concatenate([collected, partner], axis=2)
        high_first = jnp.concatenate([partner, collected], axis=2)
        collected = jnp.where(upper == 0, low_first, high_first)
    return collected


def body(
    tokens,
    lengths,
    proj_zx,
    proj_bc,
    proj_dt,
    conv_x,
    conv_bc,
    bias_x,
    bias_bc,
    dt_bias,
    decay_rate,
    skip_gain,
    proj_out,
):
    highest = lax.Precision.HIGHEST
    tensor_size = lax.axis_size("tensor")
    rows_dev = tokens.shape[0]
    shard_len = rows_dev * tensor_size
    seq_index = lax.axis_index("seq")
    tensor_index = lax.axis_index("tensor")
    heads_dev = decay_rate.shape[0]
    width_zx = proj_zx.shape[2]
    head_size = width_zx // heads_dev
    cols_bc = proj_bc.shape[2]
    taps_count = conv_x.shape[0]
    model_width = tokens.shape[1]
    zx_flat = proj_zx.reshape(model_width, 2 * width_zx)
    bc_flat = proj_bc.reshape(model_width, 2 * cols_bc)
    piece = lax.all_gather(tokens, "tensor", axis=0, tiled=True)
    projected = jnp.concatenate(
        [
            jnp.dot(piece, zx_flat, preferred_element_type=jnp.float32),
            jnp.dot(piece, bc_flat, preferred_element_type=jnp.float32),
            jnp.dot(piece, proj_dt, preferred_element_type=jnp.float32),
        ],
        axis=1,
    )
    gate_in = projected[:, :width_zx].astype(jnp.bfloat16)
    conv_in = projected[:, width_zx : 2 * width_zx + 2 * cols_bc].astype(jnp.bfloat16)
    step_size = jax.nn.softplus(projected[:, 2 * width_zx + 2 * cols_bc :] + dt_bias[None, :])
    row_ids = jnp.arange(shard_len, dtype=jnp.int32)
    positions = seq_index * shard_len + row_ids
    later = jnp.arange(lengths.shape[0])
    bounds = jnp.sum(jnp.where(later[None, :] <= later[:, None], lengths[None, :], 0), axis=1)
    reached = bounds[None, :] <= positions[:, None]
    segment = jnp.sum(reached.astype(jnp.int32), axis=1)
    seg_start = jnp.max(jnp.where(reached, bounds[None, :], 0), axis=1)
    edge_rows = conv_in[shard_len - (taps_count - 1) :]
    before = passed_along(edge_rows, "seq", 1)
    extended = jnp.concatenate([before, conv_in], axis=0)
    conv_taps = jnp.concatenate([conv_x, conv_bc.reshape(taps_count, 2 * cols_bc)], axis=1)
    conv_offset = jnp.concatenate([bias_x, bias_bc.reshape(2 * cols_bc)])
    convolved = jnp.zeros((shard_len, conv_taps.shape[1]), jnp.float32) + conv_offset[None, :]
    for lag_index in range(taps_count):
        lagged = extended[
            taps_count - 1 - lag_index : taps_count - 1 - lag_index + shard_len
        ].astype(jnp.float32)
        keep_mask = (positions - lag_index >= seg_start).astype(jnp.float32)
        convolved = convolved + conv_taps[lag_index][None, :] * lagged * keep_mask[:, None]
    activated = jax.nn.silu(convolved).astype(jnp.bfloat16)
    x_conv = activated[:, :width_zx]
    bc_own = activated[:, width_zx:].reshape(shard_len, 2, cols_bc)
    per_group = tensor_size // GROUPS
    steps_count = per_group.bit_length() - 1
    bc_group = group_columns(bc_own, tensor_index, steps_count).astype(jnp.float32)
    state_in_proj = bc_group[:, 0]
    state_out_proj = bc_group[:, 1]
    x_float = x_conv.astype(jnp.float32).reshape(shard_len, heads_dev, head_size)
    log_decay = -decay_rate[None, :] * step_size
    lower = (row_ids[:, None] >= row_ids[None, :]).astype(jnp.float32)
    cumulative = jnp.dot(lower, log_decay, precision=highest)
    cumulative_t = cumulative.T
    valid = (segment[:, None] == segment[None, :]) & (row_ids[:, None] >= row_ids[None, :])
    spread = cumulative_t[:, :, None] - cumulative_t[:, None, :]
    decay_matrix = jnp.where(valid[None], jnp.exp(jnp.where(valid[None], spread, 0.0)), 0.0)
    scores = jnp.dot(state_out_proj, state_in_proj.T, precision=highest)
    mixing = decay_matrix * scores[None] * step_size.T[:, None, :]
    y_local = jnp.einsum("hts,shp->thp", mixing, x_float, precision=highest)
    before_pos = seq_index * shard_len - 1
    seg_before = jnp.sum((bounds <= before_pos).astype(jnp.int32))
    carried = (segment == seg_before).astype(jnp.float32)
    entry_gain = jnp.exp(cumulative) * carried[:, None]
    n_seg = lengths.shape[0]
    end_rows = bounds - 1 - seq_index * shard_len
    inside = (end_rows >= 0) & (end_rows < shard_len)
    target_rows = jnp.concatenate([end_rows, jnp.full((1,), shard_len - 1, jnp.int32)])
    target_seg = jnp.concatenate([jnp.arange(n_seg, dtype=jnp.int32), segment[shard_len - 1 :]])
    target_ok = jnp.concatenate([inside, jnp.ones((1,), bool)])
    picker = (row_ids[None, :] == target_rows[:, None]).astype(jnp.float32)
    cum_end = jnp.dot(picker, cumulative, precision=highest)
    reach = (
        target_ok[:, None]
        & (row_ids[None, :] <= target_rows[:, None])
        & (segment[None, :] == target_seg[:, None])
    )
    gap_end = cum_end[:, :, None] - cumulative_t[None, :, :]
    end_weight = (
        jnp.where(reach[:, None, :], jnp.exp(jnp.where(reach[:, None, :], gap_end, 0.0)), 0.0)
        * step_size.T[None]
    )
    states = jnp.einsum("khs,shp,sn->khpn", end_weight, x_float, state_in_proj, precision=highest)
    end_local = states[:n_seg]
    shard_state = states[n_seg]
    end_gain = jnp.where((target_ok & (target_seg == seg_before))[:, None], jnp.exp(cum_end), 0.0)
    shard_gain = end_gain[n_seg]
    end_gain_seg = end_gain[:n_seg]
    gathered = (
        lax.all_gather(shard_gain[None], "seq", axis=0, tiled=True),
        lax.all_gather(shard_state[None], "seq", axis=0, tiled=True),
        lax.all_gather(end_gain_seg[None], "seq", axis=0, tiled=True),
        lax.all_gather(end_local[None], "seq", axis=0, tiled=True),
    )
    gains_all, states_all, egains_all, elocal_all = gathered

    def fold_step(carry, item):
        gain_now, state_now = item
        return (gain_now[:, None, None] * carry + state_now, carry)

    last_state, incoming = lax.scan(
        fold_step, jnp.zeros(shard_state.shape, jnp.float32), (gains_all, states_all)
    )
    state_entry = lax.dynamic_index_in_dim(incoming, seq_index, 0, keepdims=False)
    final_states = jnp.sum(elocal_all + egains_all[:, :, :, None, None] * incoming[:, None], axis=0)
    y_entry = (
        jnp.einsum("tn,hpn->thp", state_out_proj, state_entry, precision=highest)
        * entry_gain[:, :, None]
    )
    y_total = y_local + y_entry + skip_gain[None, :, None] * x_float
    gate_values = jax.nn.silu(gate_in.astype(jnp.float32)).reshape(shard_len, heads_dev, head_size)
    gated = (y_total * gate_values).reshape(shard_len, width_zx).astype(jnp.bfloat16)
    mixed = lax.psum_scatter(
        jnp.dot(gated, proj_out, preferred_element_type=jnp.float32),
        "tensor",
        scatter_dimension=0,
        tiled=True,
    )
    return (mixed.astype(jnp.bfloat16), final_states)


F32 = jnp.float32
BF16 = jnp.bfloat16
ROWS = 16
LEN = 256
WIDE = 4096
CHAN = 512
STATES = 128
HIGH = lax.Precision.HIGHEST
NT = (((1,), (1,)), ((), ()))
TN = (((0,), (0,)), ((), ()))
CUTS = (1024, 1024, 1024, 1024)
HALF = (1, 2)
LEAD = 2
SLABS = (256, 512, 512, 512, 512, 512, 512, 512, 256)
BEHIND = 4


def starts(widths):
    return tuple(sum(widths[:i]) for i in range(len(widths)))


CUT_AT = starts(CUTS)
SLAB_AT = starts(SLABS)
NQ = len(CUTS)
NR = len(SLABS)


def remote(src, dst, send, recv, **device):
    return pltpu.make_async_remote_copy(
        src_ref=src,
        dst_ref=dst,
        send_sem=send,
        recv_sem=recv,
        device_id=device,
        device_id_type=pl.DeviceIdType.MESH,
    )


def segment_of(bounds, pos):
    total = jnp.zeros(pos.shape, jnp.int32)
    for bound in bounds:
        total = total + (bound <= pos).astype(jnp.int32)
    return total


def layer_kernel(
    lengths,
    tok_in,
    zx_in,
    bc_in,
    dt_in,
    conv_x,
    bias_x,
    conv_bc,
    bias_bc,
    dt_bias,
    rate_in,
    skip_in,
    out_in,
    mixed,
    finals,
    tok,
    zx_raw,
    w_zx,
    w_bc,
    w_out,
    t_conv,
    t_bias,
    gate,
    ext,
    act,
    steps,
    fin,
    acc,
    ent_out,
    ent_in,
    keep,
    send_a,
    recv_a,
    send_b,
    recv_b,
    send_c,
    recv_c,
    load_sem,
    zx_sem,
    up_s,
    down_s,
    y_s,
    e_s,
    got,
    sib_s,
    sib_r,
    misc_s,
    misc_r,
    ent_s,
    ent_r,
    rsa_s,
    rsa_r,
    rsb_s,
    rsb_r,
    rsc_s,
    rsc_r,
):
    s = lax.axis_index("seq")
    me = lax.axis_index("tensor")
    z = me // 4
    y = (me // 2) % 2
    c = me % 2
    oy = 1 - y
    oc = 1 - c
    sib = z * 4 + y * 2 + oc
    ypal = z * 4 + oy * 2 + c
    zpal = [((z + d) % 4) * 4 + y * 2 + c for d in range(4)]
    pair = (z + 1 - 2 * (z % 2)) * 4 + y * 2 + c
    other = 1 - s

    own = pltpu.make_async_copy(tok_in, tok.at[z, y, c], load_sem.at[0])
    own.start()
    zx_loads = []
    for q in range(NQ):
        rows = pl.ds(CUT_AT[q], CUTS[q])
        load = pltpu.make_async_copy(zx_in.at[rows], zx_raw.at[rows], zx_sem.at[q])
        load.start()
        zx_loads.append(load)
    bc_load = pltpu.make_async_copy(bc_in, w_bc.at[:, c], load_sem.at[1])
    bc_load.start()
    tap_load = pltpu.make_async_copy(conv_bc, t_conv.at[c], load_sem.at[2])
    tap_load.start()
    off_load = pltpu.make_async_copy(bias_bc, t_bias.at[c], load_sem.at[5])
    off_load.start()
    out_load = pltpu.make_async_copy(out_in, w_out, load_sem.at[3])
    out_load.start()
    ext[:16] = jnp.zeros((16, CHAN + 256), BF16)

    barrier = pltpu.get_barrier_semaphore()
    for pal in [sib, ypal] + zpal[1:]:
        pl.semaphore_signal(
            barrier, inc=1, device_id={"tensor": pal}, device_id_type=pl.DeviceIdType.MESH
        )
    pl.semaphore_signal(
        barrier, inc=1, device_id={"seq": other}, device_id_type=pl.DeviceIdType.MESH
    )
    pl.semaphore_wait(barrier, 6)

    started = []

    def go(copy):
        copy.start()
        started.append(copy)
        return copy

    guarded = {}

    def maybe(name, condition, copy):
        pl.when(condition)(copy.start)
        guarded.setdefault(name, (condition, []))[1].append(copy)

    def hop(zz, yy, q, send, device):
        ref = tok.at[zz, yy, c, :, pl.ds(CUT_AT[q], CUTS[q])]
        return remote(ref, ref, send, got.at[zz, yy, q], tensor=device)

    def landed(zz, yy, q):
        hop(zz, yy, q, y_s.at[0, q], ypal).wait_recv()

    above = zpal[1]
    below = zpal[3]

    def launch(q):
        maybe("up0", z < 3, hop(z, y, q, up_s.at[0, q], above))
        maybe("down0", z > 0, hop(z, y, q, down_s.at[0, q], below))
        go(hop(z, y, q, y_s.at[0, q], ypal))

    def chain(k, q):
        ways = ((-1, z >= k, z < 3, above, up_s, 0), (1, z + k <= 3, z > 0, below, down_s, 3))
        for sign, have, more, ahead, sends, first in ways:
            zz = (z + sign * k + 4) % 4

            @pl.when(have)
            def _():
                landed(zz, y, q)

            if k < 3:
                maybe((sign, k), have & more, hop(zz, y, q, sends.at[k, q], ahead))
            over = have
            name = ("y", sign, k)
            if k == 1 and q in HALF:
                over = have & (z % 2 == (1 + sign) // 2)
                name = ("half", sign)
            maybe(name, over, hop(zz, y, q, y_s.at[first + k, q], ypal))

    def across(k, q):
        if k == 0:
            landed(z, oy, q)
            if q in HALF:
                go(hop(z, oy, q, e_s.at[q], pair))
            return
        for sign, have in ((-1, z >= k), (1, z + k <= 3)):
            zz = (z + sign * k + 4) % 4

            @pl.when(have)
            def _():
                landed(zz, oy, q)

    def share(q, core):
        ref = tok.at[:, :, core, :, pl.ds(CUT_AT[q], CUTS[q])]
        return remote(ref, ref, sib_s.at[q], sib_r.at[q], tensor=sib)

    own.wait()
    for q in range(min(LEAD, NQ)):
        launch(q)
    bc_send = go(remote(bc_in, w_bc.at[:, c], misc_s.at[0], misc_r.at[0], tensor=sib))
    tap_send = go(remote(conv_bc, t_conv.at[c], misc_s.at[1], misc_r.at[1], tensor=sib))
    off_send = go(remote(bias_bc, t_bias.at[c], misc_s.at[5], misc_r.at[5], tensor=sib))

    def split(q, part):
        size = CUTS[q] // 4

        def run():
            if part == 0:
                zx_loads[q].wait()

            @pl.loop(0, size // 128)
            def _(j):
                at = pl.multiple_of(CUT_AT[q] + part * size + j * 128, 128)
                rows = pl.ds(at, 128)
                both = pltpu.einshape("abc->bac", zx_raw[rows])
                w_zx[rows, :CHAN] = both[0]
                w_zx[rows, CHAN:] = both[1]

        return run

    def chunk(q):
        at = slice(CUT_AT[q], CUT_AT[q] + CUTS[q])
        return tok[:, :, :, :, at].reshape(LEN, CUTS[q])

    def add_to(q, rows, cols, product):
        if q == 0:
            acc[rows, cols] = product
        else:
            acc[rows, cols] += product

    def dot_zx(q, i):
        def run():
            cols = slice(i * 256, i * 256 + 256)
            at = slice(CUT_AT[q], CUT_AT[q] + CUTS[q])
            add_to(
                q,
                slice(0, LEN),
                cols,
                jnp.dot(chunk(q), w_zx[at, cols], preferred_element_type=F32),
            )

        return run

    def dot_bc(q):
        def run():
            if q == 0:
                for load in (bc_load, tap_load, off_load):
                    load.wait()
                for sent in (bc_send, tap_send, off_send):
                    sent.wait_recv()
            at = slice(CUT_AT[q], CUT_AT[q] + CUTS[q])
            weights = w_bc[:, :, :, at].reshape(256, CUTS[q])
            add_to(
                q,
                slice(0, LEN),
                slice(1024, 1280),
                lax.dot_general(chunk(q), weights, NT, preferred_element_type=F32),
            )

        return run

    def dot_dt(q):
        def run():
            at = slice(CUT_AT[q], CUT_AT[q] + CUTS[q])
            add_to(
                q,
                slice(0, 8),
                slice(1280, 1280 + LEN),
                lax.dot_general(dt_in[:, at], chunk(q), NT, preferred_element_type=F32),
            )

        return run

    last = NQ - 1
    for t in range(NQ + 4):
        if t + LEAD < NQ:
            launch(t + LEAD)
        todo = []
        if t < NQ:
            todo = [split(t, part) for part in range(4)]
        if t >= 4:
            q = t - 4
            share(q, oc).wait_recv()
            todo += [dot_bc(q), dot_zx(q, 2), dot_zx(q, 3), dot_dt(q)]
            if q != last:
                todo += [dot_zx(q, 0), dot_zx(q, 1)]
        events = [(chain, k, t - k + 1) for k in (1, 2, 3)]
        events.insert(1, (across, 0, t))
        events += [(across, k, t - k) for k in (1, 2, 3)]
        events = [event for event in events if 0 <= event[2] < NQ]
        for i, (what, k, q) in enumerate(events):
            what(k, q)
            if what is across and k == 3:
                go(share(q, c))
            rest = len(events) - i
            for work in todo[: -(-len(todo) // rest)]:
                work()
            todo = todo[-(-len(todo) // rest) :]
        for work in todo:
            work()

    ext[16:, CHAN:] = acc[:, 1024:1280].astype(BF16)
    ext[16:, :CHAN] = acc[:, 512:1024].astype(BF16)
    halo = go(
        remote(ext.at[pl.ds(256, 16)], ext.at[pl.ds(0, 16)], misc_s.at[2], misc_r.at[2], seq=other)
    )
    head_row = lax.broadcasted_iota(jnp.int32, (8, LEN), 0)

    def by_head(ref, heads):
        values = jnp.zeros(heads.shape, F32)
        for h in range(8):
            values = jnp.where(heads == h, ref[h], values)
        return values

    rate = by_head(rate_in, head_row)
    dt_own = jax.nn.softplus(acc[:8, 1280 : 1280 + LEN] + by_head(dt_bias, head_row))
    steps[s] = dt_own
    step_send = go(remote(steps.at[s], steps.at[s], misc_s.at[3], misc_r.at[3], seq=other))
    n_seg = lengths.shape[0]
    bounds = []
    run_sum = jnp.int32(0)
    for k in range(n_seg):
        run_sum = run_sum + lengths[k]
        bounds.append(run_sum)
    base = s * LEN
    row = lax.broadcasted_iota(jnp.int32, (LEN, 128), 0)
    pos = row + base
    seg_start = jnp.zeros((LEN, 128), jnp.int32)
    for bound in bounds:
        seg_start = jnp.where(bound <= pos, jnp.maximum(seg_start, bound), seg_start)
    masks = [None] + [(pos - j >= seg_start).astype(F32) for j in range(1, 4)]
    inner = [None] + [jnp.where(row >= j, masks[j], 0.0) for j in range(1, 4)]

    ri = lax.broadcasted_iota(jnp.int32, (LEN, LEN), 0)
    ci = lax.broadcasted_iota(jnp.int32, (LEN, LEN), 1)
    upper = (ri <= ci).astype(F32)
    head_of = lax.broadcasted_iota(jnp.int32, (8, CHAN), 1) // 64
    spread = (head_of == lax.broadcasted_iota(jnp.int32, (8, CHAN), 0)).astype(F32)

    def cumulate(dt):
        return jnp.dot(-rate * dt, upper, precision=HIGH, preferred_element_type=F32)

    def widen(rows):
        return lax.dot_general(rows, spread, TN, precision=HIGH, preferred_element_type=F32)

    place = lax.broadcasted_iota(jnp.int32, (8, LEN), 1)
    seg_own = segment_of(bounds, place + base)
    seg_last = segment_of(bounds, jnp.full((8, LEN), LEN - 1, jnp.int32) + base)
    cum_r = cumulate(dt_own)
    into = jnp.exp(cum_r[:, LEN - 1 :] - cum_r) * dt_own * (seg_own == seg_last).astype(F32)
    into_wide = widen(into)

    def taps_for(i, row):
        if i < 4:
            cols = slice(i * 128, i * 128 + 128)
            return bias_x[:, cols] if row == 4 else conv_x[row : row + 1, cols]
        k = i - 4
        if row == 4:
            both = [t_bias[e, k : k + 1, :] for e in range(2)]
        else:
            both = [t_conv[e, row, k : k + 1, :] for e in range(2)]
        return jnp.concatenate(both, axis=1)

    def silu(v):
        return v * lax.logistic(v)

    ent_copy = []
    for i in (4, 0, 1, 2, 3, 5):
        cols = slice(i * 128, i * 128 + 128)
        v = ext[16:, cols].astype(F32)
        total = taps_for(i, 4) + taps_for(i, 0) * v
        for j in range(1, 4):
            total = total + taps_for(i, j) * pltpu.roll(v, j, 0) * inner[j]
        made = silu(total).astype(BF16)
        act[s, :, cols] = made
        if i < 4:
            x_in = (made.astype(F32) * into_wide[:, cols]).astype(BF16)
            ent_out[i] = lax.dot_general(
                act[s, :, CHAN : CHAN + STATES], x_in, TN, preferred_element_type=F32
            ).astype(BF16)
            ent_copy.append(
                go(remote(ent_out.at[i], ent_in.at[i], ent_s.at[i], ent_r.at[i], seq=other))
            )
    halo.wait_recv()

    @pl.when(s > 0)
    def _():
        for i in range(6):
            cols = slice(i * 128, i * 128 + 128)
            v = ext[:32, cols].astype(F32)
            total = taps_for(i, 4) + taps_for(i, 0) * v[16:]
            for j in range(1, 4):
                total = total + taps_for(i, j) * pltpu.roll(v, j, 0)[16:] * masks[j][:16]
            act[s, :16, cols] = silu(total).astype(BF16)

    seen = act.at[s, :, pl.ds(0, CHAN + STATES)]
    act_send = go(remote(seen, seen, misc_s.at[4], misc_r.at[4], seq=other))

    for i in range(2):
        cols = slice(i * 256, i * 256 + 256)
        at = slice(CUT_AT[last], CUT_AT[last] + CUTS[last])
        gate[:, cols] = (
            acc[:, cols] + jnp.dot(chunk(last), w_zx[at, cols], preferred_element_type=F32)
        ).astype(BF16)

    cum_c = cum_r.T
    seg_r = segment_of(bounds, ci + base)
    seg_c = segment_of(bounds, ri + base)
    valid = (seg_r == seg_c) & (ri >= ci)
    b_own = act[s, :, CHAN : CHAN + STATES]
    c_own = act[s, :, CHAN + STATES :]
    scores = lax.dot_general(c_own, b_own, NT, preferred_element_type=F32)
    scores = jnp.where(valid, scores, 0.0)
    lane = lax.broadcasted_iota(jnp.int32, (LEN, 128), 1)
    for g in range(4):
        cols = slice(g * 128, g * 128 + 128)
        x_pair = act[s, :, cols]
        halves = []
        for h in (2 * g, 2 * g + 1):
            gap = cum_c[:, h : h + 1] - cum_r[h : h + 1, :]
            mix = jnp.exp(jnp.where(valid, gap, 0.0)) * scores * dt_own[h : h + 1, :]
            halves.append(jnp.dot(mix.astype(BF16), x_pair, preferred_element_type=F32))
        acc[:, cols] = jnp.where(lane < 64, halves[0], halves[1])

    seg_before = segment_of(bounds, jnp.full((8, LEN), LEN - 1, jnp.int32))
    carried = ((seg_own == seg_before) & (s > 0)).astype(F32)
    gain = widen(jnp.exp(cum_r) * carried)
    skips = by_head(skip_in, head_of[:1])
    for i in range(4):
        cols = slice(i * 128, i * 128 + 128)
        ent_copy[i].wait_recv()
        y_all = acc[:, cols] + jnp.dot(c_own, ent_in[i], preferred_element_type=F32) * gain[:, cols]
        y_all = y_all + skips[:, cols] * act[s, :, cols].astype(F32)
        gate[:, cols] = (y_all * silu(gate[:, cols].astype(F32))).astype(BF16)
    out_load.wait()

    def part(zz, yy, cc):
        return pl.ds(pl.multiple_of(zz * 64 + yy * 32 + cc * 16, 16), 16)

    a_copy = []
    b_copy = []
    c_copy = []

    def slab(q):
        return slice(SLAB_AT[q], SLAB_AT[q] + SLABS[q]), pl.ds(SLAB_AT[q], SLABS[q])

    def to_sib(q):
        cols, at = slab(q)
        acc[:, cols] = jnp.dot(gate[...], w_out[:, cols], preferred_element_type=F32)
        for zz in range(4):
            for yy in range(2):
                send_a[zz, yy, :, cols] = acc[part(zz, yy, oc), cols].astype(BF16)
        src, dst = send_a.at[:, :, :, at], recv_a.at[:, :, :, at]
        a_copy.append(go(remote(src, dst, rsa_s.at[q], rsa_r.at[q], tensor=sib)))

    def to_pal(q):
        cols, at = slab(q)
        a_copy[q].wait_recv()
        for zz in range(4):
            send_b[zz, :, cols] = (
                acc[part(zz, oy, c), cols] + recv_a[zz, oy, :, cols].astype(F32)
            ).astype(BF16)
        src, dst = send_b.at[:, :, at], recv_b.at[:, :, at]
        b_copy.append(go(remote(src, dst, rsb_s.at[q], rsb_r.at[q], tensor=ypal)))
        for zz in range(4):
            keep[zz, :, cols] = acc[part(zz, y, c), cols] + recv_a[zz, y, :, cols].astype(F32)

    def to_line(q):
        cols, at = slab(q)
        b_copy[q].wait_recv()
        for d in (2, 1, 3):
            zz = (z + d) % 4
            send_c[d, :, cols] = (keep[zz, :, cols] + recv_b[zz, :, cols].astype(F32)).astype(BF16)
            src, dst = send_c.at[d, :, at], recv_c.at[d, :, at]
            c_copy.append(
                go(remote(src, dst, rsc_s.at[d, q], rsc_r.at[d, q], tensor=zpal[d]))
            )

    def finals_ready():
        step_send.wait_recv()
        act_send.wait_recv()
        cum_0 = cumulate(steps[0])
        cum_1 = cumulate(steps[1]) + cum_0[:, LEN - 1 :]
        seg_0 = segment_of(bounds, place)
        seg_1 = segment_of(bounds, place + LEN)
        ends_0 = jnp.zeros((8, LEN), F32)
        ends_1 = jnp.zeros((8, LEN), F32)
        for k in range(n_seg):
            spot_0 = (place == bounds[k] - 1).astype(F32) * cum_0
            spot_1 = (place + LEN == bounds[k] - 1).astype(F32) * cum_1
            end = jnp.sum(spot_0 + spot_1, axis=1, keepdims=True)
            ends_0 = jnp.where(seg_0 == k, end, ends_0)
            ends_1 = jnp.where(seg_1 == k, end, ends_1)
        w_0 = widen(jnp.exp(ends_0 - cum_0) * steps[0])
        w_1 = widen(jnp.exp(ends_1 - cum_1) * steps[1])
        xw_0 = (act[0, :, :CHAN].astype(F32) * w_0).astype(BF16)
        xw_1 = (act[1, :, :CHAN].astype(F32) * w_1).astype(BF16)
        b_0 = act[0, :, CHAN : CHAN + STATES]
        b_1 = act[1, :, CHAN : CHAN + STATES]
        spot = lax.broadcasted_iota(jnp.int32, (LEN, STATES), 0)
        col_0 = segment_of(bounds, spot)
        col_1 = segment_of(bounds, spot + LEN)

        def fill(k):
            m_0 = jnp.where(col_0 == k, b_0.astype(F32), 0.0).astype(BF16)
            m_1 = jnp.where(col_1 == k, b_1.astype(F32), 0.0).astype(BF16)
            fin[k] = lax.dot_general(
                xw_0, m_0, TN, preferred_element_type=F32
            ) + lax.dot_general(xw_1, m_1, TN, preferred_element_type=F32)

        return fill

    fill = None
    filled = 0
    fin_out = pltpu.make_async_copy(fin, finals, load_sem.at[4])
    for t in range(NR + BEHIND):
        if t < NR:
            to_sib(t)
        if 0 <= t - 1 < NR:
            to_pal(t - 1)
        if t >= BEHIND:
            to_line(t - BEHIND)
        if t == NR:
            fill = finals_ready()
        elif t > NR:
            for k in range(filled, min(n_seg, filled + 2)):
                fill(k)
            filled = min(n_seg, filled + 2)
            if filled == n_seg and t == NR + BEHIND - 1:
                fin_out.start()
    for condition, copies in guarded.values():

        @pl.when(condition)
        def _():
            for copy in copies:
                copy.wait_send()

    for q in range(NR):
        cols, _ = slab(q)
        total = keep[z, :, cols] + recv_b[z, :, cols].astype(F32)
        for i, d in enumerate((2, 1, 3)):
            c_copy[q * 3 + i].wait_recv()
            total = total + recv_c[d, :, cols].astype(F32)
        mixed[:, cols] = total.astype(BF16)
    for copy in started:
        copy.wait_send()
    fin_out.wait()


def settle_kernel(mixed_in, finals_in, mixed, finals, sems):
    copies = [
        pltpu.make_async_copy(finals_in.at[k], finals.at[k], sems.at[k])
        for k in range(finals.shape[0])
    ]
    copies.append(pltpu.make_async_copy(mixed_in, mixed, sems.at[finals.shape[0]]))
    for copy in copies:
        copy.start()
    for copy in copies:
        copy.wait()


def fused_body(
    tokens,
    lengths,
    proj_zx,
    proj_bc,
    proj_dt,
    conv_x,
    conv_bc,
    bias_x,
    bias_bc,
    dt_bias,
    decay_rate,
    skip_gain,
    proj_out,
):
    n_seg = lengths.shape[0]
    bc_view = proj_bc.transpose(1, 2, 0)
    dt_view = proj_dt.T
    any_spec = pl.BlockSpec(memory_space=pl.ANY)
    vmem = pl.BlockSpec(memory_space=pltpu.VMEM)
    smem = pl.BlockSpec(memory_space=pltpu.SMEM)
    dma = pltpu.SemaphoreType.DMA
    out_shape = (
        jax.ShapeDtypeStruct((ROWS, WIDE), BF16),
        jax.ShapeDtypeStruct((n_seg, CHAN, STATES), F32),
    )
    mixed, finals = pl.pallas_call(
        layer_kernel,
        out_shape=out_shape,
        in_specs=[smem, any_spec, any_spec, any_spec, vmem, vmem, vmem]
        + [any_spec, any_spec, smem, smem, smem, any_spec],
        out_specs=(vmem, any_spec),
        scratch_shapes=[
            pltpu.VMEM((4, 2, 2, ROWS, WIDE), BF16),
            pltpu.VMEM((WIDE, 2, CHAN), BF16),
            pltpu.VMEM((WIDE, 2 * CHAN), BF16),
            pltpu.VMEM((2, 2, 64, WIDE), BF16),
            pltpu.VMEM((CHAN, WIDE), BF16),
            pltpu.VMEM((2, 4, 2, 64), F32),
            pltpu.VMEM((2, 2, 64), F32),
            pltpu.VMEM((LEN, CHAN), BF16),
            pltpu.VMEM((16 + LEN, CHAN + 256), BF16),
            pltpu.VMEM((2, LEN, CHAN + 256), BF16),
            pltpu.VMEM((2, 8, LEN), F32),
            pltpu.VMEM((n_seg, CHAN, STATES), F32),
            pltpu.VMEM((LEN, WIDE), F32),
            pltpu.VMEM((4, STATES, 128), BF16),
            pltpu.VMEM((4, STATES, 128), BF16),
            pltpu.VMEM((4, ROWS, WIDE), F32),
            pltpu.VMEM((4, 2, ROWS, WIDE), BF16),
            pltpu.VMEM((4, 2, ROWS, WIDE), BF16),
            pltpu.VMEM((4, ROWS, WIDE), BF16),
            pltpu.VMEM((4, ROWS, WIDE), BF16),
            pltpu.VMEM((4, ROWS, WIDE), BF16),
            pltpu.VMEM((4, ROWS, WIDE), BF16),
        ]
        + [dma((6,)), dma((NQ,)), dma((3, NQ)), dma((3, NQ)), dma((7, NQ)), dma((NQ,))]
        + [dma((4, 2, NQ)), dma((NQ,)), dma((NQ,)), dma((6,)), dma((6,)), dma((4,)), dma((4,))]
        + [dma((NR,)), dma((NR,)), dma((NR,)), dma((NR,)), dma((4, NR)), dma((4, NR))],
        compiler_params=pltpu.CompilerParams(
            collective_id=0, has_side_effects=True, vmem_limit_bytes=60 << 20
        ),
    )(
        lengths,
        tokens,
        proj_zx,
        bc_view,
        dt_view,
        conv_x,
        bias_x.reshape(1, CHAN),
        conv_bc,
        bias_bc,
        dt_bias,
        decay_rate,
        skip_gain,
        proj_out,
    )
    mixed, finals = pl.pallas_call(
        settle_kernel,
        out_shape=out_shape,
        in_specs=[any_spec, any_spec],
        out_specs=(any_spec, any_spec),
        scratch_shapes=[dma((n_seg + 1,))],
    )(mixed, finals)
    return (mixed, finals.reshape(n_seg, 8, 64, STATES))


def solution(mesh):
    in_specs = (
        P(("seq", "tensor"), None),
        P(),
        P(None, None, "tensor"),
        P(None, None, "tensor"),
        P(None, "tensor"),
        P(None, "tensor"),
        P(None, None, "tensor"),
        P("tensor"),
        P(None, "tensor"),
        P("tensor"),
        P("tensor"),
        P("tensor"),
        P("tensor", None),
    )
    out_specs = (P(("seq", "tensor"), None), P(None, "tensor", None, None))
    small = mesh.shape["seq"] == 2 and mesh.shape["tensor"] == 16
    chosen = fused_body if small else body
    return jax.shard_map(chosen, mesh=mesh, in_specs=in_specs, out_specs=out_specs, check_vma=False)
```

```python
import jax
import jax.numpy as jnp
from jax import lax
from jax.experimental import pallas as pl
from jax.experimental.pallas import tpu as pltpu
from jax.sharding import PartitionSpec as P

GROUPS = 8


def partner_2(value, axis, bit):
    mask = 2**bit
    pairs = [(source, source ^ mask) for source in range(lax.axis_size(axis))]
    return lax.ppermute(value, axis, pairs)


def passed_along(block, axis, distance):
    devices = range(lax.axis_size(axis))
    route = [(i - distance, i) for i in devices if i - distance in devices]
    return lax.ppermute(block, axis, route)


def group_columns(bc_own, tensor_index, steps_count):
    collected = bc_own
    for bit_number in range(steps_count):
        partner = partner_2(collected, "tensor", bit_number)
        upper = tensor_index // 2**bit_number % 2
        low_first = jnp.concatenate([collected, partner], axis=2)
        high_first = jnp.concatenate([partner, collected], axis=2)
        collected = jnp.where(upper == 0, low_first, high_first)
    return collected


def body(
    tokens,
    lengths,
    proj_zx,
    proj_bc,
    proj_dt,
    conv_x,
    conv_bc,
    bias_x,
    bias_bc,
    dt_bias,
    decay_rate,
    skip_gain,
    proj_out,
):
    highest = lax.Precision.HIGHEST
    tensor_size = lax.axis_size("tensor")
    rows_dev = tokens.shape[0]
    shard_len = rows_dev * tensor_size
    seq_index = lax.axis_index("seq")
    tensor_index = lax.axis_index("tensor")
    heads_dev = decay_rate.shape[0]
    width_zx = proj_zx.shape[2]
    head_size = width_zx // heads_dev
    cols_bc = proj_bc.shape[2]
    taps_count = conv_x.shape[0]
    model_width = tokens.shape[1]
    zx_flat = proj_zx.reshape(model_width, 2 * width_zx)
    bc_flat = proj_bc.reshape(model_width, 2 * cols_bc)
    piece = lax.all_gather(tokens, "tensor", axis=0, tiled=True)
    projected = jnp.concatenate(
        [
            jnp.dot(piece, zx_flat, preferred_element_type=jnp.float32),
            jnp.dot(piece, bc_flat, preferred_element_type=jnp.float32),
            jnp.dot(piece, proj_dt, preferred_element_type=jnp.float32),
        ],
        axis=1,
    )
    gate_in = projected[:, :width_zx].astype(jnp.bfloat16)
    conv_in = projected[:, width_zx : 2 * width_zx + 2 * cols_bc].astype(jnp.bfloat16)
    step_size = jax.nn.softplus(projected[:, 2 * width_zx + 2 * cols_bc :] + dt_bias[None, :])
    row_ids = jnp.arange(shard_len, dtype=jnp.int32)
    positions = seq_index * shard_len + row_ids
    later = jnp.arange(lengths.shape[0])
    bounds = jnp.sum(jnp.where(later[None, :] <= later[:, None], lengths[None, :], 0), axis=1)
    reached = bounds[None, :] <= positions[:, None]
    segment = jnp.sum(reached.astype(jnp.int32), axis=1)
    seg_start = jnp.max(jnp.where(reached, bounds[None, :], 0), axis=1)
    edge_rows = conv_in[shard_len - (taps_count - 1) :]
    before = passed_along(edge_rows, "seq", 1)
    extended = jnp.concatenate([before, conv_in], axis=0)
    conv_taps = jnp.concatenate([conv_x, conv_bc.reshape(taps_count, 2 * cols_bc)], axis=1)
    conv_offset = jnp.concatenate([bias_x, bias_bc.reshape(2 * cols_bc)])
    convolved = jnp.zeros((shard_len, conv_taps.shape[1]), jnp.float32) + conv_offset[None, :]
    for lag_index in range(taps_count):
        lagged = extended[
            taps_count - 1 - lag_index : taps_count - 1 - lag_index + shard_len
        ].astype(jnp.float32)
        keep_mask = (positions - lag_index >= seg_start).astype(jnp.float32)
        convolved = convolved + conv_taps[lag_index][None, :] * lagged * keep_mask[:, None]
    activated = jax.nn.silu(convolved).astype(jnp.bfloat16)
    x_conv = activated[:, :width_zx]
    bc_own = activated[:, width_zx:].reshape(shard_len, 2, cols_bc)
    per_group = tensor_size // GROUPS
    steps_count = per_group.bit_length() - 1
    bc_group = group_columns(bc_own, tensor_index, steps_count).astype(jnp.float32)
    state_in_proj = bc_group[:, 0]
    state_out_proj = bc_group[:, 1]
    x_float = x_conv.astype(jnp.float32).reshape(shard_len, heads_dev, head_size)
    log_decay = -decay_rate[None, :] * step_size
    lower = (row_ids[:, None] >= row_ids[None, :]).astype(jnp.float32)
    cumulative = jnp.dot(lower, log_decay, precision=highest)
    cumulative_t = cumulative.T
    valid = (segment[:, None] == segment[None, :]) & (row_ids[:, None] >= row_ids[None, :])
    spread = cumulative_t[:, :, None] - cumulative_t[:, None, :]
    decay_matrix = jnp.where(valid[None], jnp.exp(jnp.where(valid[None], spread, 0.0)), 0.0)
    scores = jnp.dot(state_out_proj, state_in_proj.T, precision=highest)
    mixing = decay_matrix * scores[None] * step_size.T[:, None, :]
    y_local = jnp.einsum("hts,shp->thp", mixing, x_float, precision=highest)
    before_pos = seq_index * shard_len - 1
    seg_before = jnp.sum((bounds <= before_pos).astype(jnp.int32))
    carried = (segment == seg_before).astype(jnp.float32)
    entry_gain = jnp.exp(cumulative) * carried[:, None]
    n_seg = lengths.shape[0]
    end_rows = bounds - 1 - seq_index * shard_len
    inside = (end_rows >= 0) & (end_rows < shard_len)
    target_rows = jnp.concatenate([end_rows, jnp.full((1,), shard_len - 1, jnp.int32)])
    target_seg = jnp.concatenate([jnp.arange(n_seg, dtype=jnp.int32), segment[shard_len - 1 :]])
    target_ok = jnp.concatenate([inside, jnp.ones((1,), bool)])
    picker = (row_ids[None, :] == target_rows[:, None]).astype(jnp.float32)
    cum_end = jnp.dot(picker, cumulative, precision=highest)
    reach = (
        target_ok[:, None]
        & (row_ids[None, :] <= target_rows[:, None])
        & (segment[None, :] == target_seg[:, None])
    )
    gap_end = cum_end[:, :, None] - cumulative_t[None, :, :]
    end_weight = (
        jnp.where(reach[:, None, :], jnp.exp(jnp.where(reach[:, None, :], gap_end, 0.0)), 0.0)
        * step_size.T[None]
    )
    states = jnp.einsum("khs,shp,sn->khpn", end_weight, x_float, state_in_proj, precision=highest)
    end_local = states[:n_seg]
    shard_state = states[n_seg]
    end_gain = jnp.where((target_ok & (target_seg == seg_before))[:, None], jnp.exp(cum_end), 0.0)
    shard_gain = end_gain[n_seg]
    end_gain_seg = end_gain[:n_seg]
    gathered = (
        lax.all_gather(shard_gain[None], "seq", axis=0, tiled=True),
        lax.all_gather(shard_state[None], "seq", axis=0, tiled=True),
        lax.all_gather(end_gain_seg[None], "seq", axis=0, tiled=True),
        lax.all_gather(end_local[None], "seq", axis=0, tiled=True),
    )
    gains_all, states_all, egains_all, elocal_all = gathered

    def fold_step(carry, item):
        gain_now, state_now = item
        return (gain_now[:, None, None] * carry + state_now, carry)

    last_state, incoming = lax.scan(
        fold_step, jnp.zeros(shard_state.shape, jnp.float32), (gains_all, states_all)
    )
    state_entry = lax.dynamic_index_in_dim(incoming, seq_index, 0, keepdims=False)
    final_states = jnp.sum(elocal_all + egains_all[:, :, :, None, None] * incoming[:, None], axis=0)
    y_entry = (
        jnp.einsum("tn,hpn->thp", state_out_proj, state_entry, precision=highest)
        * entry_gain[:, :, None]
    )
    y_total = y_local + y_entry + skip_gain[None, :, None] * x_float
    gate_values = jax.nn.silu(gate_in.astype(jnp.float32)).reshape(shard_len, heads_dev, head_size)
    gated = (y_total * gate_values).reshape(shard_len, width_zx).astype(jnp.bfloat16)
    mixed = lax.psum_scatter(
        jnp.dot(gated, proj_out, preferred_element_type=jnp.float32),
        "tensor",
        scatter_dimension=0,
        tiled=True,
    )
    return (mixed.astype(jnp.bfloat16), final_states)


F32 = jnp.float32
BF16 = jnp.bfloat16
ROWS = 16
LEN = 256
WIDE = 4096
CHAN = 512
STATES = 128
HIGH = lax.Precision.HIGHEST
NT = (((1,), (1,)), ((), ()))
TN = (((0,), (0,)), ((), ()))
CUTS = (1536, 1536, 1024)
LEAD = 2
SLABS = (256, 512, 512, 512, 512, 512, 512, 512, 256)
BEHIND = 4


def starts(widths):
    return tuple(sum(widths[:i]) for i in range(len(widths)))


CUT_AT = starts(CUTS)
SLAB_AT = starts(SLABS)
NQ = len(CUTS)
NR = len(SLABS)


def remote(src, dst, send, recv, **device):
    return pltpu.make_async_remote_copy(
        src_ref=src,
        dst_ref=dst,
        send_sem=send,
        recv_sem=recv,
        device_id=device,
        device_id_type=pl.DeviceIdType.MESH,
    )


def segment_of(bounds, pos):
    total = jnp.zeros(pos.shape, jnp.int32)
    for bound in bounds:
        total = total + (bound <= pos).astype(jnp.int32)
    return total


def layer_kernel(
    lengths,
    tok_in,
    zx_in,
    bc_in,
    dt_in,
    conv_x,
    bias_x,
    conv_bc,
    bias_bc,
    dt_bias,
    rate_in,
    skip_in,
    out_in,
    mixed,
    finals,
    tok,
    zx_raw,
    w_zx,
    w_bc,
    w_out,
    t_conv,
    t_bias,
    gate,
    ext,
    act,
    steps,
    fin,
    acc,
    ent_out,
    ent_in,
    keep,
    send_a,
    recv_a,
    send_b,
    recv_b,
    send_c,
    recv_c,
    load_sem,
    zx_sem,
    z_s,
    y_s,
    got,
    sib_s,
    sib_r,
    misc_s,
    misc_r,
    ent_s,
    ent_r,
    rsa_s,
    rsa_r,
    rsb_s,
    rsb_r,
    rsc_s,
    rsc_r,
):
    s = lax.axis_index("seq")
    me = lax.axis_index("tensor")
    z = me // 4
    y = (me // 2) % 2
    c = me % 2
    oy = 1 - y
    oc = 1 - c
    sib = z * 4 + y * 2 + oc
    ypal = z * 4 + oy * 2 + c
    zpal = [((z + d) % 4) * 4 + y * 2 + c for d in range(4)]
    other = 1 - s

    own = pltpu.make_async_copy(tok_in, tok.at[z, y, c], load_sem.at[0])
    own.start()
    zx_loads = []
    for q in range(NQ):
        rows = pl.ds(CUT_AT[q], CUTS[q])
        load = pltpu.make_async_copy(zx_in.at[rows], zx_raw.at[rows], zx_sem.at[q])
        load.start()
        zx_loads.append(load)
    bc_load = pltpu.make_async_copy(bc_in, w_bc.at[:, c], load_sem.at[1])
    bc_load.start()
    tap_load = pltpu.make_async_copy(conv_bc, t_conv.at[c], load_sem.at[2])
    tap_load.start()
    off_load = pltpu.make_async_copy(bias_bc, t_bias.at[c], load_sem.at[5])
    off_load.start()
    out_load = pltpu.make_async_copy(out_in, w_out, load_sem.at[3])
    out_load.start()
    ext[:16] = jnp.zeros((16, CHAN + 256), BF16)

    barrier = pltpu.get_barrier_semaphore()
    for pal in [sib, ypal] + zpal[1:]:
        pl.semaphore_signal(
            barrier, inc=1, device_id={"tensor": pal}, device_id_type=pl.DeviceIdType.MESH
        )
    pl.semaphore_signal(
        barrier, inc=1, device_id={"seq": other}, device_id_type=pl.DeviceIdType.MESH
    )
    pl.semaphore_wait(barrier, 6)

    started = []

    def go(copy):
        copy.start()
        started.append(copy)
        return copy

    guarded = {}

    def maybe(name, condition, copy):
        pl.when(condition)(copy.start)
        guarded.setdefault(name, (condition, []))[1].append(copy)

    def hop(zz, yy, q, send, device):
        ref = tok.at[zz, yy, c, :, pl.ds(CUT_AT[q], CUTS[q])]
        return remote(ref, ref, send, got.at[zz, yy, q], tensor=device)

    def landed(zz, yy, q):
        hop(zz, yy, q, y_s.at[0, q], ypal).wait_recv()

    mid = (z == 1) | (z == 2)
    ends = (z == 0) | (z == 3)
    first = z + 1 - 2 * (z % 2)
    second = 2 - z // 2
    third = 3 - 3 * (z // 2)
    inner = jnp.where(mid, 3 - z, first)
    line = {k: zz * 4 + y * 2 + c for k, zz in (("first", first), ("inner", inner))}

    def launch(q):
        go(hop(z, y, q, z_s.at[0, q], zpal[2]))
        go(hop(z, y, q, y_s.at[0, q], ypal))
        go(hop(z, y, q, z_s.at[1, q], line["inner"]))
        maybe("mid", mid, hop(z, y, q, z_s.at[2, q], line["first"]))

    def nearby(q):
        @pl.when(mid)
        def _():
            landed(third, y, q)

        maybe("mid", mid, hop(third, y, q, z_s.at[3, q], line["first"]))
        landed(first, y, q)
        go(hop(first, y, q, y_s.at[1, q], ypal))
        landed(second, y, q)
        go(hop(second, y, q, y_s.at[2, q], ypal))

    def far(q):
        @pl.when(ends)
        def _():
            landed(third, y, q)

        go(hop(third, y, q, y_s.at[3, q], ypal))

    def across_own(q):
        landed(z, oy, q)

    def across_near(q):
        landed(first, oy, q)
        landed(second, oy, q)

    def across_far(q):
        landed(third, oy, q)
        go(share(q, c))

    def share(q, core):
        ref = tok.at[:, :, core, :, pl.ds(CUT_AT[q], CUTS[q])]
        return remote(ref, ref, sib_s.at[q], sib_r.at[q], tensor=sib)

    own.wait()
    for q in range(min(LEAD, NQ)):
        launch(q)
    bc_send = go(remote(bc_in, w_bc.at[:, c], misc_s.at[0], misc_r.at[0], tensor=sib))
    tap_send = go(remote(conv_bc, t_conv.at[c], misc_s.at[1], misc_r.at[1], tensor=sib))
    off_send = go(remote(bias_bc, t_bias.at[c], misc_s.at[5], misc_r.at[5], tensor=sib))

    def split(q, part):
        size = CUTS[q] // 4

        def run():
            if part == 0:
                zx_loads[q].wait()

            @pl.loop(0, size // 128)
            def _(j):
                at = pl.multiple_of(CUT_AT[q] + part * size + j * 128, 128)
                rows = pl.ds(at, 128)
                both = pltpu.einshape("abc->bac", zx_raw[rows])
                w_zx[rows, :CHAN] = both[0]
                w_zx[rows, CHAN:] = both[1]

        return run

    def chunk(q):
        at = slice(CUT_AT[q], CUT_AT[q] + CUTS[q])
        return tok[:, :, :, :, at].reshape(LEN, CUTS[q])

    def add_to(q, rows, cols, product):
        if q == 0:
            acc[rows, cols] = product
        else:
            acc[rows, cols] += product

    def dot_zx(q, i):
        def run():
            cols = slice(i * 256, i * 256 + 256)
            at = slice(CUT_AT[q], CUT_AT[q] + CUTS[q])
            add_to(
                q,
                slice(0, LEN),
                cols,
                jnp.dot(chunk(q), w_zx[at, cols], preferred_element_type=F32),
            )

        return run

    def dot_bc(q):
        def run():
            if q == 0:
                for load in (bc_load, tap_load, off_load):
                    load.wait()
                for sent in (bc_send, tap_send, off_send):
                    sent.wait_recv()
            at = slice(CUT_AT[q], CUT_AT[q] + CUTS[q])
            weights = w_bc[:, :, :, at].reshape(256, CUTS[q])
            add_to(
                q,
                slice(0, LEN),
                slice(1024, 1280),
                lax.dot_general(chunk(q), weights, NT, preferred_element_type=F32),
            )

        return run

    def dot_dt(q):
        def run():
            at = slice(CUT_AT[q], CUT_AT[q] + CUTS[q])
            add_to(
                q,
                slice(0, 8),
                slice(1280, 1280 + LEN),
                lax.dot_general(dt_in[:, at], chunk(q), NT, preferred_element_type=F32),
            )

        return run

    last = NQ - 1
    for t in range(NQ + 3):
        if t + LEAD < NQ:
            launch(t + LEAD)
        todo = []
        if t < NQ:
            todo = [split(t, part) for part in range(4)]
        if t >= 3:
            q = t - 3
            share(q, oc).wait_recv()
            todo += [dot_bc(q), dot_zx(q, 2), dot_zx(q, 3), dot_dt(q)]
            if q != last:
                todo += [dot_zx(q, 0), dot_zx(q, 1)]
        events = [(nearby, t), (far, t - 1), (across_own, t)]
        events += [(across_near, t - 1), (across_far, t - 2)]
        events = [(what, q) for what, q in events if 0 <= q < NQ]
        for i, (what, q) in enumerate(events):
            what(q)
            count = -(-len(todo) // (len(events) - i))
            for work in todo[:count]:
                work()
            todo = todo[count:]
        for work in todo:
            work()

    ext[16:, CHAN:] = acc[:, 1024:1280].astype(BF16)
    ext[16:, :CHAN] = acc[:, 512:1024].astype(BF16)
    halo = go(
        remote(ext.at[pl.ds(256, 16)], ext.at[pl.ds(0, 16)], misc_s.at[2], misc_r.at[2], seq=other)
    )
    head_row = lax.broadcasted_iota(jnp.int32, (8, LEN), 0)

    def by_head(ref, heads):
        values = jnp.zeros(heads.shape, F32)
        for h in range(8):
            values = jnp.where(heads == h, ref[h], values)
        return values

    rate = by_head(rate_in, head_row)
    dt_own = jax.nn.softplus(acc[:8, 1280 : 1280 + LEN] + by_head(dt_bias, head_row))
    steps[s] = dt_own
    step_send = go(remote(steps.at[s], steps.at[s], misc_s.at[3], misc_r.at[3], seq=other))
    n_seg = lengths.shape[0]
    bounds = []
    run_sum = jnp.int32(0)
    for k in range(n_seg):
        run_sum = run_sum + lengths[k]
        bounds.append(run_sum)
    base = s * LEN
    row = lax.broadcasted_iota(jnp.int32, (LEN, 128), 0)
    pos = row + base
    seg_start = jnp.zeros((LEN, 128), jnp.int32)
    for bound in bounds:
        seg_start = jnp.where(bound <= pos, jnp.maximum(seg_start, bound), seg_start)
    masks = [None] + [(pos - j >= seg_start).astype(F32) for j in range(1, 4)]
    masks_in = [None] + [jnp.where(row >= j, masks[j], 0.0) for j in range(1, 4)]

    ri = lax.broadcasted_iota(jnp.int32, (LEN, LEN), 0)
    ci = lax.broadcasted_iota(jnp.int32, (LEN, LEN), 1)
    upper = (ri <= ci).astype(F32)
    head_of = lax.broadcasted_iota(jnp.int32, (8, CHAN), 1) // 64
    spread = (head_of == lax.broadcasted_iota(jnp.int32, (8, CHAN), 0)).astype(F32)

    def cumulate(dt):
        return jnp.dot(-rate * dt, upper, precision=HIGH, preferred_element_type=F32)

    def widen(rows):
        return lax.dot_general(rows, spread, TN, precision=HIGH, preferred_element_type=F32)

    place = lax.broadcasted_iota(jnp.int32, (8, LEN), 1)
    seg_own = segment_of(bounds, place + base)
    seg_last = segment_of(bounds, jnp.full((8, LEN), LEN - 1, jnp.int32) + base)
    cum_r = cumulate(dt_own)
    into = jnp.exp(cum_r[:, LEN - 1 :] - cum_r) * dt_own * (seg_own == seg_last).astype(F32)
    into_wide = widen(into)

    def taps_for(i, row):
        if i < 4:
            cols = slice(i * 128, i * 128 + 128)
            return bias_x[:, cols] if row == 4 else conv_x[row : row + 1, cols]
        k = i - 4
        if row == 4:
            both = [t_bias[e, k : k + 1, :] for e in range(2)]
        else:
            both = [t_conv[e, row, k : k + 1, :] for e in range(2)]
        return jnp.concatenate(both, axis=1)

    def silu(v):
        return v * lax.logistic(v)

    ent_copy = []
    for i in (4, 0, 1, 2, 3, 5):
        cols = slice(i * 128, i * 128 + 128)
        v = ext[16:, cols].astype(F32)
        total = taps_for(i, 4) + taps_for(i, 0) * v
        for j in range(1, 4):
            total = total + taps_for(i, j) * pltpu.roll(v, j, 0) * masks_in[j]
        made = silu(total).astype(BF16)
        act[s, :, cols] = made
        if i < 4:
            x_in = (made.astype(F32) * into_wide[:, cols]).astype(BF16)
            ent_out[i] = lax.dot_general(
                act[s, :, CHAN : CHAN + STATES], x_in, TN, preferred_element_type=F32
            ).astype(BF16)
            ent_copy.append(
                go(remote(ent_out.at[i], ent_in.at[i], ent_s.at[i], ent_r.at[i], seq=other))
            )
    halo.wait_recv()

    @pl.when(s > 0)
    def _():
        for i in range(6):
            cols = slice(i * 128, i * 128 + 128)
            v = ext[:32, cols].astype(F32)
            total = taps_for(i, 4) + taps_for(i, 0) * v[16:]
            for j in range(1, 4):
                total = total + taps_for(i, j) * pltpu.roll(v, j, 0)[16:] * masks[j][:16]
            act[s, :16, cols] = silu(total).astype(BF16)

    seen = act.at[s, :, pl.ds(0, CHAN + STATES)]
    act_send = go(remote(seen, seen, misc_s.at[4], misc_r.at[4], seq=other))

    for i in range(2):
        cols = slice(i * 256, i * 256 + 256)
        at = slice(CUT_AT[last], CUT_AT[last] + CUTS[last])
        gate[:, cols] = (
            acc[:, cols] + jnp.dot(chunk(last), w_zx[at, cols], preferred_element_type=F32)
        ).astype(BF16)

    cum_c = cum_r.T
    seg_r = segment_of(bounds, ci + base)
    seg_c = segment_of(bounds, ri + base)
    valid = (seg_r == seg_c) & (ri >= ci)
    b_own = act[s, :, CHAN : CHAN + STATES]
    c_own = act[s, :, CHAN + STATES :]
    scores = lax.dot_general(c_own, b_own, NT, preferred_element_type=F32)
    scores = jnp.where(valid, scores, 0.0)
    lane = lax.broadcasted_iota(jnp.int32, (LEN, 128), 1)
    for g in range(4):
        cols = slice(g * 128, g * 128 + 128)
        x_pair = act[s, :, cols]
        halves = []
        for h in (2 * g, 2 * g + 1):
            gap = cum_c[:, h : h + 1] - cum_r[h : h + 1, :]
            mix = jnp.exp(jnp.where(valid, gap, 0.0)) * scores * dt_own[h : h + 1, :]
            halves.append(jnp.dot(mix.astype(BF16), x_pair, preferred_element_type=F32))
        acc[:, cols] = jnp.where(lane < 64, halves[0], halves[1])

    seg_before = segment_of(bounds, jnp.full((8, LEN), LEN - 1, jnp.int32))
    carried = ((seg_own == seg_before) & (s > 0)).astype(F32)
    gain = widen(jnp.exp(cum_r) * carried)
    skips = by_head(skip_in, head_of[:1])
    for i in range(4):
        cols = slice(i * 128, i * 128 + 128)
        ent_copy[i].wait_recv()
        y_all = acc[:, cols] + jnp.dot(c_own, ent_in[i], preferred_element_type=F32) * gain[:, cols]
        y_all = y_all + skips[:, cols] * act[s, :, cols].astype(F32)
        gate[:, cols] = (y_all * silu(gate[:, cols].astype(F32))).astype(BF16)
    out_load.wait()

    def part(zz, yy, cc):
        return pl.ds(pl.multiple_of(zz * 64 + yy * 32 + cc * 16, 16), 16)

    a_copy = []
    b_copy = []
    c_copy = []

    def slab(q):
        return slice(SLAB_AT[q], SLAB_AT[q] + SLABS[q]), pl.ds(SLAB_AT[q], SLABS[q])

    def to_sib(q):
        cols, at = slab(q)
        acc[:, cols] = jnp.dot(gate[...], w_out[:, cols], preferred_element_type=F32)
        for zz in range(4):
            for yy in range(2):
                send_a[zz, yy, :, cols] = acc[part(zz, yy, oc), cols].astype(BF16)
        src, dst = send_a.at[:, :, :, at], recv_a.at[:, :, :, at]
        a_copy.append(go(remote(src, dst, rsa_s.at[q], rsa_r.at[q], tensor=sib)))

    def to_pal(q):
        cols, at = slab(q)
        a_copy[q].wait_recv()
        for zz in range(4):
            send_b[zz, :, cols] = (
                acc[part(zz, oy, c), cols] + recv_a[zz, oy, :, cols].astype(F32)
            ).astype(BF16)
        src, dst = send_b.at[:, :, at], recv_b.at[:, :, at]
        b_copy.append(go(remote(src, dst, rsb_s.at[q], rsb_r.at[q], tensor=ypal)))
        for zz in range(4):
            keep[zz, :, cols] = acc[part(zz, y, c), cols] + recv_a[zz, y, :, cols].astype(F32)

    def to_line(q):
        cols, at = slab(q)
        b_copy[q].wait_recv()
        for d in (2, 1, 3):
            zz = (z + d) % 4
            send_c[d, :, cols] = (keep[zz, :, cols] + recv_b[zz, :, cols].astype(F32)).astype(BF16)
            src, dst = send_c.at[d, :, at], recv_c.at[d, :, at]
            c_copy.append(
                go(remote(src, dst, rsc_s.at[d, q], rsc_r.at[d, q], tensor=zpal[d]))
            )

    def finals_ready():
        step_send.wait_recv()
        act_send.wait_recv()
        cum_0 = cumulate(steps[0])
        cum_1 = cumulate(steps[1]) + cum_0[:, LEN - 1 :]
        seg_0 = segment_of(bounds, place)
        seg_1 = segment_of(bounds, place + LEN)
        ends_0 = jnp.zeros((8, LEN), F32)
        ends_1 = jnp.zeros((8, LEN), F32)
        for k in range(n_seg):
            spot_0 = (place == bounds[k] - 1).astype(F32) * cum_0
            spot_1 = (place + LEN == bounds[k] - 1).astype(F32) * cum_1
            end = jnp.sum(spot_0 + spot_1, axis=1, keepdims=True)
            ends_0 = jnp.where(seg_0 == k, end, ends_0)
            ends_1 = jnp.where(seg_1 == k, end, ends_1)
        w_0 = widen(jnp.exp(ends_0 - cum_0) * steps[0])
        w_1 = widen(jnp.exp(ends_1 - cum_1) * steps[1])
        xw_0 = (act[0, :, :CHAN].astype(F32) * w_0).astype(BF16)
        xw_1 = (act[1, :, :CHAN].astype(F32) * w_1).astype(BF16)
        b_0 = act[0, :, CHAN : CHAN + STATES]
        b_1 = act[1, :, CHAN : CHAN + STATES]
        spot = lax.broadcasted_iota(jnp.int32, (LEN, STATES), 0)
        col_0 = segment_of(bounds, spot)
        col_1 = segment_of(bounds, spot + LEN)

        def fill(k):
            m_0 = jnp.where(col_0 == k, b_0.astype(F32), 0.0).astype(BF16)
            m_1 = jnp.where(col_1 == k, b_1.astype(F32), 0.0).astype(BF16)
            fin[k] = lax.dot_general(
                xw_0, m_0, TN, preferred_element_type=F32
            ) + lax.dot_general(xw_1, m_1, TN, preferred_element_type=F32)

        return fill

    fill = None
    filled = 0
    fin_out = pltpu.make_async_copy(fin, finals, load_sem.at[4])
    for t in range(NR + BEHIND):
        if t < NR:
            to_sib(t)
        if 0 <= t - 1 < NR:
            to_pal(t - 1)
        if t >= BEHIND:
            to_line(t - BEHIND)
        if t == NR:
            fill = finals_ready()
        elif t > NR:
            for k in range(filled, min(n_seg, filled + 2)):
                fill(k)
            filled = min(n_seg, filled + 2)
            if filled == n_seg and t == NR + BEHIND - 1:
                fin_out.start()
    for condition, copies in guarded.values():

        @pl.when(condition)
        def _():
            for copy in copies:
                copy.wait_send()

    for q in range(NR):
        cols, _ = slab(q)
        total = keep[z, :, cols] + recv_b[z, :, cols].astype(F32)
        for i, d in enumerate((2, 1, 3)):
            c_copy[q * 3 + i].wait_recv()
            total = total + recv_c[d, :, cols].astype(F32)
        mixed[:, cols] = total.astype(BF16)
    for copy in started:
        copy.wait_send()
    fin_out.wait()


def settle_kernel(mixed_in, finals_in, mixed, finals, rows, held, in_sem, out_sem):
    n_seg = finals.shape[0]
    ways = [(finals_in.at[k], held.at[k], finals.at[k]) for k in range(n_seg)]
    ways.append((mixed_in, rows, mixed))
    loads = [pltpu.make_async_copy(a, b, in_sem.at[i]) for i, (a, b, _) in enumerate(ways)]
    stores = [pltpu.make_async_copy(b, o, out_sem.at[i]) for i, (_, b, o) in enumerate(ways)]
    for load in loads:
        load.start()
    for load, store in zip(loads, stores):
        load.wait()
        store.start()
    for store in stores:
        store.wait()


def fused_body(
    tokens,
    lengths,
    proj_zx,
    proj_bc,
    proj_dt,
    conv_x,
    conv_bc,
    bias_x,
    bias_bc,
    dt_bias,
    decay_rate,
    skip_gain,
    proj_out,
):
    n_seg = lengths.shape[0]
    bc_view = proj_bc.transpose(1, 2, 0)
    dt_view = proj_dt.T
    any_spec = pl.BlockSpec(memory_space=pl.ANY)
    vmem = pl.BlockSpec(memory_space=pltpu.VMEM)
    smem = pl.BlockSpec(memory_space=pltpu.SMEM)
    dma = pltpu.SemaphoreType.DMA
    out_shape = (
        jax.ShapeDtypeStruct((ROWS, WIDE), BF16),
        jax.ShapeDtypeStruct((n_seg, CHAN, STATES), F32),
    )
    mixed, finals = pl.pallas_call(
        layer_kernel,
        out_shape=out_shape,
        in_specs=[smem, any_spec, any_spec, any_spec, vmem, vmem, vmem]
        + [any_spec, any_spec, smem, smem, smem, any_spec],
        out_specs=(vmem, any_spec),
        scratch_shapes=[
            pltpu.VMEM((4, 2, 2, ROWS, WIDE), BF16),
            pltpu.VMEM((WIDE, 2, CHAN), BF16),
            pltpu.VMEM((WIDE, 2 * CHAN), BF16),
            pltpu.VMEM((2, 2, 64, WIDE), BF16),
            pltpu.VMEM((CHAN, WIDE), BF16),
            pltpu.VMEM((2, 4, 2, 64), F32),
            pltpu.VMEM((2, 2, 64), F32),
            pltpu.VMEM((LEN, CHAN), BF16),
            pltpu.VMEM((16 + LEN, CHAN + 256), BF16),
            pltpu.VMEM((2, LEN, CHAN + 256), BF16),
            pltpu.VMEM((2, 8, LEN), F32),
            pltpu.VMEM((n_seg, CHAN, STATES), F32),
            pltpu.VMEM((LEN, WIDE), F32),
            pltpu.VMEM((4, STATES, 128), BF16),
            pltpu.VMEM((4, STATES, 128), BF16),
            pltpu.VMEM((4, ROWS, WIDE), F32),
            pltpu.VMEM((4, 2, ROWS, WIDE), BF16),
            pltpu.VMEM((4, 2, ROWS, WIDE), BF16),
            pltpu.VMEM((4, ROWS, WIDE), BF16),
            pltpu.VMEM((4, ROWS, WIDE), BF16),
            pltpu.VMEM((4, ROWS, WIDE), BF16),
            pltpu.VMEM((4, ROWS, WIDE), BF16),
        ]
        + [dma((6,)), dma((NQ,)), dma((4, NQ)), dma((4, NQ))]
        + [dma((4, 2, NQ)), dma((NQ,)), dma((NQ,)), dma((6,)), dma((6,)), dma((4,)), dma((4,))]
        + [dma((NR,)), dma((NR,)), dma((NR,)), dma((NR,)), dma((4, NR)), dma((4, NR))],
        compiler_params=pltpu.CompilerParams(
            collective_id=0, has_side_effects=True, vmem_limit_bytes=60 << 20
        ),
    )(
        lengths,
        tokens,
        proj_zx,
        bc_view,
        dt_view,
        conv_x,
        bias_x.reshape(1, CHAN),
        conv_bc,
        bias_bc,
        dt_bias,
        decay_rate,
        skip_gain,
        proj_out,
    )
    mixed, finals = pl.pallas_call(
        settle_kernel,
        out_shape=out_shape,
        in_specs=[any_spec, any_spec],
        out_specs=(any_spec, any_spec),
        scratch_shapes=[
            pltpu.VMEM((ROWS, WIDE), BF16),
            pltpu.VMEM((n_seg, CHAN, STATES), F32),
            dma((n_seg + 1,)),
            dma((n_seg + 1,)),
        ],
    )(mixed, finals)
    return (mixed, finals.reshape(n_seg, 8, 64, STATES))


def solution(mesh):
    in_specs = (
        P(("seq", "tensor"), None),
        P(),
        P(None, None, "tensor"),
        P(None, None, "tensor"),
        P(None, "tensor"),
        P(None, "tensor"),
        P(None, None, "tensor"),
        P("tensor"),
        P(None, "tensor"),
        P("tensor"),
        P("tensor"),
        P("tensor"),
        P("tensor", None),
    )
    out_specs = (P(("seq", "tensor"), None), P(None, "tensor", None, None))
    small = mesh.shape["seq"] == 2 and mesh.shape["tensor"] == 16
    chosen = fused_body if small else body
    return jax.shard_map(chosen, mesh=mesh, in_specs=in_specs, out_specs=out_specs, check_vma=False)
```

```python
import jax
import jax.numpy as jnp
from jax import lax
from jax.experimental import pallas as pl
from jax.experimental.pallas import tpu as pltpu
from jax.sharding import PartitionSpec as P

GROUPS = 8


def partner_2(value, axis, bit):
    mask = 2**bit
    pairs = [(source, source ^ mask) for source in range(lax.axis_size(axis))]
    return lax.ppermute(value, axis, pairs)


def passed_along(block, axis, distance):
    devices = range(lax.axis_size(axis))
    route = [(i - distance, i) for i in devices if i - distance in devices]
    return lax.ppermute(block, axis, route)


def group_columns(bc_own, tensor_index, steps_count):
    collected = bc_own
    for bit_number in range(steps_count):
        partner = partner_2(collected, "tensor", bit_number)
        upper = tensor_index // 2**bit_number % 2
        low_first = jnp.concatenate([collected, partner], axis=2)
        high_first = jnp.concatenate([partner, collected], axis=2)
        collected = jnp.where(upper == 0, low_first, high_first)
    return collected


def body(
    tokens,
    lengths,
    proj_zx,
    proj_bc,
    proj_dt,
    conv_x,
    conv_bc,
    bias_x,
    bias_bc,
    dt_bias,
    decay_rate,
    skip_gain,
    proj_out,
):
    highest = lax.Precision.HIGHEST
    tensor_size = lax.axis_size("tensor")
    rows_dev = tokens.shape[0]
    shard_len = rows_dev * tensor_size
    seq_index = lax.axis_index("seq")
    tensor_index = lax.axis_index("tensor")
    heads_dev = decay_rate.shape[0]
    width_zx = proj_zx.shape[2]
    head_size = width_zx // heads_dev
    cols_bc = proj_bc.shape[2]
    taps_count = conv_x.shape[0]
    model_width = tokens.shape[1]
    zx_flat = proj_zx.reshape(model_width, 2 * width_zx)
    bc_flat = proj_bc.reshape(model_width, 2 * cols_bc)
    piece = lax.all_gather(tokens, "tensor", axis=0, tiled=True)
    projected = jnp.concatenate(
        [
            jnp.dot(piece, zx_flat, preferred_element_type=jnp.float32),
            jnp.dot(piece, bc_flat, preferred_element_type=jnp.float32),
            jnp.dot(piece, proj_dt, preferred_element_type=jnp.float32),
        ],
        axis=1,
    )
    gate_in = projected[:, :width_zx].astype(jnp.bfloat16)
    conv_in = projected[:, width_zx : 2 * width_zx + 2 * cols_bc].astype(jnp.bfloat16)
    step_size = jax.nn.softplus(projected[:, 2 * width_zx + 2 * cols_bc :] + dt_bias[None, :])
    row_ids = jnp.arange(shard_len, dtype=jnp.int32)
    positions = seq_index * shard_len + row_ids
    later = jnp.arange(lengths.shape[0])
    bounds = jnp.sum(jnp.where(later[None, :] <= later[:, None], lengths[None, :], 0), axis=1)
    reached = bounds[None, :] <= positions[:, None]
    segment = jnp.sum(reached.astype(jnp.int32), axis=1)
    seg_start = jnp.max(jnp.where(reached, bounds[None, :], 0), axis=1)
    edge_rows = conv_in[shard_len - (taps_count - 1) :]
    before = passed_along(edge_rows, "seq", 1)
    extended = jnp.concatenate([before, conv_in], axis=0)
    conv_taps = jnp.concatenate([conv_x, conv_bc.reshape(taps_count, 2 * cols_bc)], axis=1)
    conv_offset = jnp.concatenate([bias_x, bias_bc.reshape(2 * cols_bc)])
    convolved = jnp.zeros((shard_len, conv_taps.shape[1]), jnp.float32) + conv_offset[None, :]
    for lag_index in range(taps_count):
        lagged = extended[
            taps_count - 1 - lag_index : taps_count - 1 - lag_index + shard_len
        ].astype(jnp.float32)
        keep_mask = (positions - lag_index >= seg_start).astype(jnp.float32)
        convolved = convolved + conv_taps[lag_index][None, :] * lagged * keep_mask[:, None]
    activated = jax.nn.silu(convolved).astype(jnp.bfloat16)
    x_conv = activated[:, :width_zx]
    bc_own = activated[:, width_zx:].reshape(shard_len, 2, cols_bc)
    per_group = tensor_size // GROUPS
    steps_count = per_group.bit_length() - 1
    bc_group = group_columns(bc_own, tensor_index, steps_count).astype(jnp.float32)
    state_in_proj = bc_group[:, 0]
    state_out_proj = bc_group[:, 1]
    x_float = x_conv.astype(jnp.float32).reshape(shard_len, heads_dev, head_size)
    log_decay = -decay_rate[None, :] * step_size
    lower = (row_ids[:, None] >= row_ids[None, :]).astype(jnp.float32)
    cumulative = jnp.dot(lower, log_decay, precision=highest)
    cumulative_t = cumulative.T
    valid = (segment[:, None] == segment[None, :]) & (row_ids[:, None] >= row_ids[None, :])
    spread = cumulative_t[:, :, None] - cumulative_t[:, None, :]
    decay_matrix = jnp.where(valid[None], jnp.exp(jnp.where(valid[None], spread, 0.0)), 0.0)
    scores = jnp.dot(state_out_proj, state_in_proj.T, precision=highest)
    mixing = decay_matrix * scores[None] * step_size.T[:, None, :]
    y_local = jnp.einsum("hts,shp->thp", mixing, x_float, precision=highest)
    before_pos = seq_index * shard_len - 1
    seg_before = jnp.sum((bounds <= before_pos).astype(jnp.int32))
    carried = (segment == seg_before).astype(jnp.float32)
    entry_gain = jnp.exp(cumulative) * carried[:, None]
    n_seg = lengths.shape[0]
    end_rows = bounds - 1 - seq_index * shard_len
    inside = (end_rows >= 0) & (end_rows < shard_len)
    target_rows = jnp.concatenate([end_rows, jnp.full((1,), shard_len - 1, jnp.int32)])
    target_seg = jnp.concatenate([jnp.arange(n_seg, dtype=jnp.int32), segment[shard_len - 1 :]])
    target_ok = jnp.concatenate([inside, jnp.ones((1,), bool)])
    picker = (row_ids[None, :] == target_rows[:, None]).astype(jnp.float32)
    cum_end = jnp.dot(picker, cumulative, precision=highest)
    reach = (
        target_ok[:, None]
        & (row_ids[None, :] <= target_rows[:, None])
        & (segment[None, :] == target_seg[:, None])
    )
    gap_end = cum_end[:, :, None] - cumulative_t[None, :, :]
    end_weight = (
        jnp.where(reach[:, None, :], jnp.exp(jnp.where(reach[:, None, :], gap_end, 0.0)), 0.0)
        * step_size.T[None]
    )
    states = jnp.einsum("khs,shp,sn->khpn", end_weight, x_float, state_in_proj, precision=highest)
    end_local = states[:n_seg]
    shard_state = states[n_seg]
    end_gain = jnp.where((target_ok & (target_seg == seg_before))[:, None], jnp.exp(cum_end), 0.0)
    shard_gain = end_gain[n_seg]
    end_gain_seg = end_gain[:n_seg]
    gathered = (
        lax.all_gather(shard_gain[None], "seq", axis=0, tiled=True),
        lax.all_gather(shard_state[None], "seq", axis=0, tiled=True),
        lax.all_gather(end_gain_seg[None], "seq", axis=0, tiled=True),
        lax.all_gather(end_local[None], "seq", axis=0, tiled=True),
    )
    gains_all, states_all, egains_all, elocal_all = gathered

    def fold_step(carry, item):
        gain_now, state_now = item
        return (gain_now[:, None, None] * carry + state_now, carry)

    last_state, incoming = lax.scan(
        fold_step, jnp.zeros(shard_state.shape, jnp.float32), (gains_all, states_all)
    )
    state_entry = lax.dynamic_index_in_dim(incoming, seq_index, 0, keepdims=False)
    final_states = jnp.sum(elocal_all + egains_all[:, :, :, None, None] * incoming[:, None], axis=0)
    y_entry = (
        jnp.einsum("tn,hpn->thp", state_out_proj, state_entry, precision=highest)
        * entry_gain[:, :, None]
    )
    y_total = y_local + y_entry + skip_gain[None, :, None] * x_float
    gate_values = jax.nn.silu(gate_in.astype(jnp.float32)).reshape(shard_len, heads_dev, head_size)
    gated = (y_total * gate_values).reshape(shard_len, width_zx).astype(jnp.bfloat16)
    mixed = lax.psum_scatter(
        jnp.dot(gated, proj_out, preferred_element_type=jnp.float32),
        "tensor",
        scatter_dimension=0,
        tiled=True,
    )
    return (mixed.astype(jnp.bfloat16), final_states)


F32 = jnp.float32
BF16 = jnp.bfloat16
ROWS = 16
LEN = 256
WIDE = 4096
CHAN = 512
STATES = 128
HIGH = lax.Precision.HIGHEST
NT = (((1,), (1,)), ((), ()))
TN = (((0,), (0,)), ((), ()))
CUTS = (1536, 1536, 1024)
LEAD = 2
SLABS = (256, 512, 512, 512, 512, 512, 512, 512, 256)
BEHIND = 4
DIRECT = (len(SLABS) - 2, len(SLABS) - 1)


def starts(widths):
    return tuple(sum(widths[:i]) for i in range(len(widths)))


CUT_AT = starts(CUTS)
SLAB_AT = starts(SLABS)
NQ = len(CUTS)
NR = len(SLABS)


def remote(src, dst, send, recv, **device):
    return pltpu.make_async_remote_copy(
        src_ref=src,
        dst_ref=dst,
        send_sem=send,
        recv_sem=recv,
        device_id=device,
        device_id_type=pl.DeviceIdType.MESH,
    )


def segment_of(bounds, pos):
    total = jnp.zeros(pos.shape, jnp.int32)
    for bound in bounds:
        total = total + (bound <= pos).astype(jnp.int32)
    return total


def layer_kernel(
    lengths,
    tok_in,
    zx_in,
    bc_in,
    dt_from,
    conv_from,
    bias_from,
    conv_bc,
    bias_bc,
    dt_bias,
    rate_in,
    skip_in,
    out_in,
    mixed,
    finals,
    tok,
    zx_raw,
    w_zx,
    w_bc,
    w_out,
    t_conv,
    t_bias,
    gate,
    ext,
    act,
    steps,
    dt_in,
    conv_x,
    bias_x,
    early,
    okay,
    acc,
    ent_out,
    ent_in,
    keep,
    send_a,
    recv_a,
    send_b,
    recv_b,
    send_c,
    recv_c,
    load_sem,
    zx_sem,
    z_s,
    y_s,
    got,
    sib_s,
    sib_r,
    misc_s,
    misc_r,
    ent_s,
    ent_r,
    rsa_s,
    rsa_r,
    rsb_s,
    rsb_r,
    rsc_s,
    rsc_r,
):
    s = lax.axis_index("seq")
    me = lax.axis_index("tensor")
    z = me // 4
    y = (me // 2) % 2
    c = me % 2
    oy = 1 - y
    oc = 1 - c
    sib = z * 4 + y * 2 + oc
    ypal = z * 4 + oy * 2 + c
    zpal = [((z + d) % 4) * 4 + y * 2 + c for d in range(4)]
    other = 1 - s

    own = pltpu.make_async_copy(tok_in, tok.at[z, y, c], load_sem.at[0])
    own.start()
    zx_loads = []
    for q in range(NQ):
        rows = pl.ds(CUT_AT[q], CUTS[q])
        load = pltpu.make_async_copy(zx_in.at[rows], zx_raw.at[rows], zx_sem.at[q])
        load.start()
        zx_loads.append(load)
    bc_load = pltpu.make_async_copy(bc_in, w_bc.at[:, c], load_sem.at[1])
    bc_load.start()
    tap_load = pltpu.make_async_copy(conv_bc, t_conv.at[c], load_sem.at[2])
    tap_load.start()
    off_load = pltpu.make_async_copy(bias_bc, t_bias.at[c], load_sem.at[5])
    off_load.start()
    small_loads = [
        pltpu.make_async_copy(src, dst, load_sem.at[i])
        for i, src, dst in ((4, dt_from, dt_in), (6, conv_from, conv_x), (7, bias_from, bias_x))
    ]
    for load in small_loads:
        load.start()
    out_load = pltpu.make_async_copy(out_in, w_out, load_sem.at[3])
    out_load.start()
    ext[:16] = jnp.zeros((16, CHAN + 256), BF16)

    barrier = pltpu.get_barrier_semaphore()
    for pal in [sib, ypal] + zpal[1:]:
        pl.semaphore_signal(
            barrier, inc=1, device_id={"tensor": pal}, device_id_type=pl.DeviceIdType.MESH
        )
    pl.semaphore_signal(
        barrier, inc=1, device_id={"seq": other}, device_id_type=pl.DeviceIdType.MESH
    )
    pl.semaphore_wait(barrier, 6)

    started = []

    def go(copy):
        copy.start()
        started.append(copy)
        return copy

    guarded = {}

    def maybe(name, condition, copy):
        pl.when(condition)(copy.start)
        guarded.setdefault(name, (condition, []))[1].append(copy)

    def hop(zz, yy, q, send, device):
        ref = tok.at[zz, yy, c, :, pl.ds(CUT_AT[q], CUTS[q])]
        return remote(ref, ref, send, got.at[zz, yy, q], tensor=device)

    def landed(zz, yy, q):
        hop(zz, yy, q, y_s.at[0, q], ypal).wait_recv()

    mid = (z == 1) | (z == 2)
    ends = (z == 0) | (z == 3)
    first = z + 1 - 2 * (z % 2)
    second = 2 - z // 2
    third = 3 - 3 * (z // 2)
    inner = jnp.where(mid, 3 - z, first)
    line = {k: zz * 4 + y * 2 + c for k, zz in (("first", first), ("inner", inner), ("third", third))}

    def launch(q):
        go(hop(z, y, q, z_s.at[0, q], zpal[2]))
        go(hop(z, y, q, y_s.at[0, q], ypal))
        go(hop(z, y, q, z_s.at[1, q], line["inner"]))
        maybe("mid", mid, hop(z, y, q, z_s.at[2, q], line["first"]))

    def nearby(q):
        @pl.when(mid)
        def _():
            landed(third, y, q)

        maybe("mid", mid, hop(third, y, q, z_s.at[3, q], line["first"]))
        landed(first, y, q)
        go(hop(first, y, q, y_s.at[1, q], ypal))
        landed(second, y, q)
        go(hop(second, y, q, y_s.at[2, q], ypal))

    def far(q):
        @pl.when(ends)
        def _():
            landed(third, y, q)

        go(hop(third, y, q, y_s.at[3, q], ypal))

    def across_own(q):
        landed(z, oy, q)

    def across_near(q):
        landed(first, oy, q)
        landed(second, oy, q)

    def across_far(q):
        landed(third, oy, q)
        go(share(q, c))

    def share(q, core):
        ref = tok.at[:, :, core, :, pl.ds(CUT_AT[q], CUTS[q])]
        return remote(ref, ref, sib_s.at[q], sib_r.at[q], tensor=sib)

    own.wait()
    for q in range(min(LEAD, NQ)):
        launch(q)
    bc_send = go(remote(bc_in, w_bc.at[:, c], misc_s.at[0], misc_r.at[0], tensor=sib))
    tap_send = go(remote(conv_bc, t_conv.at[c], misc_s.at[1], misc_r.at[1], tensor=sib))
    off_send = go(remote(bias_bc, t_bias.at[c], misc_s.at[5], misc_r.at[5], tensor=sib))

    def split(q, part):
        size = CUTS[q] // 4

        def run():
            if part == 0:
                zx_loads[q].wait()

            @pl.loop(0, size // 128)
            def _(j):
                at = pl.multiple_of(CUT_AT[q] + part * size + j * 128, 128)
                rows = pl.ds(at, 128)
                both = pltpu.einshape("abc->bac", zx_raw[rows])
                w_zx[rows, :CHAN] = both[0]
                w_zx[rows, CHAN:] = both[1]

        return run

    def chunk(q):
        at = slice(CUT_AT[q], CUT_AT[q] + CUTS[q])
        return tok[:, :, :, :, at].reshape(LEN, CUTS[q])

    def add_to(q, rows, cols, product):
        if q == 0:
            acc[rows, cols] = product
        else:
            acc[rows, cols] += product

    def dot_zx(q, i):
        def run():
            cols = slice(i * 256, i * 256 + 256)
            at = slice(CUT_AT[q], CUT_AT[q] + CUTS[q])
            add_to(
                q,
                slice(0, LEN),
                cols,
                jnp.dot(chunk(q), w_zx[at, cols], preferred_element_type=F32),
            )

        return run

    def dot_bc(q):
        def run():
            if q == 0:
                for load in (bc_load, tap_load, off_load, *small_loads[1:]):
                    load.wait()
                for sent in (bc_send, tap_send, off_send):
                    sent.wait_recv()
            at = slice(CUT_AT[q], CUT_AT[q] + CUTS[q])
            weights = w_bc[:, :, :, at].reshape(256, CUTS[q])
            add_to(
                q,
                slice(0, LEN),
                slice(1024, 1280),
                lax.dot_general(chunk(q), weights, NT, preferred_element_type=F32),
            )

        return run

    def dot_dt(q):
        def run():
            if q == 0:
                small_loads[0].wait()
            at = slice(CUT_AT[q], CUT_AT[q] + CUTS[q])
            add_to(
                q,
                slice(0, 8),
                slice(1280, 1280 + LEN),
                lax.dot_general(dt_in[:, at], chunk(q), NT, preferred_element_type=F32),
            )

        return run

    n_seg = lengths.shape[0]
    bounds = []
    run_sum = jnp.int32(0)
    for k in range(n_seg):
        run_sum = run_sum + lengths[k]
        bounds.append(run_sum)
    base = s * LEN

    def since(rows):
        pos = lax.broadcasted_iota(jnp.int32, (rows, 128), 0) + base
        seg_start = jnp.zeros((rows, 128), jnp.int32)
        for bound in bounds:
            seg_start = jnp.where(bound <= pos, jnp.maximum(seg_start, bound), seg_start)
        return pos - seg_start

    def ready():
        age = since(LEN)
        row = lax.broadcasted_iota(jnp.int32, (LEN, 128), 0)
        for j in range(1, 4):
            early[j - 1] = ((age >= j) & (row >= j)).astype(F32)
        ri = lax.broadcasted_iota(jnp.int32, (LEN, LEN), 0)
        ci = lax.broadcasted_iota(jnp.int32, (LEN, LEN), 1)
        same = segment_of(bounds, ci + base) == segment_of(bounds, ri + base)
        okay[...] = (same & (ri >= ci)).astype(F32)

    last = NQ - 1
    for t in range(NQ + 3):
        if t + LEAD < NQ:
            launch(t + LEAD)
        todo = []
        if t < NQ:
            todo = [split(t, part) for part in range(4)]
        if t == 0:
            todo.append(ready)
        if t >= 3:
            q = t - 3
            share(q, oc).wait_recv()
            todo += [dot_dt(q), dot_bc(q), dot_zx(q, 2), dot_zx(q, 3)]
            if q != last:
                todo += [dot_zx(q, 0), dot_zx(q, 1)]
        events = [(nearby, t), (far, t - 1), (across_own, t)]
        events += [(across_near, t - 1), (across_far, t - 2)]
        events = [(what, q) for what, q in events if 0 <= q < NQ]
        for i, (what, q) in enumerate(events):
            what(q)
            count = -(-len(todo) // (len(events) - i))
            for work in todo[:count]:
                work()
            todo = todo[count:]
        for work in todo:
            work()

    ext[16:, CHAN:] = acc[:, 1024:1280].astype(BF16)
    ext[16:, :CHAN] = acc[:, 512:1024].astype(BF16)
    halo = go(
        remote(ext.at[pl.ds(256, 16)], ext.at[pl.ds(0, 16)], misc_s.at[2], misc_r.at[2], seq=other)
    )
    head_row = lax.broadcasted_iota(jnp.int32, (8, LEN), 0)

    def by_head(ref, heads):
        values = jnp.zeros(heads.shape, F32)
        for h in range(8):
            values = jnp.where(heads == h, ref[h], values)
        return values

    rate = by_head(rate_in, head_row)
    dt_own = jax.nn.softplus(acc[:8, 1280 : 1280 + LEN] + by_head(dt_bias, head_row))
    steps[s] = dt_own
    step_send = go(remote(steps.at[s], steps.at[s], misc_s.at[3], misc_r.at[3], seq=other))
    upper = (
        lax.broadcasted_iota(jnp.int32, (LEN, LEN), 0)
        <= lax.broadcasted_iota(jnp.int32, (LEN, LEN), 1)
    ).astype(BF16)
    head_of = lax.broadcasted_iota(jnp.int32, (8, CHAN), 1) // 64
    row_of = lax.broadcasted_iota(jnp.int32, (24, CHAN), 0) % 8
    spread = (lax.broadcasted_iota(jnp.int32, (24, CHAN), 1) // 64 == row_of).astype(BF16)

    def terms(v):
        high = v.astype(BF16)
        rest = v - high.astype(F32)
        middle = rest.astype(BF16)
        return [high, middle, (rest - middle.astype(F32)).astype(BF16)]

    def cumulate(dt):
        parts = jnp.concatenate([t.astype(F32) for t in terms(-rate * dt)], axis=0).astype(BF16)
        sums = jnp.dot(parts, upper, preferred_element_type=F32)
        return sums[:8] + sums[8:16] + sums[16:]

    def widen(rows):
        parts = jnp.concatenate([t.astype(F32) for t in terms(rows)], axis=0).astype(BF16)
        return lax.dot_general(parts, spread, TN, preferred_element_type=F32)

    place = lax.broadcasted_iota(jnp.int32, (8, LEN), 1)
    seg_own = segment_of(bounds, place + base)
    seg_last = segment_of(bounds, jnp.full((8, LEN), LEN - 1, jnp.int32) + base)
    cum_r = cumulate(dt_own)
    into = jnp.exp(cum_r[:, LEN - 1 :] - cum_r) * dt_own * (seg_own == seg_last).astype(F32)
    into_wide = widen(into)

    def taps_for(i, row):
        if i < 4:
            cols = slice(i * 128, i * 128 + 128)
            return bias_x[:, cols] if row == 4 else conv_x[row : row + 1, cols]
        k = i - 4
        if row == 4:
            both = [t_bias[e, k : k + 1, :] for e in range(2)]
        else:
            both = [t_conv[e, row, k : k + 1, :] for e in range(2)]
        return jnp.concatenate(both, axis=1)

    def silu(v):
        return v * lax.logistic(v)

    ent_copy = []
    for i in (4, 0, 1, 2, 3, 5):
        cols = slice(i * 128, i * 128 + 128)
        v = ext[16:, cols].astype(F32)
        total = taps_for(i, 4) + taps_for(i, 0) * v
        for j in range(1, 4):
            total = total + taps_for(i, j) * pltpu.roll(v, j, 0) * early[j - 1]
        made = silu(total).astype(BF16)
        act[s, :, cols] = made
        if i < 4:
            x_in = (made.astype(F32) * into_wide[:, cols]).astype(BF16)
            ent_out[i] = lax.dot_general(
                act[s, :, CHAN : CHAN + STATES], x_in, TN, preferred_element_type=F32
            ).astype(BF16)
            ent_copy.append(
                go(remote(ent_out.at[i], ent_in.at[i], ent_s.at[i], ent_r.at[i], seq=other))
            )
    halo.wait_recv()

    @pl.when(s > 0)
    def _():
        age = since(16)
        for i in range(6):
            cols = slice(i * 128, i * 128 + 128)
            v = ext[:32, cols].astype(F32)
            total = taps_for(i, 4) + taps_for(i, 0) * v[16:]
            for j in range(1, 4):
                total = total + taps_for(i, j) * pltpu.roll(v, j, 0)[16:] * (age >= j).astype(F32)
            act[s, :16, cols] = silu(total).astype(BF16)

    seen = act.at[s, :, pl.ds(0, CHAN + STATES)]
    act_send = go(remote(seen, seen, misc_s.at[4], misc_r.at[4], seq=other))

    for i in range(2):
        cols = slice(i * 256, i * 256 + 256)
        at = slice(CUT_AT[last], CUT_AT[last] + CUTS[last])
        gate[:, cols] = (
            acc[:, cols] + jnp.dot(chunk(last), w_zx[at, cols], preferred_element_type=F32)
        ).astype(BF16)

    cum_c = cum_r.T
    b_own = act[s, :, CHAN : CHAN + STATES]
    c_own = act[s, :, CHAN + STATES :]
    lane = lax.broadcasted_iota(jnp.int32, (128, 128), 1)
    for r in range(2):
        rows = slice(r * 128, r * 128 + 128)
        past = slice(0, r * 128 + 128)
        scores = lax.dot_general(c_own[rows], b_own[past], NT, preferred_element_type=F32)
        scores = scores * okay[rows, past]
        for g in range(4):
            cols = slice(g * 128, g * 128 + 128)
            halves = []
            for h in (2 * g, 2 * g + 1):
                gap = jnp.minimum(cum_c[rows, h : h + 1] - cum_r[h : h + 1, past], 0.0)
                mix = jnp.exp(gap) * scores * dt_own[h : h + 1, past]
                halves.append(
                    jnp.dot(mix.astype(BF16), act[s, past, cols], preferred_element_type=F32)
                )
            acc[rows, cols] = jnp.where(lane < 64, halves[0], halves[1])

    seg_before = segment_of(bounds, jnp.full((8, LEN), LEN - 1, jnp.int32))
    carried = ((seg_own == seg_before) & (s > 0)).astype(F32)
    gain = widen(jnp.exp(cum_r) * carried)
    skips = by_head(skip_in, head_of[:1])
    for i in range(4):
        cols = slice(i * 128, i * 128 + 128)
        ent_copy[i].wait_recv()
        y_all = acc[:, cols] + jnp.dot(c_own, ent_in[i], preferred_element_type=F32) * gain[:, cols]
        y_all = y_all + skips[:, cols] * act[s, :, cols].astype(F32)
        gate[:, cols] = (y_all * silu(gate[:, cols].astype(F32))).astype(BF16)
    out_load.wait()

    def part(zz, yy, cc):
        return pl.ds(pl.multiple_of(zz * 64 + yy * 32 + cc * 16, 16), 16)

    a_copy = []
    b_copy = []

    def slab(q):
        return slice(SLAB_AT[q], SLAB_AT[q] + SLABS[q]), pl.ds(SLAB_AT[q], SLABS[q])

    def to_sib(q):
        cols, at = slab(q)
        acc[:, cols] = jnp.dot(gate[...], w_out[:, cols], preferred_element_type=F32)
        for zz in range(4):
            for yy in range(2):
                send_a[zz, yy, :, cols] = acc[part(zz, yy, oc), cols].astype(BF16)
        src, dst = send_a.at[:, :, :, at], recv_a.at[:, :, :, at]
        a_copy.append(go(remote(src, dst, rsa_s.at[q], rsa_r.at[q], tensor=sib)))

    def to_pal(q):
        cols, at = slab(q)
        a_copy[q].wait_recv()
        for zz in range(4):
            send_b[zz, :, cols] = (
                acc[part(zz, oy, c), cols] + recv_a[zz, oy, :, cols].astype(F32)
            ).astype(BF16)
        src, dst = send_b.at[:, :, at], recv_b.at[:, :, at]
        b_copy.append(go(remote(src, dst, rsb_s.at[q], rsb_r.at[q], tensor=ypal)))
        for zz in range(4):
            keep[zz, :, cols] = acc[part(zz, y, c), cols] + recv_a[zz, y, :, cols].astype(F32)

    def line_copy(i, q, device):
        src, dst = send_c.at[i, :, slab(q)[1]], recv_c.at[i, :, slab(q)[1]]
        return remote(src, dst, rsc_s.at[i, q], rsc_r.at[i, q], tensor=device)

    def to_line(q):
        cols, _ = slab(q)
        b_copy[q].wait_recv()

        def ship(i, zz, device):
            send_c[i, :, cols] = (keep[zz, :, cols] + recv_b[zz, :, cols].astype(F32)).astype(BF16)
            line_copy(i, q, device).start()

        @pl.when(ends)
        def _():
            ship(3, third, line["third"] if q in DIRECT else line["first"])
            ship(0, second, zpal[2])

        @pl.when(mid)
        def _():
            if q in DIRECT:
                ship(0, third, zpal[2])
            ship(1, second, line["inner"])

        ship(2, first, line["first"])

    def onward(q):
        cols, _ = slab(q)

        def take(i):
            line_copy(i, q, line["first"]).wait_recv()
            return recv_c[i, :, cols].astype(F32)

        @pl.when(mid)
        def _():
            if q not in DIRECT:
                far_sum = keep[third, :, cols] + recv_b[third, :, cols].astype(F32)
                send_c[0, :, cols] = (far_sum + take(3)).astype(BF16)
                line_copy(0, q, zpal[2]).start()
            keep[z, :, cols] = keep[z, :, cols] + take(1)

        if q in DIRECT:

            @pl.when(ends)
            def _():
                keep[z, :, cols] = keep[z, :, cols] + take(3)

    def finals_ready():
        step_send.wait_recv()
        act_send.wait_recv()
        cum_0 = cumulate(steps[0])
        cum_1 = cumulate(steps[1]) + cum_0[:, LEN - 1 :]
        seg_0 = segment_of(bounds, place)
        seg_1 = segment_of(bounds, place + LEN)
        ends_0 = jnp.zeros((8, LEN), F32)
        ends_1 = jnp.zeros((8, LEN), F32)
        for k in range(n_seg):
            spot_0 = (place == bounds[k] - 1).astype(F32) * cum_0
            spot_1 = (place + LEN == bounds[k] - 1).astype(F32) * cum_1
            end = jnp.sum(spot_0 + spot_1, axis=1, keepdims=True)
            ends_0 = jnp.where(seg_0 == k, end, ends_0)
            ends_1 = jnp.where(seg_1 == k, end, ends_1)
        w_0 = widen(jnp.exp(ends_0 - cum_0) * steps[0])
        w_1 = widen(jnp.exp(ends_1 - cum_1) * steps[1])
        xw_0 = (act[0, :, :CHAN].astype(F32) * w_0).astype(BF16)
        xw_1 = (act[1, :, :CHAN].astype(F32) * w_1).astype(BF16)
        b_0 = act[0, :, CHAN : CHAN + STATES]
        b_1 = act[1, :, CHAN : CHAN + STATES]
        spot = lax.broadcasted_iota(jnp.int32, (LEN, STATES), 0)
        col_0 = segment_of(bounds, spot)
        col_1 = segment_of(bounds, spot + LEN)

        def fill(k):
            m_0 = jnp.where(col_0 == k, b_0.astype(F32), 0.0).astype(BF16)
            m_1 = jnp.where(col_1 == k, b_1.astype(F32), 0.0).astype(BF16)
            finals[k] = lax.dot_general(
                xw_0, m_0, TN, preferred_element_type=F32
            ) + lax.dot_general(xw_1, m_1, TN, preferred_element_type=F32)

        return fill

    fill = None
    filled = 0
    for t in range(NR + BEHIND + 1):
        if t < NR:
            to_sib(t)
        if 0 <= t - 1 < NR:
            to_pal(t - 1)
        if 0 <= t - BEHIND < NR:
            to_line(t - BEHIND)
        if t > BEHIND:
            onward(t - BEHIND - 1)
        if t == NR:
            fill = finals_ready()
        elif t > NR:
            for k in range(filled, min(n_seg, filled + 2)):
                fill(k)
            filled = min(n_seg, filled + 2)
    for condition, copies in guarded.values():

        @pl.when(condition)
        def _():
            for copy in copies:
                copy.wait_send()

    for q in range(NR):
        cols, _ = slab(q)
        total = keep[z, :, cols] + recv_b[z, :, cols].astype(F32)
        for i in (2, 0):
            line_copy(i, q, zpal[2]).wait_recv()
            total = total + recv_c[i, :, cols].astype(F32)
        mixed[:, cols] = total.astype(BF16)
    for condition, places in ((ends, (3,)), (mid, (1,)), (z >= 0, (0, 2))):

        @pl.when(condition)
        def _():
            for i in places:
                for q in range(NR):
                    line_copy(i, q, zpal[2]).wait_send()

    for copy in started:
        copy.wait_send()


def settle_kernel(mixed_in, finals_in, mixed, finals, sems):
    copies = [
        pltpu.make_async_copy(finals_in, finals, sems.at[0]),
        pltpu.make_async_copy(mixed_in, mixed, sems.at[1]),
    ]
    for copy in copies:
        copy.start()
    for copy in copies:
        copy.wait()


def fused_body(
    tokens,
    lengths,
    proj_zx,
    proj_bc,
    proj_dt,
    conv_x,
    conv_bc,
    bias_x,
    bias_bc,
    dt_bias,
    decay_rate,
    skip_gain,
    proj_out,
):
    n_seg = lengths.shape[0]
    bc_view = proj_bc.transpose(1, 2, 0)
    dt_view = proj_dt.T
    any_spec = pl.BlockSpec(memory_space=pl.ANY)
    vmem = pl.BlockSpec(memory_space=pltpu.VMEM)
    smem = pl.BlockSpec(memory_space=pltpu.SMEM)
    dma = pltpu.SemaphoreType.DMA
    out_shape = (
        jax.ShapeDtypeStruct((ROWS, WIDE), BF16),
        jax.ShapeDtypeStruct((n_seg, CHAN, STATES), F32),
    )
    mixed, finals = pl.pallas_call(
        layer_kernel,
        out_shape=tuple(pltpu.VMEM(o.shape, o.dtype) for o in out_shape),
        in_specs=[smem, any_spec, any_spec, any_spec, any_spec, any_spec, any_spec]
        + [any_spec, any_spec, smem, smem, smem, any_spec],
        out_specs=(vmem, vmem),
        scratch_shapes=[
            pltpu.VMEM((4, 2, 2, ROWS, WIDE), BF16),
            pltpu.VMEM((WIDE, 2, CHAN), BF16),
            pltpu.VMEM((WIDE, 2 * CHAN), BF16),
            pltpu.VMEM((2, 2, 64, WIDE), BF16),
            pltpu.VMEM((CHAN, WIDE), BF16),
            pltpu.VMEM((2, 4, 2, 64), F32),
            pltpu.VMEM((2, 2, 64), F32),
            pltpu.VMEM((LEN, CHAN), BF16),
            pltpu.VMEM((16 + LEN, CHAN + 256), BF16),
            pltpu.VMEM((2, LEN, CHAN + 256), BF16),
            pltpu.VMEM((2, 8, LEN), F32),
            pltpu.VMEM((8, WIDE), BF16),
            pltpu.VMEM((4, CHAN), F32),
            pltpu.VMEM((1, CHAN), F32),
            pltpu.VMEM((3, LEN, 128), F32),
            pltpu.VMEM((LEN, LEN), F32),
            pltpu.VMEM((LEN, WIDE), F32),
            pltpu.VMEM((4, STATES, 128), BF16),
            pltpu.VMEM((4, STATES, 128), BF16),
            pltpu.VMEM((4, ROWS, WIDE), F32),
            pltpu.VMEM((4, 2, ROWS, WIDE), BF16),
            pltpu.VMEM((4, 2, ROWS, WIDE), BF16),
            pltpu.VMEM((4, ROWS, WIDE), BF16),
            pltpu.VMEM((4, ROWS, WIDE), BF16),
            pltpu.VMEM((4, ROWS, WIDE), BF16),
            pltpu.VMEM((4, ROWS, WIDE), BF16),
        ]
        + [dma((8,)), dma((NQ,)), dma((4, NQ)), dma((4, NQ))]
        + [dma((4, 2, NQ)), dma((NQ,)), dma((NQ,)), dma((6,)), dma((6,)), dma((4,)), dma((4,))]
        + [dma((NR,)), dma((NR,)), dma((NR,)), dma((NR,)), dma((4, NR)), dma((4, NR))],
        compiler_params=pltpu.CompilerParams(
            collective_id=0, has_side_effects=True, vmem_limit_bytes=56 << 20
        ),
    )(
        lengths,
        tokens,
        proj_zx,
        bc_view,
        dt_view,
        conv_x,
        bias_x.reshape(1, CHAN),
        conv_bc,
        bias_bc,
        dt_bias,
        decay_rate,
        skip_gain,
        proj_out,
    )
    mixed, finals = pl.pallas_call(
        settle_kernel,
        out_shape=out_shape,
        in_specs=[vmem, vmem],
        out_specs=(any_spec, any_spec),
        scratch_shapes=[dma((2,))],
    )(*(pltpu.with_memory_space_constraint(o, pltpu.VMEM) for o in (mixed, finals)))
    return (mixed, finals.reshape(n_seg, 8, 64, STATES))


def solution(mesh):
    in_specs = (
        P(("seq", "tensor"), None),
        P(),
        P(None, None, "tensor"),
        P(None, None, "tensor"),
        P(None, "tensor"),
        P(None, "tensor"),
        P(None, None, "tensor"),
        P("tensor"),
        P(None, "tensor"),
        P("tensor"),
        P("tensor"),
        P("tensor"),
        P("tensor", None),
    )
    out_specs = (P(("seq", "tensor"), None), P(None, "tensor", None, None))
    small = mesh.shape["seq"] == 2 and mesh.shape["tensor"] == 16
    chosen = fused_body if small else body
    return jax.shard_map(chosen, mesh=mesh, in_specs=in_specs, out_specs=out_specs, check_vma=False)
```

```python
import jax
import jax.numpy as jnp
from jax import lax
from jax.experimental import pallas as pl
from jax.experimental.pallas import tpu as pltpu
from jax.sharding import PartitionSpec as P

GROUPS = 8


def partner_2(value, axis, bit):
    mask = 2**bit
    pairs = [(source, source ^ mask) for source in range(lax.axis_size(axis))]
    return lax.ppermute(value, axis, pairs)


def passed_along(block, axis, distance):
    devices = range(lax.axis_size(axis))
    route = [(i - distance, i) for i in devices if i - distance in devices]
    return lax.ppermute(block, axis, route)


def group_columns(bc_own, tensor_index, steps_count):
    collected = bc_own
    for bit_number in range(steps_count):
        partner = partner_2(collected, "tensor", bit_number)
        upper = tensor_index // 2**bit_number % 2
        low_first = jnp.concatenate([collected, partner], axis=2)
        high_first = jnp.concatenate([partner, collected], axis=2)
        collected = jnp.where(upper == 0, low_first, high_first)
    return collected


def body(
    tokens,
    lengths,
    proj_zx,
    proj_bc,
    proj_dt,
    conv_x,
    conv_bc,
    bias_x,
    bias_bc,
    dt_bias,
    decay_rate,
    skip_gain,
    proj_out,
):
    highest = lax.Precision.HIGHEST
    tensor_size = lax.axis_size("tensor")
    rows_dev = tokens.shape[0]
    shard_len = rows_dev * tensor_size
    seq_index = lax.axis_index("seq")
    tensor_index = lax.axis_index("tensor")
    heads_dev = decay_rate.shape[0]
    width_zx = proj_zx.shape[2]
    head_size = width_zx // heads_dev
    cols_bc = proj_bc.shape[2]
    taps_count = conv_x.shape[0]
    model_width = tokens.shape[1]
    zx_flat = proj_zx.reshape(model_width, 2 * width_zx)
    bc_flat = proj_bc.reshape(model_width, 2 * cols_bc)
    piece = lax.all_gather(tokens, "tensor", axis=0, tiled=True)
    projected = jnp.concatenate(
        [
            jnp.dot(piece, zx_flat, preferred_element_type=jnp.float32),
            jnp.dot(piece, bc_flat, preferred_element_type=jnp.float32),
            jnp.dot(piece, proj_dt, preferred_element_type=jnp.float32),
        ],
        axis=1,
    )
    gate_in = projected[:, :width_zx].astype(jnp.bfloat16)
    conv_in = projected[:, width_zx : 2 * width_zx + 2 * cols_bc].astype(jnp.bfloat16)
    step_size = jax.nn.softplus(projected[:, 2 * width_zx + 2 * cols_bc :] + dt_bias[None, :])
    row_ids = jnp.arange(shard_len, dtype=jnp.int32)
    positions = seq_index * shard_len + row_ids
    later = jnp.arange(lengths.shape[0])
    bounds = jnp.sum(jnp.where(later[None, :] <= later[:, None], lengths[None, :], 0), axis=1)
    reached = bounds[None, :] <= positions[:, None]
    segment = jnp.sum(reached.astype(jnp.int32), axis=1)
    seg_start = jnp.max(jnp.where(reached, bounds[None, :], 0), axis=1)
    edge_rows = conv_in[shard_len - (taps_count - 1) :]
    before = passed_along(edge_rows, "seq", 1)
    extended = jnp.concatenate([before, conv_in], axis=0)
    conv_taps = jnp.concatenate([conv_x, conv_bc.reshape(taps_count, 2 * cols_bc)], axis=1)
    conv_offset = jnp.concatenate([bias_x, bias_bc.reshape(2 * cols_bc)])
    convolved = jnp.zeros((shard_len, conv_taps.shape[1]), jnp.float32) + conv_offset[None, :]
    for lag_index in range(taps_count):
        lagged = extended[
            taps_count - 1 - lag_index : taps_count - 1 - lag_index + shard_len
        ].astype(jnp.float32)
        keep_mask = (positions - lag_index >= seg_start).astype(jnp.float32)
        convolved = convolved + conv_taps[lag_index][None, :] * lagged * keep_mask[:, None]
    activated = jax.nn.silu(convolved).astype(jnp.bfloat16)
    x_conv = activated[:, :width_zx]
    bc_own = activated[:, width_zx:].reshape(shard_len, 2, cols_bc)
    per_group = tensor_size // GROUPS
    steps_count = per_group.bit_length() - 1
    bc_group = group_columns(bc_own, tensor_index, steps_count).astype(jnp.float32)
    state_in_proj = bc_group[:, 0]
    state_out_proj = bc_group[:, 1]
    x_float = x_conv.astype(jnp.float32).reshape(shard_len, heads_dev, head_size)
    log_decay = -decay_rate[None, :] * step_size
    lower = (row_ids[:, None] >= row_ids[None, :]).astype(jnp.float32)
    cumulative = jnp.dot(lower, log_decay, precision=highest)
    cumulative_t = cumulative.T
    valid = (segment[:, None] == segment[None, :]) & (row_ids[:, None] >= row_ids[None, :])
    spread = cumulative_t[:, :, None] - cumulative_t[:, None, :]
    decay_matrix = jnp.where(valid[None], jnp.exp(jnp.where(valid[None], spread, 0.0)), 0.0)
    scores = jnp.dot(state_out_proj, state_in_proj.T, precision=highest)
    mixing = decay_matrix * scores[None] * step_size.T[:, None, :]
    y_local = jnp.einsum("hts,shp->thp", mixing, x_float, precision=highest)
    before_pos = seq_index * shard_len - 1
    seg_before = jnp.sum((bounds <= before_pos).astype(jnp.int32))
    carried = (segment == seg_before).astype(jnp.float32)
    entry_gain = jnp.exp(cumulative) * carried[:, None]
    n_seg = lengths.shape[0]
    end_rows = bounds - 1 - seq_index * shard_len
    inside = (end_rows >= 0) & (end_rows < shard_len)
    target_rows = jnp.concatenate([end_rows, jnp.full((1,), shard_len - 1, jnp.int32)])
    target_seg = jnp.concatenate([jnp.arange(n_seg, dtype=jnp.int32), segment[shard_len - 1 :]])
    target_ok = jnp.concatenate([inside, jnp.ones((1,), bool)])
    picker = (row_ids[None, :] == target_rows[:, None]).astype(jnp.float32)
    cum_end = jnp.dot(picker, cumulative, precision=highest)
    reach = (
        target_ok[:, None]
        & (row_ids[None, :] <= target_rows[:, None])
        & (segment[None, :] == target_seg[:, None])
    )
    gap_end = cum_end[:, :, None] - cumulative_t[None, :, :]
    end_weight = (
        jnp.where(reach[:, None, :], jnp.exp(jnp.where(reach[:, None, :], gap_end, 0.0)), 0.0)
        * step_size.T[None]
    )
    states = jnp.einsum("khs,shp,sn->khpn", end_weight, x_float, state_in_proj, precision=highest)
    end_local = states[:n_seg]
    shard_state = states[n_seg]
    end_gain = jnp.where((target_ok & (target_seg == seg_before))[:, None], jnp.exp(cum_end), 0.0)
    shard_gain = end_gain[n_seg]
    end_gain_seg = end_gain[:n_seg]
    gathered = (
        lax.all_gather(shard_gain[None], "seq", axis=0, tiled=True),
        lax.all_gather(shard_state[None], "seq", axis=0, tiled=True),
        lax.all_gather(end_gain_seg[None], "seq", axis=0, tiled=True),
        lax.all_gather(end_local[None], "seq", axis=0, tiled=True),
    )
    gains_all, states_all, egains_all, elocal_all = gathered

    def fold_step(carry, item):
        gain_now, state_now = item
        return (gain_now[:, None, None] * carry + state_now, carry)

    last_state, incoming = lax.scan(
        fold_step, jnp.zeros(shard_state.shape, jnp.float32), (gains_all, states_all)
    )
    state_entry = lax.dynamic_index_in_dim(incoming, seq_index, 0, keepdims=False)
    final_states = jnp.sum(elocal_all + egains_all[:, :, :, None, None] * incoming[:, None], axis=0)
    y_entry = (
        jnp.einsum("tn,hpn->thp", state_out_proj, state_entry, precision=highest)
        * entry_gain[:, :, None]
    )
    y_total = y_local + y_entry + skip_gain[None, :, None] * x_float
    gate_values = jax.nn.silu(gate_in.astype(jnp.float32)).reshape(shard_len, heads_dev, head_size)
    gated = (y_total * gate_values).reshape(shard_len, width_zx).astype(jnp.bfloat16)
    mixed = lax.psum_scatter(
        jnp.dot(gated, proj_out, preferred_element_type=jnp.float32),
        "tensor",
        scatter_dimension=0,
        tiled=True,
    )
    return (mixed.astype(jnp.bfloat16), final_states)


F32 = jnp.float32
BF16 = jnp.bfloat16
ROWS = 16
LEN = 256
WIDE = 4096
CHAN = 512
STATES = 128
HIGH = lax.Precision.HIGHEST
NT = (((1,), (1,)), ((), ()))
TN = (((0,), (0,)), ((), ()))
CUTS = (1536, 1536, 1024)
LEAD = 2
SLABS = (256, 512, 512, 512, 512, 512, 512, 512, 256)
BEHIND = 4


def starts(widths):
    return tuple(sum(widths[:i]) for i in range(len(widths)))


CUT_AT = starts(CUTS)
SLAB_AT = starts(SLABS)
NQ = len(CUTS)
NR = len(SLABS)


def remote(src, dst, send, recv, **device):
    return pltpu.make_async_remote_copy(
        src_ref=src,
        dst_ref=dst,
        send_sem=send,
        recv_sem=recv,
        device_id=device,
        device_id_type=pl.DeviceIdType.MESH,
    )


def segment_of(bounds, pos):
    total = jnp.zeros(pos.shape, jnp.int32)
    for bound in bounds:
        total = total + (bound <= pos).astype(jnp.int32)
    return total


def layer_kernel(
    lengths,
    tok_in,
    zx_in,
    bc_in,
    dt_from,
    conv_from,
    bias_from,
    conv_bc,
    bias_bc,
    dt_bias,
    rate_in,
    skip_in,
    out_in,
    mixed,
    finals,
    tok,
    zx_raw,
    w_zx,
    w_bc,
    w_out,
    t_conv,
    t_bias,
    gate,
    ext,
    act,
    steps,
    dt_in,
    conv_x,
    bias_x,
    early,
    okay,
    acc,
    ent_out,
    ent_in,
    keep,
    send_a,
    recv_a,
    send_b,
    recv_b,
    send_c,
    recv_c,
    load_sem,
    zx_sem,
    z_s,
    y_s,
    got,
    sib_s,
    sib_r,
    misc_s,
    misc_r,
    ent_s,
    ent_r,
    rsa_s,
    rsa_r,
    rsb_s,
    rsb_r,
    rsc_s,
    rsc_r,
):
    s = lax.axis_index("seq")
    me = lax.axis_index("tensor")
    z = me // 4
    y = (me // 2) % 2
    c = me % 2
    oy = 1 - y
    oc = 1 - c
    sib = z * 4 + y * 2 + oc
    ypal = z * 4 + oy * 2 + c
    zpal = [((z + d) % 4) * 4 + y * 2 + c for d in range(4)]
    other = 1 - s

    ext[:16] = jnp.zeros((16, CHAN + 256), BF16)
    barrier = pltpu.get_barrier_semaphore()
    for pal in [sib, ypal] + zpal[1:]:
        pl.semaphore_signal(
            barrier, inc=1, device_id={"tensor": pal}, device_id_type=pl.DeviceIdType.MESH
        )
    pl.semaphore_signal(
        barrier, inc=1, device_id={"seq": other}, device_id_type=pl.DeviceIdType.MESH
    )

    own = pltpu.make_async_copy(tok_in, tok.at[z, y, c], load_sem.at[0])
    own.start()
    zx_loads = []
    for q in range(NQ):
        rows = pl.ds(CUT_AT[q], CUTS[q])
        load = pltpu.make_async_copy(zx_in.at[rows], zx_raw.at[rows], zx_sem.at[q])
        load.start()
        zx_loads.append(load)
    bc_load = pltpu.make_async_copy(bc_in, w_bc.at[:, c], load_sem.at[1])
    bc_load.start()
    tap_load = pltpu.make_async_copy(conv_bc, t_conv.at[c], load_sem.at[2])
    tap_load.start()
    off_load = pltpu.make_async_copy(bias_bc, t_bias.at[c], load_sem.at[5])
    off_load.start()
    small_loads = [
        pltpu.make_async_copy(src, dst, load_sem.at[i])
        for i, src, dst in ((4, dt_from, dt_in), (6, conv_from, conv_x), (7, bias_from, bias_x))
    ]
    for load in small_loads:
        load.start()
    out_load = pltpu.make_async_copy(out_in, w_out, load_sem.at[3])
    out_load.start()
    pl.semaphore_wait(barrier, 6)

    started = []

    def go(copy):
        copy.start()
        started.append(copy)
        return copy

    guarded = {}

    def maybe(name, condition, copy):
        pl.when(condition)(copy.start)
        guarded.setdefault(name, (condition, []))[1].append(copy)

    def hop(zz, yy, q, send, device):
        ref = tok.at[zz, yy, c, :, pl.ds(CUT_AT[q], CUTS[q])]
        return remote(ref, ref, send, got.at[zz, yy, q], tensor=device)

    def landed(zz, yy, q):
        hop(zz, yy, q, y_s.at[0, q], ypal).wait_recv()

    mid = (z == 1) | (z == 2)
    ends = (z == 0) | (z == 3)
    first = z + 1 - 2 * (z % 2)
    second = 2 - z // 2
    third = 3 - 3 * (z // 2)
    inner = jnp.where(mid, 3 - z, first)
    line = {k: zz * 4 + y * 2 + c for k, zz in (("first", first), ("inner", inner))}

    def launch(q):
        go(hop(z, y, q, z_s.at[0, q], zpal[2]))
        go(hop(z, y, q, y_s.at[0, q], ypal))
        go(hop(z, y, q, z_s.at[1, q], line["inner"]))
        maybe("mid", mid, hop(z, y, q, z_s.at[2, q], line["first"]))

    def nearby(q):
        @pl.when(mid)
        def _():
            landed(third, y, q)

        maybe("mid", mid, hop(third, y, q, z_s.at[3, q], line["first"]))
        landed(first, y, q)
        go(hop(first, y, q, y_s.at[1, q], ypal))
        landed(second, y, q)
        go(hop(second, y, q, y_s.at[2, q], ypal))

    def far(q):
        @pl.when(ends)
        def _():
            landed(third, y, q)

        go(hop(third, y, q, y_s.at[3, q], ypal))

    def across_own(q):
        landed(z, oy, q)

    def across_near(q):
        landed(first, oy, q)
        landed(second, oy, q)

    def across_far(q):
        landed(third, oy, q)
        go(share(q, c))

    def share(q, core):
        ref = tok.at[:, :, core, :, pl.ds(CUT_AT[q], CUTS[q])]
        return remote(ref, ref, sib_s.at[q], sib_r.at[q], tensor=sib)

    own.wait()
    for q in range(min(LEAD, NQ)):
        launch(q)
    bc_send = go(remote(bc_in, w_bc.at[:, c], misc_s.at[0], misc_r.at[0], tensor=sib))
    tap_send = go(remote(conv_bc, t_conv.at[c], misc_s.at[1], misc_r.at[1], tensor=sib))
    off_send = go(remote(bias_bc, t_bias.at[c], misc_s.at[5], misc_r.at[5], tensor=sib))

    def split(q, part):
        size = CUTS[q] // 4

        def run():
            if part == 0:
                zx_loads[q].wait()

            @pl.loop(0, size // 128)
            def _(j):
                at = pl.multiple_of(CUT_AT[q] + part * size + j * 128, 128)
                rows = pl.ds(at, 128)
                both = pltpu.einshape("abc->bac", zx_raw[rows])
                w_zx[rows, :CHAN] = both[0]
                w_zx[rows, CHAN:] = both[1]

        return run

    def chunk(q):
        at = slice(CUT_AT[q], CUT_AT[q] + CUTS[q])
        return tok[:, :, :, :, at].reshape(LEN, CUTS[q])

    def add_to(q, rows, cols, product):
        if q == 0:
            acc[rows, cols] = product
        else:
            acc[rows, cols] += product

    def dot_zx(q, i):
        def run():
            cols = slice(i * 256, i * 256 + 256)
            at = slice(CUT_AT[q], CUT_AT[q] + CUTS[q])
            add_to(
                q,
                slice(0, LEN),
                cols,
                jnp.dot(chunk(q), w_zx[at, cols], preferred_element_type=F32),
            )

        return run

    def dot_bc(q):
        def run():
            if q == 0:
                for load in (bc_load, tap_load, off_load, *small_loads[1:]):
                    load.wait()
                for sent in (bc_send, tap_send, off_send):
                    sent.wait_recv()
            at = slice(CUT_AT[q], CUT_AT[q] + CUTS[q])
            weights = w_bc[:, :, :, at].reshape(256, CUTS[q])
            add_to(
                q,
                slice(0, LEN),
                slice(1024, 1280),
                lax.dot_general(chunk(q), weights, NT, preferred_element_type=F32),
            )

        return run

    def dot_dt(q):
        def run():
            if q == 0:
                small_loads[0].wait()
            at = slice(CUT_AT[q], CUT_AT[q] + CUTS[q])
            add_to(
                q,
                slice(0, 8),
                slice(1280, 1280 + LEN),
                lax.dot_general(dt_in[:, at], chunk(q), NT, preferred_element_type=F32),
            )

        return run

    n_seg = lengths.shape[0]
    bounds = []
    run_sum = jnp.int32(0)
    for k in range(n_seg):
        run_sum = run_sum + lengths[k]
        bounds.append(run_sum)
    base = s * LEN

    def since(rows):
        pos = lax.broadcasted_iota(jnp.int32, (rows, 128), 0) + base
        seg_start = jnp.zeros((rows, 128), jnp.int32)
        for bound in bounds:
            seg_start = jnp.where(bound <= pos, jnp.maximum(seg_start, bound), seg_start)
        return pos - seg_start

    def ready():
        age = since(LEN)
        row = lax.broadcasted_iota(jnp.int32, (LEN, 128), 0)
        for j in range(1, 4):
            early[j - 1] = ((age >= j) & (row >= j)).astype(F32)
        ri = lax.broadcasted_iota(jnp.int32, (LEN, LEN), 0)
        ci = lax.broadcasted_iota(jnp.int32, (LEN, LEN), 1)
        same = segment_of(bounds, ci + base) == segment_of(bounds, ri + base)
        okay[...] = (same & (ri >= ci)).astype(F32)

    last = NQ - 1
    for t in range(NQ + 3):
        if t + LEAD < NQ:
            launch(t + LEAD)
        todo = []
        if t < NQ:
            todo = [split(t, part) for part in range(4)]
        if t == 0:
            todo.append(ready)
        if t >= 3:
            q = t - 3
            share(q, oc).wait_recv()
            todo += [dot_dt(q), dot_bc(q), dot_zx(q, 2), dot_zx(q, 3)]
            if q != last:
                todo += [dot_zx(q, 0), dot_zx(q, 1)]
        events = [(nearby, t), (far, t - 1), (across_own, t)]
        events += [(across_near, t - 1), (across_far, t - 2)]
        events = [(what, q) for what, q in events if 0 <= q < NQ]
        for i, (what, q) in enumerate(events):
            what(q)
            count = -(-len(todo) // (len(events) - i))
            for work in todo[:count]:
                work()
            todo = todo[count:]
        for work in todo:
            work()

    ext[16:, CHAN:] = acc[:, 1024:1280].astype(BF16)
    ext[16:, :CHAN] = acc[:, 512:1024].astype(BF16)
    halo = go(
        remote(ext.at[pl.ds(256, 16)], ext.at[pl.ds(0, 16)], misc_s.at[2], misc_r.at[2], seq=other)
    )
    head_row = lax.broadcasted_iota(jnp.int32, (8, LEN), 0)

    def by_head(ref, heads):
        values = jnp.zeros(heads.shape, F32)
        for h in range(8):
            values = jnp.where(heads == h, ref[h], values)
        return values

    rate = by_head(rate_in, head_row)
    dt_own = jax.nn.softplus(acc[:8, 1280 : 1280 + LEN] + by_head(dt_bias, head_row))
    steps[s] = dt_own
    step_send = go(remote(steps.at[s], steps.at[s], misc_s.at[3], misc_r.at[3], seq=other))
    upper = (
        lax.broadcasted_iota(jnp.int32, (LEN, LEN), 0)
        <= lax.broadcasted_iota(jnp.int32, (LEN, LEN), 1)
    ).astype(BF16)
    head_of = lax.broadcasted_iota(jnp.int32, (8, CHAN), 1) // 64
    row_of = lax.broadcasted_iota(jnp.int32, (24, CHAN), 0) % 8
    spread = (lax.broadcasted_iota(jnp.int32, (24, CHAN), 1) // 64 == row_of).astype(BF16)

    def terms(v):
        high = v.astype(BF16)
        rest = v - high.astype(F32)
        middle = rest.astype(BF16)
        return [high, middle, (rest - middle.astype(F32)).astype(BF16)]

    def cumulate(dt):
        parts = jnp.concatenate([t.astype(F32) for t in terms(-rate * dt)], axis=0).astype(BF16)
        sums = jnp.dot(parts, upper, preferred_element_type=F32)
        return sums[:8] + sums[8:16] + sums[16:]

    def widen(rows):
        parts = jnp.concatenate([t.astype(F32) for t in terms(rows)], axis=0).astype(BF16)
        return lax.dot_general(parts, spread, TN, preferred_element_type=F32)

    place = lax.broadcasted_iota(jnp.int32, (8, LEN), 1)
    seg_own = segment_of(bounds, place + base)
    seg_last = segment_of(bounds, jnp.full((8, LEN), LEN - 1, jnp.int32) + base)
    cum_r = cumulate(dt_own)
    into = jnp.exp(cum_r[:, LEN - 1 :] - cum_r) * dt_own * (seg_own == seg_last).astype(F32)
    into_wide = widen(into)

    def taps_for(i, row):
        if i < 4:
            cols = slice(i * 128, i * 128 + 128)
            return bias_x[:, cols] if row == 4 else conv_x[row : row + 1, cols]
        k = i - 4
        if row == 4:
            both = [t_bias[e, k : k + 1, :] for e in range(2)]
        else:
            both = [t_conv[e, row, k : k + 1, :] for e in range(2)]
        return jnp.concatenate(both, axis=1)

    def silu(v):
        return v * lax.logistic(v)

    ent_copy = []
    for i in (4, 0, 1, 2, 3, 5):
        cols = slice(i * 128, i * 128 + 128)
        v = ext[16:, cols].astype(F32)
        total = taps_for(i, 4) + taps_for(i, 0) * v
        for j in range(1, 4):
            total = total + taps_for(i, j) * pltpu.roll(v, j, 0) * early[j - 1]
        made = silu(total).astype(BF16)
        act[s, :, cols] = made
        if i < 4:
            x_in = (made.astype(F32) * into_wide[:, cols]).astype(BF16)
            ent_out[i] = lax.dot_general(
                act[s, :, CHAN : CHAN + STATES], x_in, TN, preferred_element_type=F32
            ).astype(BF16)
            ent_copy.append(
                go(remote(ent_out.at[i], ent_in.at[i], ent_s.at[i], ent_r.at[i], seq=other))
            )
    halo.wait_recv()

    @pl.when(s > 0)
    def _():
        age = since(16)
        for i in range(6):
            cols = slice(i * 128, i * 128 + 128)
            v = ext[:32, cols].astype(F32)
            total = taps_for(i, 4) + taps_for(i, 0) * v[16:]
            for j in range(1, 4):
                total = total + taps_for(i, j) * pltpu.roll(v, j, 0)[16:] * (age >= j).astype(F32)
            act[s, :16, cols] = silu(total).astype(BF16)

    seen = act.at[s, :, pl.ds(0, CHAN + STATES)]
    act_send = go(remote(seen, seen, misc_s.at[4], misc_r.at[4], seq=other))

    for i in range(2):
        cols = slice(i * 256, i * 256 + 256)
        at = slice(CUT_AT[last], CUT_AT[last] + CUTS[last])
        gate[:, cols] = (
            acc[:, cols] + jnp.dot(chunk(last), w_zx[at, cols], preferred_element_type=F32)
        ).astype(BF16)

    cum_c = cum_r.T
    b_own = act[s, :, CHAN : CHAN + STATES]
    c_own = act[s, :, CHAN + STATES :]
    lane = lax.broadcasted_iota(jnp.int32, (128, 128), 1)
    for r in range(2):
        rows = slice(r * 128, r * 128 + 128)
        past = slice(0, r * 128 + 128)
        scores = lax.dot_general(c_own[rows], b_own[past], NT, preferred_element_type=F32)
        scores = scores * okay[rows, past]
        for g in range(4):
            cols = slice(g * 128, g * 128 + 128)
            halves = []
            for h in (2 * g, 2 * g + 1):
                gap = jnp.minimum(cum_c[rows, h : h + 1] - cum_r[h : h + 1, past], 0.0)
                mix = jnp.exp(gap) * scores * dt_own[h : h + 1, past]
                halves.append(
                    jnp.dot(mix.astype(BF16), act[s, past, cols], preferred_element_type=F32)
                )
            acc[rows, cols] = jnp.where(lane < 64, halves[0], halves[1])

    seg_before = segment_of(bounds, jnp.full((8, LEN), LEN - 1, jnp.int32))
    carried = ((seg_own == seg_before) & (s > 0)).astype(F32)
    gain = widen(jnp.exp(cum_r) * carried)
    skips = by_head(skip_in, head_of[:1])
    for i in range(4):
        cols = slice(i * 128, i * 128 + 128)
        ent_copy[i].wait_recv()
        y_all = acc[:, cols] + jnp.dot(c_own, ent_in[i], preferred_element_type=F32) * gain[:, cols]
        y_all = y_all + skips[:, cols] * act[s, :, cols].astype(F32)
        gate[:, cols] = (y_all * silu(gate[:, cols].astype(F32))).astype(BF16)
    out_load.wait()

    def part(zz, yy, cc):
        return pl.ds(pl.multiple_of(zz * 64 + yy * 32 + cc * 16, 16), 16)

    a_copy = []
    b_copy = []
    c_copy = []

    def slab(q):
        return slice(SLAB_AT[q], SLAB_AT[q] + SLABS[q]), pl.ds(SLAB_AT[q], SLABS[q])

    def to_sib(q):
        cols, at = slab(q)
        acc[:, cols] = jnp.dot(gate[...], w_out[:, cols], preferred_element_type=F32)
        for zz in range(4):
            for yy in range(2):
                send_a[zz, yy, :, cols] = acc[part(zz, yy, oc), cols].astype(BF16)
        src, dst = send_a.at[:, :, :, at], recv_a.at[:, :, :, at]
        a_copy.append(go(remote(src, dst, rsa_s.at[q], rsa_r.at[q], tensor=sib)))

    def to_pal(q):
        cols, at = slab(q)
        a_copy[q].wait_recv()
        for zz in range(4):
            send_b[zz, :, cols] = (
                acc[part(zz, oy, c), cols] + recv_a[zz, oy, :, cols].astype(F32)
            ).astype(BF16)
        src, dst = send_b.at[:, :, at], recv_b.at[:, :, at]
        b_copy.append(go(remote(src, dst, rsb_s.at[q], rsb_r.at[q], tensor=ypal)))
        for zz in range(4):
            keep[zz, :, cols] = acc[part(zz, y, c), cols] + recv_a[zz, y, :, cols].astype(F32)

    def to_line(q):
        cols, at = slab(q)
        b_copy[q].wait_recv()
        for d in (2, 1, 3):
            zz = (z + d) % 4
            send_c[d, :, cols] = (keep[zz, :, cols] + recv_b[zz, :, cols].astype(F32)).astype(BF16)
            src, dst = send_c.at[d, :, at], recv_c.at[d, :, at]
            c_copy.append(
                go(remote(src, dst, rsc_s.at[d, q], rsc_r.at[d, q], tensor=zpal[d]))
            )

    def finals_ready():
        step_send.wait_recv()
        act_send.wait_recv()
        cum_0 = cumulate(steps[0])
        cum_1 = cumulate(steps[1]) + cum_0[:, LEN - 1 :]
        seg_0 = segment_of(bounds, place)
        seg_1 = segment_of(bounds, place + LEN)
        ends_0 = jnp.zeros((8, LEN), F32)
        ends_1 = jnp.zeros((8, LEN), F32)
        for k in range(n_seg):
            spot_0 = (place == bounds[k] - 1).astype(F32) * cum_0
            spot_1 = (place + LEN == bounds[k] - 1).astype(F32) * cum_1
            end = jnp.sum(spot_0 + spot_1, axis=1, keepdims=True)
            ends_0 = jnp.where(seg_0 == k, end, ends_0)
            ends_1 = jnp.where(seg_1 == k, end, ends_1)
        w_0 = widen(jnp.exp(ends_0 - cum_0) * steps[0])
        w_1 = widen(jnp.exp(ends_1 - cum_1) * steps[1])
        xw_0 = (act[0, :, :CHAN].astype(F32) * w_0).astype(BF16)
        xw_1 = (act[1, :, :CHAN].astype(F32) * w_1).astype(BF16)
        b_0 = act[0, :, CHAN : CHAN + STATES]
        b_1 = act[1, :, CHAN : CHAN + STATES]
        spot = lax.broadcasted_iota(jnp.int32, (LEN, STATES), 0)
        col_0 = segment_of(bounds, spot)
        col_1 = segment_of(bounds, spot + LEN)

        def fill(k):
            m_0 = jnp.where(col_0 == k, b_0.astype(F32), 0.0).astype(BF16)
            m_1 = jnp.where(col_1 == k, b_1.astype(F32), 0.0).astype(BF16)
            finals[k] = lax.dot_general(
                xw_0, m_0, TN, preferred_element_type=F32
            ) + lax.dot_general(xw_1, m_1, TN, preferred_element_type=F32)

        return fill

    fill = None
    filled = 0
    for t in range(NR + BEHIND):
        if t < NR:
            to_sib(t)
        if 0 <= t - 1 < NR:
            to_pal(t - 1)
        if t >= BEHIND:
            to_line(t - BEHIND)
        if t == NR:
            fill = finals_ready()
        elif t > NR:
            for k in range(filled, min(n_seg, filled + 2)):
                fill(k)
            filled = min(n_seg, filled + 2)
    for condition, copies in guarded.values():

        @pl.when(condition)
        def _():
            for copy in copies:
                copy.wait_send()

    for q in range(NR):
        cols, _ = slab(q)
        total = keep[z, :, cols] + recv_b[z, :, cols].astype(F32)
        for i, d in enumerate((2, 1, 3)):
            c_copy[q * 3 + i].wait_recv()
            total = total + recv_c[d, :, cols].astype(F32)
        mixed[:, cols] = total.astype(BF16)
    for copy in started:
        copy.wait_send()


def settle_kernel(mixed_in, finals_in, mixed, finals, sems):
    copies = [
        pltpu.make_async_copy(finals_in, finals, sems.at[0]),
        pltpu.make_async_copy(mixed_in, mixed, sems.at[1]),
    ]
    for copy in copies:
        copy.start()
    for copy in copies:
        copy.wait()


def fused_body(
    tokens,
    lengths,
    proj_zx,
    proj_bc,
    proj_dt,
    conv_x,
    conv_bc,
    bias_x,
    bias_bc,
    dt_bias,
    decay_rate,
    skip_gain,
    proj_out,
):
    n_seg = lengths.shape[0]
    bc_view = proj_bc.transpose(1, 2, 0)
    dt_view = proj_dt.T
    any_spec = pl.BlockSpec(memory_space=pl.ANY)
    vmem = pl.BlockSpec(memory_space=pltpu.VMEM)
    smem = pl.BlockSpec(memory_space=pltpu.SMEM)
    dma = pltpu.SemaphoreType.DMA
    out_shape = (
        jax.ShapeDtypeStruct((ROWS, WIDE), BF16),
        jax.ShapeDtypeStruct((n_seg, CHAN, STATES), F32),
    )
    mixed, finals = pl.pallas_call(
        layer_kernel,
        out_shape=tuple(pltpu.VMEM(o.shape, o.dtype) for o in out_shape),
        in_specs=[smem, any_spec, any_spec, any_spec, any_spec, any_spec, any_spec]
        + [any_spec, any_spec, smem, smem, smem, any_spec],
        out_specs=(vmem, vmem),
        scratch_shapes=[
            pltpu.VMEM((4, 2, 2, ROWS, WIDE), BF16),
            pltpu.VMEM((WIDE, 2, CHAN), BF16),
            pltpu.VMEM((WIDE, 2 * CHAN), BF16),
            pltpu.VMEM((2, 2, 64, WIDE), BF16),
            pltpu.VMEM((CHAN, WIDE), BF16),
            pltpu.VMEM((2, 4, 2, 64), F32),
            pltpu.VMEM((2, 2, 64), F32),
            pltpu.VMEM((LEN, CHAN), BF16),
            pltpu.VMEM((16 + LEN, CHAN + 256), BF16),
            pltpu.VMEM((2, LEN, CHAN + 256), BF16),
            pltpu.VMEM((2, 8, LEN), F32),
            pltpu.VMEM((8, WIDE), BF16),
            pltpu.VMEM((4, CHAN), F32),
            pltpu.VMEM((1, CHAN), F32),
            pltpu.VMEM((3, LEN, 128), F32),
            pltpu.VMEM((LEN, LEN), F32),
            pltpu.VMEM((LEN, WIDE), F32),
            pltpu.VMEM((4, STATES, 128), BF16),
            pltpu.VMEM((4, STATES, 128), BF16),
            pltpu.VMEM((4, ROWS, WIDE), F32),
            pltpu.VMEM((4, 2, ROWS, WIDE), BF16),
            pltpu.VMEM((4, 2, ROWS, WIDE), BF16),
            pltpu.VMEM((4, ROWS, WIDE), BF16),
            pltpu.VMEM((4, ROWS, WIDE), BF16),
            pltpu.VMEM((4, ROWS, WIDE), BF16),
            pltpu.VMEM((4, ROWS, WIDE), BF16),
        ]
        + [dma((8,)), dma((NQ,)), dma((4, NQ)), dma((4, NQ))]
        + [dma((4, 2, NQ)), dma((NQ,)), dma((NQ,)), dma((6,)), dma((6,)), dma((4,)), dma((4,))]
        + [dma((NR,)), dma((NR,)), dma((NR,)), dma((NR,)), dma((4, NR)), dma((4, NR))],
        compiler_params=pltpu.CompilerParams(
            collective_id=0, has_side_effects=True, vmem_limit_bytes=56 << 20
        ),
    )(
        lengths,
        tokens,
        proj_zx,
        bc_view,
        dt_view,
        conv_x,
        bias_x.reshape(1, CHAN),
        conv_bc,
        bias_bc,
        dt_bias,
        decay_rate,
        skip_gain,
        proj_out,
    )
    mixed, finals = pl.pallas_call(
        settle_kernel,
        out_shape=out_shape,
        in_specs=[vmem, vmem],
        out_specs=(any_spec, any_spec),
        scratch_shapes=[dma((2,))],
    )(*(pltpu.with_memory_space_constraint(o, pltpu.VMEM) for o in (mixed, finals)))
    return (mixed, finals.reshape(n_seg, 8, 64, STATES))


def solution(mesh):
    in_specs = (
        P(("seq", "tensor"), None),
        P(),
        P(None, None, "tensor"),
        P(None, None, "tensor"),
        P(None, "tensor"),
        P(None, "tensor"),
        P(None, None, "tensor"),
        P("tensor"),
        P(None, "tensor"),
        P("tensor"),
        P("tensor"),
        P("tensor"),
        P("tensor", None),
    )
    out_specs = (P(("seq", "tensor"), None), P(None, "tensor", None, None))
    small = mesh.shape["seq"] == 2 and mesh.shape["tensor"] == 16
    chosen = fused_body if small else body
    return jax.shard_map(chosen, mesh=mesh, in_specs=in_specs, out_specs=out_specs, check_vma=False)
```

```python
import jax
import jax.numpy as jnp
from jax import lax
from jax.experimental import pallas as pl
from jax.experimental.pallas import tpu as pltpu
from jax.sharding import PartitionSpec as P

GROUPS = 8


def partner_2(value, axis, bit):
    mask = 2**bit
    pairs = [(source, source ^ mask) for source in range(lax.axis_size(axis))]
    return lax.ppermute(value, axis, pairs)


def passed_along(block, axis, distance):
    devices = range(lax.axis_size(axis))
    route = [(i - distance, i) for i in devices if i - distance in devices]
    return lax.ppermute(block, axis, route)


def group_columns(bc_own, tensor_index, steps_count):
    collected = bc_own
    for bit_number in range(steps_count):
        partner = partner_2(collected, "tensor", bit_number)
        upper = tensor_index // 2**bit_number % 2
        low_first = jnp.concatenate([collected, partner], axis=2)
        high_first = jnp.concatenate([partner, collected], axis=2)
        collected = jnp.where(upper == 0, low_first, high_first)
    return collected


def body(
    tokens,
    lengths,
    proj_zx,
    proj_bc,
    proj_dt,
    conv_x,
    conv_bc,
    bias_x,
    bias_bc,
    dt_bias,
    decay_rate,
    skip_gain,
    proj_out,
):
    highest = lax.Precision.HIGHEST
    tensor_size = lax.axis_size("tensor")
    rows_dev = tokens.shape[0]
    shard_len = rows_dev * tensor_size
    seq_index = lax.axis_index("seq")
    tensor_index = lax.axis_index("tensor")
    heads_dev = decay_rate.shape[0]
    width_zx = proj_zx.shape[2]
    head_size = width_zx // heads_dev
    cols_bc = proj_bc.shape[2]
    taps_count = conv_x.shape[0]
    model_width = tokens.shape[1]
    zx_flat = proj_zx.reshape(model_width, 2 * width_zx)
    bc_flat = proj_bc.reshape(model_width, 2 * cols_bc)
    piece = lax.all_gather(tokens, "tensor", axis=0, tiled=True)
    projected = jnp.concatenate(
        [
            jnp.dot(piece, zx_flat, preferred_element_type=jnp.float32),
            jnp.dot(piece, bc_flat, preferred_element_type=jnp.float32),
            jnp.dot(piece, proj_dt, preferred_element_type=jnp.float32),
        ],
        axis=1,
    )
    gate_in = projected[:, :width_zx].astype(jnp.bfloat16)
    conv_in = projected[:, width_zx : 2 * width_zx + 2 * cols_bc].astype(jnp.bfloat16)
    step_size = jax.nn.softplus(projected[:, 2 * width_zx + 2 * cols_bc :] + dt_bias[None, :])
    row_ids = jnp.arange(shard_len, dtype=jnp.int32)
    positions = seq_index * shard_len + row_ids
    later = jnp.arange(lengths.shape[0])
    bounds = jnp.sum(jnp.where(later[None, :] <= later[:, None], lengths[None, :], 0), axis=1)
    reached = bounds[None, :] <= positions[:, None]
    segment = jnp.sum(reached.astype(jnp.int32), axis=1)
    seg_start = jnp.max(jnp.where(reached, bounds[None, :], 0), axis=1)
    edge_rows = conv_in[shard_len - (taps_count - 1) :]
    before = passed_along(edge_rows, "seq", 1)
    extended = jnp.concatenate([before, conv_in], axis=0)
    conv_taps = jnp.concatenate([conv_x, conv_bc.reshape(taps_count, 2 * cols_bc)], axis=1)
    conv_offset = jnp.concatenate([bias_x, bias_bc.reshape(2 * cols_bc)])
    convolved = jnp.zeros((shard_len, conv_taps.shape[1]), jnp.float32) + conv_offset[None, :]
    for lag_index in range(taps_count):
        lagged = extended[
            taps_count - 1 - lag_index : taps_count - 1 - lag_index + shard_len
        ].astype(jnp.float32)
        keep_mask = (positions - lag_index >= seg_start).astype(jnp.float32)
        convolved = convolved + conv_taps[lag_index][None, :] * lagged * keep_mask[:, None]
    activated = jax.nn.silu(convolved).astype(jnp.bfloat16)
    x_conv = activated[:, :width_zx]
    bc_own = activated[:, width_zx:].reshape(shard_len, 2, cols_bc)
    per_group = tensor_size // GROUPS
    steps_count = per_group.bit_length() - 1
    bc_group = group_columns(bc_own, tensor_index, steps_count).astype(jnp.float32)
    state_in_proj = bc_group[:, 0]
    state_out_proj = bc_group[:, 1]
    x_float = x_conv.astype(jnp.float32).reshape(shard_len, heads_dev, head_size)
    log_decay = -decay_rate[None, :] * step_size
    lower = (row_ids[:, None] >= row_ids[None, :]).astype(jnp.float32)
    cumulative = jnp.dot(lower, log_decay, precision=highest)
    cumulative_t = cumulative.T
    valid = (segment[:, None] == segment[None, :]) & (row_ids[:, None] >= row_ids[None, :])
    spread = cumulative_t[:, :, None] - cumulative_t[:, None, :]
    decay_matrix = jnp.where(valid[None], jnp.exp(jnp.where(valid[None], spread, 0.0)), 0.0)
    scores = jnp.dot(state_out_proj, state_in_proj.T, precision=highest)
    mixing = decay_matrix * scores[None] * step_size.T[:, None, :]
    y_local = jnp.einsum("hts,shp->thp", mixing, x_float, precision=highest)
    before_pos = seq_index * shard_len - 1
    seg_before = jnp.sum((bounds <= before_pos).astype(jnp.int32))
    carried = (segment == seg_before).astype(jnp.float32)
    entry_gain = jnp.exp(cumulative) * carried[:, None]
    n_seg = lengths.shape[0]
    end_rows = bounds - 1 - seq_index * shard_len
    inside = (end_rows >= 0) & (end_rows < shard_len)
    target_rows = jnp.concatenate([end_rows, jnp.full((1,), shard_len - 1, jnp.int32)])
    target_seg = jnp.concatenate([jnp.arange(n_seg, dtype=jnp.int32), segment[shard_len - 1 :]])
    target_ok = jnp.concatenate([inside, jnp.ones((1,), bool)])
    picker = (row_ids[None, :] == target_rows[:, None]).astype(jnp.float32)
    cum_end = jnp.dot(picker, cumulative, precision=highest)
    reach = (
        target_ok[:, None]
        & (row_ids[None, :] <= target_rows[:, None])
        & (segment[None, :] == target_seg[:, None])
    )
    gap_end = cum_end[:, :, None] - cumulative_t[None, :, :]
    end_weight = (
        jnp.where(reach[:, None, :], jnp.exp(jnp.where(reach[:, None, :], gap_end, 0.0)), 0.0)
        * step_size.T[None]
    )
    states = jnp.einsum("khs,shp,sn->khpn", end_weight, x_float, state_in_proj, precision=highest)
    end_local = states[:n_seg]
    shard_state = states[n_seg]
    end_gain = jnp.where((target_ok & (target_seg == seg_before))[:, None], jnp.exp(cum_end), 0.0)
    shard_gain = end_gain[n_seg]
    end_gain_seg = end_gain[:n_seg]
    gathered = (
        lax.all_gather(shard_gain[None], "seq", axis=0, tiled=True),
        lax.all_gather(shard_state[None], "seq", axis=0, tiled=True),
        lax.all_gather(end_gain_seg[None], "seq", axis=0, tiled=True),
        lax.all_gather(end_local[None], "seq", axis=0, tiled=True),
    )
    gains_all, states_all, egains_all, elocal_all = gathered

    def fold_step(carry, item):
        gain_now, state_now = item
        return (gain_now[:, None, None] * carry + state_now, carry)

    last_state, incoming = lax.scan(
        fold_step, jnp.zeros(shard_state.shape, jnp.float32), (gains_all, states_all)
    )
    state_entry = lax.dynamic_index_in_dim(incoming, seq_index, 0, keepdims=False)
    final_states = jnp.sum(elocal_all + egains_all[:, :, :, None, None] * incoming[:, None], axis=0)
    y_entry = (
        jnp.einsum("tn,hpn->thp", state_out_proj, state_entry, precision=highest)
        * entry_gain[:, :, None]
    )
    y_total = y_local + y_entry + skip_gain[None, :, None] * x_float
    gate_values = jax.nn.silu(gate_in.astype(jnp.float32)).reshape(shard_len, heads_dev, head_size)
    gated = (y_total * gate_values).reshape(shard_len, width_zx).astype(jnp.bfloat16)
    mixed = lax.psum_scatter(
        jnp.dot(gated, proj_out, preferred_element_type=jnp.float32),
        "tensor",
        scatter_dimension=0,
        tiled=True,
    )
    return (mixed.astype(jnp.bfloat16), final_states)


F32 = jnp.float32
BF16 = jnp.bfloat16
ROWS = 16
LEN = 256
WIDE = 4096
CHAN = 512
STATES = 128
HIGH = lax.Precision.HIGHEST
NT = (((1,), (1,)), ((), ()))
TN = (((0,), (0,)), ((), ()))
CUTS = (1536, 1536, 1024)
LEAD = 2
SLABS = (768, 256, 512, 512, 512, 512, 512, 512)
BEHIND = 4


def starts(widths):
    return tuple(sum(widths[:i]) for i in range(len(widths)))


CUT_AT = starts(CUTS)
SLAB_AT = starts(SLABS)
NQ = len(CUTS)
NR = len(SLABS)


def remote(src, dst, send, recv, **device):
    return pltpu.make_async_remote_copy(
        src_ref=src,
        dst_ref=dst,
        send_sem=send,
        recv_sem=recv,
        device_id=device,
        device_id_type=pl.DeviceIdType.MESH,
    )


def segment_of(bounds, pos):
    total = jnp.zeros(pos.shape, jnp.int32)
    for bound in bounds:
        total = total + (bound <= pos).astype(jnp.int32)
    return total


def layer_kernel(
    lengths,
    tok_in,
    zx_in,
    bc_in,
    dt_from,
    conv_from,
    bias_from,
    conv_bc,
    bias_bc,
    dt_bias,
    rate_in,
    skip_in,
    out_in,
    mixed,
    finals,
    tok,
    zx_raw,
    w_zx,
    w_bc,
    w_out,
    t_conv,
    t_bias,
    gate,
    ext,
    act,
    steps,
    dt_in,
    conv_x,
    bias_x,
    early,
    okay,
    acc,
    ent_out,
    ent_in,
    keep,
    send_a,
    recv_a,
    send_b,
    recv_b,
    send_c,
    recv_c,
    send_d,
    recv_d,
    send_e,
    recv_e,
    load_sem,
    zx_sem,
    z_s,
    y_s,
    got,
    sib_s,
    sib_r,
    misc_s,
    misc_r,
    ent_s,
    ent_r,
    rsa_s,
    rsa_r,
    rsb_s,
    rsb_r,
    rsc_s,
    rsc_r,
    rsd_s,
    rsd_r,
):
    s = lax.axis_index("seq")
    me = lax.axis_index("tensor")
    z = me // 4
    y = (me // 2) % 2
    c = me % 2
    oy = 1 - y
    oc = 1 - c
    sib = z * 4 + y * 2 + oc
    ypal = z * 4 + oy * 2 + c
    zpal = [((z + d) % 4) * 4 + y * 2 + c for d in range(4)]
    other = 1 - s

    ext[:16] = jnp.zeros((16, CHAN + 256), BF16)
    barrier = pltpu.get_barrier_semaphore()
    for pal in [sib, ypal] + zpal[1:]:
        pl.semaphore_signal(
            barrier, inc=1, device_id={"tensor": pal}, device_id_type=pl.DeviceIdType.MESH
        )
    pl.semaphore_signal(
        barrier, inc=1, device_id={"seq": other}, device_id_type=pl.DeviceIdType.MESH
    )

    own = pltpu.make_async_copy(tok_in, tok.at[z, y, c], load_sem.at[0])
    own.start()
    zx_loads = []
    for q in range(NQ):
        rows = pl.ds(CUT_AT[q], CUTS[q])
        load = pltpu.make_async_copy(zx_in.at[rows], zx_raw.at[rows], zx_sem.at[q])
        load.start()
        zx_loads.append(load)
    bc_load = pltpu.make_async_copy(bc_in, w_bc.at[:, c], load_sem.at[1])
    bc_load.start()
    tap_load = pltpu.make_async_copy(conv_bc, t_conv.at[c], load_sem.at[2])
    tap_load.start()
    off_load = pltpu.make_async_copy(bias_bc, t_bias.at[c], load_sem.at[5])
    off_load.start()
    small_loads = [
        pltpu.make_async_copy(src, dst, load_sem.at[i])
        for i, src, dst in ((4, dt_from, dt_in), (6, conv_from, conv_x), (7, bias_from, bias_x))
    ]
    for load in small_loads:
        load.start()
    out_load = pltpu.make_async_copy(out_in, w_out, load_sem.at[3])
    out_load.start()
    pl.semaphore_wait(barrier, 6)

    started = []

    def go(copy):
        copy.start()
        started.append(copy)
        return copy

    guarded = {}

    def maybe(name, condition, copy):
        pl.when(condition)(copy.start)
        guarded.setdefault(name, (condition, []))[1].append(copy)

    def hop(zz, yy, q, send, device):
        ref = tok.at[zz, yy, c, :, pl.ds(CUT_AT[q], CUTS[q])]
        return remote(ref, ref, send, got.at[zz, yy, q], tensor=device)

    def landed(zz, yy, q):
        hop(zz, yy, q, y_s.at[0, q], ypal).wait_recv()

    mid = (z == 1) | (z == 2)
    ends = (z == 0) | (z == 3)
    first = z + 1 - 2 * (z % 2)
    second = 2 - z // 2
    third = 3 - 3 * (z // 2)
    inner = jnp.where(mid, 3 - z, first)
    line = {k: zz * 4 + y * 2 + c for k, zz in (("first", first), ("inner", inner))}

    def launch(q):
        go(hop(z, y, q, z_s.at[0, q], zpal[2]))
        go(hop(z, y, q, y_s.at[0, q], ypal))
        go(hop(z, y, q, z_s.at[1, q], line["inner"]))
        maybe("mid", mid, hop(z, y, q, z_s.at[2, q], line["first"]))

    def nearby(q):
        @pl.when(mid)
        def _():
            landed(third, y, q)

        maybe("mid", mid, hop(third, y, q, z_s.at[3, q], line["first"]))
        landed(first, y, q)
        go(hop(first, y, q, y_s.at[1, q], ypal))
        landed(second, y, q)
        go(hop(second, y, q, y_s.at[2, q], ypal))

    def far(q):
        @pl.when(ends)
        def _():
            landed(third, y, q)

        go(hop(third, y, q, y_s.at[3, q], ypal))

    def across_own(q):
        landed(z, oy, q)

    def across_near(q):
        landed(first, oy, q)
        landed(second, oy, q)

    def across_far(q):
        landed(third, oy, q)
        go(share(q, c))

    def share(q, core):
        ref = tok.at[:, :, core, :, pl.ds(CUT_AT[q], CUTS[q])]
        return remote(ref, ref, sib_s.at[q], sib_r.at[q], tensor=sib)

    own.wait()
    for q in range(min(LEAD, NQ)):
        launch(q)
    bc_send = go(remote(bc_in, w_bc.at[:, c], misc_s.at[0], misc_r.at[0], tensor=sib))
    tap_send = go(remote(conv_bc, t_conv.at[c], misc_s.at[1], misc_r.at[1], tensor=sib))
    off_send = go(remote(bias_bc, t_bias.at[c], misc_s.at[5], misc_r.at[5], tensor=sib))

    def split(q, part):
        size = CUTS[q] // 4

        def run():
            if part == 0:
                zx_loads[q].wait()

            @pl.loop(0, size // 128)
            def _(j):
                at = pl.multiple_of(CUT_AT[q] + part * size + j * 128, 128)
                rows = pl.ds(at, 128)
                both = pltpu.einshape("abc->bac", zx_raw[rows])
                w_zx[rows, :CHAN] = both[0]
                w_zx[rows, CHAN:] = both[1]

        return run

    def chunk(q):
        at = slice(CUT_AT[q], CUT_AT[q] + CUTS[q])
        return tok[:, :, :, :, at].reshape(LEN, CUTS[q])

    def add_to(q, rows, cols, product):
        if q == 0:
            acc[rows, cols] = product
        else:
            acc[rows, cols] += product

    def dot_zx(q, i):
        def run():
            cols = slice(i * 256, i * 256 + 256)
            at = slice(CUT_AT[q], CUT_AT[q] + CUTS[q])
            add_to(
                q,
                slice(0, LEN),
                cols,
                jnp.dot(chunk(q), w_zx[at, cols], preferred_element_type=F32),
            )

        return run

    def dot_bc(q):
        def run():
            if q == 0:
                for load in (bc_load, tap_load, off_load, *small_loads[1:]):
                    load.wait()
                for sent in (bc_send, tap_send, off_send):
                    sent.wait_recv()
            at = slice(CUT_AT[q], CUT_AT[q] + CUTS[q])
            weights = w_bc[:, :, :, at].reshape(256, CUTS[q])
            add_to(
                q,
                slice(0, LEN),
                slice(1024, 1280),
                lax.dot_general(chunk(q), weights, NT, preferred_element_type=F32),
            )

        return run

    def dot_dt(q):
        def run():
            if q == 0:
                small_loads[0].wait()
            at = slice(CUT_AT[q], CUT_AT[q] + CUTS[q])
            add_to(
                q,
                slice(0, 8),
                slice(1280, 1280 + LEN),
                lax.dot_general(dt_in[:, at], chunk(q), NT, preferred_element_type=F32),
            )

        return run

    n_seg = lengths.shape[0]
    bounds = []
    run_sum = jnp.int32(0)
    for k in range(n_seg):
        run_sum = run_sum + lengths[k]
        bounds.append(run_sum)
    base = s * LEN

    def since(rows):
        pos = lax.broadcasted_iota(jnp.int32, (rows, 128), 0) + base
        seg_start = jnp.zeros((rows, 128), jnp.int32)
        for bound in bounds:
            seg_start = jnp.where(bound <= pos, jnp.maximum(seg_start, bound), seg_start)
        return pos - seg_start

    def ready():
        age = since(LEN)
        row = lax.broadcasted_iota(jnp.int32, (LEN, 128), 0)
        for j in range(1, 4):
            early[j - 1] = ((age >= j) & (row >= j)).astype(F32)
        ri = lax.broadcasted_iota(jnp.int32, (LEN, LEN), 0)
        ci = lax.broadcasted_iota(jnp.int32, (LEN, LEN), 1)
        same = segment_of(bounds, ci + base) == segment_of(bounds, ri + base)
        okay[...] = (same & (ri >= ci)).astype(F32)

    last = NQ - 1
    for t in range(NQ + 3):
        if t + LEAD < NQ:
            launch(t + LEAD)
        todo = []
        if t < NQ:
            todo = [split(t, part) for part in range(4)]
        if t == 0:
            todo.append(ready)
        if t >= 3:
            q = t - 3
            share(q, oc).wait_recv()
            todo += [dot_dt(q), dot_bc(q), dot_zx(q, 2), dot_zx(q, 3)]
            if q != last:
                todo += [dot_zx(q, 0), dot_zx(q, 1)]
        events = [(nearby, t), (far, t - 1), (across_own, t)]
        events += [(across_near, t - 1), (across_far, t - 2)]
        events = [(what, q) for what, q in events if 0 <= q < NQ]
        for i, (what, q) in enumerate(events):
            what(q)
            count = -(-len(todo) // (len(events) - i))
            for work in todo[:count]:
                work()
            todo = todo[count:]
        for work in todo:
            work()

    ext[16:, CHAN:] = acc[:, 1024:1280].astype(BF16)
    ext[16:, :CHAN] = acc[:, 512:1024].astype(BF16)
    halo = go(
        remote(ext.at[pl.ds(256, 16)], ext.at[pl.ds(0, 16)], misc_s.at[2], misc_r.at[2], seq=other)
    )
    head_row = lax.broadcasted_iota(jnp.int32, (8, LEN), 0)

    def by_head(ref, heads):
        values = jnp.zeros(heads.shape, F32)
        for h in range(8):
            values = jnp.where(heads == h, ref[h], values)
        return values

    rate = by_head(rate_in, head_row)
    dt_own = jax.nn.softplus(acc[:8, 1280 : 1280 + LEN] + by_head(dt_bias, head_row))
    steps[s] = dt_own
    step_send = go(remote(steps.at[s], steps.at[s], misc_s.at[3], misc_r.at[3], seq=other))
    upper = (
        lax.broadcasted_iota(jnp.int32, (LEN, LEN), 0)
        <= lax.broadcasted_iota(jnp.int32, (LEN, LEN), 1)
    ).astype(BF16)
    head_of = lax.broadcasted_iota(jnp.int32, (8, CHAN), 1) // 64
    row_of = lax.broadcasted_iota(jnp.int32, (24, CHAN), 0) % 8
    spread = (lax.broadcasted_iota(jnp.int32, (24, CHAN), 1) // 64 == row_of).astype(BF16)

    def terms(v):
        high = v.astype(BF16)
        rest = v - high.astype(F32)
        middle = rest.astype(BF16)
        return [high, middle, (rest - middle.astype(F32)).astype(BF16)]

    def cumulate(dt):
        parts = jnp.concatenate([t.astype(F32) for t in terms(-rate * dt)], axis=0).astype(BF16)
        sums = jnp.dot(parts, upper, preferred_element_type=F32)
        return sums[:8] + sums[8:16] + sums[16:]

    def widen(rows):
        parts = jnp.concatenate([t.astype(F32) for t in terms(rows)], axis=0).astype(BF16)
        return lax.dot_general(parts, spread, TN, preferred_element_type=F32)

    place = lax.broadcasted_iota(jnp.int32, (8, LEN), 1)
    seg_own = segment_of(bounds, place + base)
    seg_last = segment_of(bounds, jnp.full((8, LEN), LEN - 1, jnp.int32) + base)
    cum_r = cumulate(dt_own)
    into = jnp.exp(cum_r[:, LEN - 1 :] - cum_r) * dt_own * (seg_own == seg_last).astype(F32)
    into_wide = widen(into)

    def taps_for(i, row):
        if i < 4:
            cols = slice(i * 128, i * 128 + 128)
            return bias_x[:, cols] if row == 4 else conv_x[row : row + 1, cols]
        k = i - 4
        if row == 4:
            both = [t_bias[e, k : k + 1, :] for e in range(2)]
        else:
            both = [t_conv[e, row, k : k + 1, :] for e in range(2)]
        return jnp.concatenate(both, axis=1)

    def silu(v):
        return v * lax.logistic(v)

    ent_copy = []
    for i in (4, 0, 1, 2, 3, 5):
        cols = slice(i * 128, i * 128 + 128)
        v = ext[16:, cols].astype(F32)
        total = taps_for(i, 4) + taps_for(i, 0) * v
        for j in range(1, 4):
            total = total + taps_for(i, j) * pltpu.roll(v, j, 0) * early[j - 1]
        made = silu(total).astype(BF16)
        act[s, :, cols] = made
        if i < 4:
            x_in = (made.astype(F32) * into_wide[:, cols]).astype(BF16)
            ent_out[i] = lax.dot_general(
                act[s, :, CHAN : CHAN + STATES], x_in, TN, preferred_element_type=F32
            ).astype(BF16)
            ent_copy.append(
                go(remote(ent_out.at[i], ent_in.at[i], ent_s.at[i], ent_r.at[i], seq=other))
            )
    halo.wait_recv()

    @pl.when(s > 0)
    def _():
        age = since(16)
        for i in range(6):
            cols = slice(i * 128, i * 128 + 128)
            v = ext[:32, cols].astype(F32)
            total = taps_for(i, 4) + taps_for(i, 0) * v[16:]
            for j in range(1, 4):
                total = total + taps_for(i, j) * pltpu.roll(v, j, 0)[16:] * (age >= j).astype(F32)
            act[s, :16, cols] = silu(total).astype(BF16)

    seen = act.at[s, :, pl.ds(0, CHAN + STATES)]
    act_send = go(remote(seen, seen, misc_s.at[4], misc_r.at[4], seq=other))

    for i in range(2):
        cols = slice(i * 256, i * 256 + 256)
        at = slice(CUT_AT[last], CUT_AT[last] + CUTS[last])
        gate[:, cols] = (
            acc[:, cols] + jnp.dot(chunk(last), w_zx[at, cols], preferred_element_type=F32)
        ).astype(BF16)

    cum_c = cum_r.T
    b_own = act[s, :, CHAN : CHAN + STATES]
    c_own = act[s, :, CHAN + STATES :]
    lane = lax.broadcasted_iota(jnp.int32, (128, 128), 1)
    for r in range(2):
        rows = slice(r * 128, r * 128 + 128)
        past = slice(0, r * 128 + 128)
        scores = lax.dot_general(c_own[rows], b_own[past], NT, preferred_element_type=F32)
        scores = scores * okay[rows, past]
        for g in range(4):
            cols = slice(g * 128, g * 128 + 128)
            halves = []
            for h in (2 * g, 2 * g + 1):
                gap = jnp.minimum(cum_c[rows, h : h + 1] - cum_r[h : h + 1, past], 0.0)
                mix = jnp.exp(gap) * scores * dt_own[h : h + 1, past]
                halves.append(
                    jnp.dot(mix.astype(BF16), act[s, past, cols], preferred_element_type=F32)
                )
            acc[rows, cols] = jnp.where(lane < 64, halves[0], halves[1])

    seg_before = segment_of(bounds, jnp.full((8, LEN), LEN - 1, jnp.int32))
    carried = ((seg_own == seg_before) & (s > 0)).astype(F32)
    gain = widen(jnp.exp(cum_r) * carried)
    skips = by_head(skip_in, head_of[:1])
    for i in range(4):
        cols = slice(i * 128, i * 128 + 128)
        ent_copy[i].wait_recv()
        y_all = acc[:, cols] + jnp.dot(c_own, ent_in[i], preferred_element_type=F32) * gain[:, cols]
        y_all = y_all + skips[:, cols] * act[s, :, cols].astype(F32)
        gate[:, cols] = (y_all * silu(gate[:, cols].astype(F32))).astype(BF16)
    out_load.wait()

    def part(zz, yy, cc):
        return pl.ds(pl.multiple_of(zz * 64 + yy * 32 + cc * 16, 16), 16)

    a_copy = []
    b_copy = []
    c_copy = []

    def slab(q):
        return slice(SLAB_AT[q], SLAB_AT[q] + SLABS[q]), pl.ds(SLAB_AT[q], SLABS[q])

    def to_sib(q):
        cols, at = slab(q)
        acc[:, cols] = jnp.dot(gate[...], w_out[:, cols], preferred_element_type=F32)
        for zz in range(4):
            for yy in range(2):
                send_a[zz, yy, :, cols] = acc[part(zz, yy, oc), cols].astype(BF16)
        src, dst = send_a.at[:, :, :, at], recv_a.at[:, :, :, at]
        a_copy.append(go(remote(src, dst, rsa_s.at[q], rsa_r.at[q], tensor=sib)))

    d_copy = {}
    cols_0 = slice(0, SLABS[0])

    def line_first():
        def summed(zz, yy):
            return acc[part(zz, yy, c), cols_0] + recv_a[zz, yy, :, cols_0].astype(F32)

        for d in (2, 1, 3):
            for yy in range(2):
                send_d[d, yy] = summed((z + d) % 4, yy).astype(BF16)
            d_copy[d] = go(
                remote(send_d.at[d], recv_d.at[d], rsd_s.at[d], rsd_r.at[d], tensor=zpal[d])
            )
        for yy in range(2):
            keep[yy, :, cols_0] = summed(z, yy)
        b_copy.append(None)

    def turn():
        for d in (2, 1, 3):
            d_copy[d].wait_recv()

        def summed(yy):
            total = keep[yy, :, cols_0]
            for d in (2, 1, 3):
                total = total + recv_d[d, yy].astype(F32)
            return total

        send_e[...] = summed(oy).astype(BF16)
        d_copy[0] = go(remote(send_e, recv_e, rsd_s.at[0], rsd_r.at[0], tensor=ypal))
        keep[2, :, cols_0] = summed(y)

    def to_pal(q):
        cols, at = slab(q)
        a_copy[q].wait_recv()
        if q == 0:
            return line_first()
        for zz in range(4):
            send_b[zz, :, cols] = (
                acc[part(zz, oy, c), cols] + recv_a[zz, oy, :, cols].astype(F32)
            ).astype(BF16)
        src, dst = send_b.at[:, :, at], recv_b.at[:, :, at]
        b_copy.append(go(remote(src, dst, rsb_s.at[q], rsb_r.at[q], tensor=ypal)))
        for zz in range(4):
            keep[zz, :, cols] = acc[part(zz, y, c), cols] + recv_a[zz, y, :, cols].astype(F32)

    def to_line(q):
        cols, at = slab(q)
        b_copy[q].wait_recv()
        for d in (2, 1, 3):
            zz = (z + d) % 4
            send_c[d, :, cols] = (keep[zz, :, cols] + recv_b[zz, :, cols].astype(F32)).astype(BF16)
            src, dst = send_c.at[d, :, at], recv_c.at[d, :, at]
            c_copy.append(
                go(remote(src, dst, rsc_s.at[d, q], rsc_r.at[d, q], tensor=zpal[d]))
            )

    def finals_ready():
        step_send.wait_recv()
        act_send.wait_recv()
        cum_0 = cumulate(steps[0])
        cum_1 = cumulate(steps[1]) + cum_0[:, LEN - 1 :]
        seg_0 = segment_of(bounds, place)
        seg_1 = segment_of(bounds, place + LEN)
        ends_0 = jnp.zeros((8, LEN), F32)
        ends_1 = jnp.zeros((8, LEN), F32)
        for k in range(n_seg):
            spot_0 = (place == bounds[k] - 1).astype(F32) * cum_0
            spot_1 = (place + LEN == bounds[k] - 1).astype(F32) * cum_1
            end = jnp.sum(spot_0 + spot_1, axis=1, keepdims=True)
            ends_0 = jnp.where(seg_0 == k, end, ends_0)
            ends_1 = jnp.where(seg_1 == k, end, ends_1)
        w_0 = widen(jnp.exp(ends_0 - cum_0) * steps[0])
        w_1 = widen(jnp.exp(ends_1 - cum_1) * steps[1])
        xw_0 = (act[0, :, :CHAN].astype(F32) * w_0).astype(BF16)
        xw_1 = (act[1, :, :CHAN].astype(F32) * w_1).astype(BF16)
        b_0 = act[0, :, CHAN : CHAN + STATES]
        b_1 = act[1, :, CHAN : CHAN + STATES]
        spot = lax.broadcasted_iota(jnp.int32, (LEN, STATES), 0)
        col_0 = segment_of(bounds, spot)
        col_1 = segment_of(bounds, spot + LEN)

        def fill(k):
            m_0 = jnp.where(col_0 == k, b_0.astype(F32), 0.0).astype(BF16)
            m_1 = jnp.where(col_1 == k, b_1.astype(F32), 0.0).astype(BF16)
            finals[k] = lax.dot_general(
                xw_0, m_0, TN, preferred_element_type=F32
            ) + lax.dot_general(xw_1, m_1, TN, preferred_element_type=F32)

        return fill

    fill = None
    filled = 0
    for t in range(NR + BEHIND):
        if t < NR:
            to_sib(t)
        if 0 <= t - 1 < NR:
            to_pal(t - 1)
        if t > BEHIND:
            to_line(t - BEHIND)
        if t == BEHIND + 3:
            turn()
        if t == NR:
            fill = finals_ready()
        elif t > NR:
            for k in range(filled, min(n_seg, filled + 2)):
                fill(k)
            filled = min(n_seg, filled + 2)
    for condition, copies in guarded.values():

        @pl.when(condition)
        def _():
            for copy in copies:
                copy.wait_send()

    d_copy[0].wait_recv()
    mixed[:, cols_0] = (keep[2, :, cols_0] + recv_e[...].astype(F32)).astype(BF16)
    for q in range(1, NR):
        cols, _ = slab(q)
        total = keep[z, :, cols] + recv_b[z, :, cols].astype(F32)
        for i, d in enumerate((2, 1, 3)):
            c_copy[(q - 1) * 3 + i].wait_recv()
            total = total + recv_c[d, :, cols].astype(F32)
        mixed[:, cols] = total.astype(BF16)
    for copy in started:
        copy.wait_send()


def settle_kernel(mixed_in, finals_in, mixed, finals, sems):
    copies = [
        pltpu.make_async_copy(finals_in, finals, sems.at[0]),
        pltpu.make_async_copy(mixed_in, mixed, sems.at[1]),
    ]
    for copy in copies:
        copy.start()
    for copy in copies:
        copy.wait()


def fused_body(
    tokens,
    lengths,
    proj_zx,
    proj_bc,
    proj_dt,
    conv_x,
    conv_bc,
    bias_x,
    bias_bc,
    dt_bias,
    decay_rate,
    skip_gain,
    proj_out,
):
    n_seg = lengths.shape[0]
    bc_view = proj_bc.transpose(1, 2, 0)
    dt_view = proj_dt.T
    any_spec = pl.BlockSpec(memory_space=pl.ANY)
    vmem = pl.BlockSpec(memory_space=pltpu.VMEM)
    smem = pl.BlockSpec(memory_space=pltpu.SMEM)
    dma = pltpu.SemaphoreType.DMA
    out_shape = (
        jax.ShapeDtypeStruct((ROWS, WIDE), BF16),
        jax.ShapeDtypeStruct((n_seg, CHAN, STATES), F32),
    )
    mixed, finals = pl.pallas_call(
        layer_kernel,
        out_shape=tuple(pltpu.VMEM(o.shape, o.dtype) for o in out_shape),
        in_specs=[smem, any_spec, any_spec, any_spec, any_spec, any_spec, any_spec]
        + [any_spec, any_spec, smem, smem, smem, any_spec],
        out_specs=(vmem, vmem),
        scratch_shapes=[
            pltpu.VMEM((4, 2, 2, ROWS, WIDE), BF16),
            pltpu.VMEM((WIDE, 2, CHAN), BF16),
            pltpu.VMEM((WIDE, 2 * CHAN), BF16),
            pltpu.VMEM((2, 2, 64, WIDE), BF16),
            pltpu.VMEM((CHAN, WIDE), BF16),
            pltpu.VMEM((2, 4, 2, 64), F32),
            pltpu.VMEM((2, 2, 64), F32),
            pltpu.VMEM((LEN, CHAN), BF16),
            pltpu.VMEM((16 + LEN, CHAN + 256), BF16),
            pltpu.VMEM((2, LEN, CHAN + 256), BF16),
            pltpu.VMEM((2, 8, LEN), F32),
            pltpu.VMEM((8, WIDE), BF16),
            pltpu.VMEM((4, CHAN), F32),
            pltpu.VMEM((1, CHAN), F32),
            pltpu.VMEM((3, LEN, 128), F32),
            pltpu.VMEM((LEN, LEN), F32),
            pltpu.VMEM((LEN, WIDE), F32),
            pltpu.VMEM((4, STATES, 128), BF16),
            pltpu.VMEM((4, STATES, 128), BF16),
            pltpu.VMEM((4, ROWS, WIDE), F32),
            pltpu.VMEM((4, 2, ROWS, WIDE), BF16),
            pltpu.VMEM((4, 2, ROWS, WIDE), BF16),
            pltpu.VMEM((4, ROWS, WIDE), BF16),
            pltpu.VMEM((4, ROWS, WIDE), BF16),
            pltpu.VMEM((4, ROWS, WIDE), BF16),
            pltpu.VMEM((4, ROWS, WIDE), BF16),
            pltpu.VMEM((4, 2, ROWS, SLABS[0]), BF16),
            pltpu.VMEM((4, 2, ROWS, SLABS[0]), BF16),
            pltpu.VMEM((ROWS, SLABS[0]), BF16),
            pltpu.VMEM((ROWS, SLABS[0]), BF16),
        ]
        + [dma((8,)), dma((NQ,)), dma((4, NQ)), dma((4, NQ))]
        + [dma((4, 2, NQ)), dma((NQ,)), dma((NQ,)), dma((6,)), dma((6,)), dma((4,)), dma((4,))]
        + [dma((NR,)), dma((NR,)), dma((NR,)), dma((NR,)), dma((4, NR)), dma((4, NR)), dma((4,)), dma((4,))],
        compiler_params=pltpu.CompilerParams(
            collective_id=0, has_side_effects=True, vmem_limit_bytes=56 << 20
        ),
    )(
        lengths,
        tokens,
        proj_zx,
        bc_view,
        dt_view,
        conv_x,
        bias_x.reshape(1, CHAN),
        conv_bc,
        bias_bc,
        dt_bias,
        decay_rate,
        skip_gain,
        proj_out,
    )
    mixed, finals = pl.pallas_call(
        settle_kernel,
        out_shape=out_shape,
        in_specs=[vmem, vmem],
        out_specs=(any_spec, any_spec),
        scratch_shapes=[dma((2,))],
    )(*(pltpu.with_memory_space_constraint(o, pltpu.VMEM) for o in (mixed, finals)))
    return (mixed, finals.reshape(n_seg, 8, 64, STATES))


def solution(mesh):
    in_specs = (
        P(("seq", "tensor"), None),
        P(),
        P(None, None, "tensor"),
        P(None, None, "tensor"),
        P(None, "tensor"),
        P(None, "tensor"),
        P(None, None, "tensor"),
        P("tensor"),
        P(None, "tensor"),
        P("tensor"),
        P("tensor"),
        P("tensor"),
        P("tensor", None),
    )
    out_specs = (P(("seq", "tensor"), None), P(None, "tensor", None, None))
    small = mesh.shape["seq"] == 2 and mesh.shape["tensor"] == 16
    chosen = fused_body if small else body
    return jax.shard_map(chosen, mesh=mesh, in_specs=in_specs, out_specs=out_specs, check_vma=False)
```

```python
import jax
import jax.numpy as jnp
from jax import lax
from jax.experimental import pallas as pl
from jax.experimental.pallas import tpu as pltpu
from jax.sharding import PartitionSpec as P

GROUPS = 8


def partner_2(value, axis, bit):
    mask = 2**bit
    pairs = [(source, source ^ mask) for source in range(lax.axis_size(axis))]
    return lax.ppermute(value, axis, pairs)


def passed_along(block, axis, distance):
    devices = range(lax.axis_size(axis))
    route = [(i - distance, i) for i in devices if i - distance in devices]
    return lax.ppermute(block, axis, route)


def group_columns(bc_own, tensor_index, steps_count):
    collected = bc_own
    for bit_number in range(steps_count):
        partner = partner_2(collected, "tensor", bit_number)
        upper = tensor_index // 2**bit_number % 2
        low_first = jnp.concatenate([collected, partner], axis=2)
        high_first = jnp.concatenate([partner, collected], axis=2)
        collected = jnp.where(upper == 0, low_first, high_first)
    return collected


def body(
    tokens,
    lengths,
    proj_zx,
    proj_bc,
    proj_dt,
    conv_x,
    conv_bc,
    bias_x,
    bias_bc,
    dt_bias,
    decay_rate,
    skip_gain,
    proj_out,
):
    highest = lax.Precision.HIGHEST
    tensor_size = lax.axis_size("tensor")
    rows_dev = tokens.shape[0]
    shard_len = rows_dev * tensor_size
    seq_index = lax.axis_index("seq")
    tensor_index = lax.axis_index("tensor")
    heads_dev = decay_rate.shape[0]
    width_zx = proj_zx.shape[2]
    head_size = width_zx // heads_dev
    cols_bc = proj_bc.shape[2]
    taps_count = conv_x.shape[0]
    model_width = tokens.shape[1]
    zx_flat = proj_zx.reshape(model_width, 2 * width_zx)
    bc_flat = proj_bc.reshape(model_width, 2 * cols_bc)
    piece = lax.all_gather(tokens, "tensor", axis=0, tiled=True)
    projected = jnp.concatenate(
        [
            jnp.dot(piece, zx_flat, preferred_element_type=jnp.float32),
            jnp.dot(piece, bc_flat, preferred_element_type=jnp.float32),
            jnp.dot(piece, proj_dt, preferred_element_type=jnp.float32),
        ],
        axis=1,
    )
    gate_in = projected[:, :width_zx].astype(jnp.bfloat16)
    conv_in = projected[:, width_zx : 2 * width_zx + 2 * cols_bc].astype(jnp.bfloat16)
    step_size = jax.nn.softplus(projected[:, 2 * width_zx + 2 * cols_bc :] + dt_bias[None, :])
    row_ids = jnp.arange(shard_len, dtype=jnp.int32)
    positions = seq_index * shard_len + row_ids
    later = jnp.arange(lengths.shape[0])
    bounds = jnp.sum(jnp.where(later[None, :] <= later[:, None], lengths[None, :], 0), axis=1)
    reached = bounds[None, :] <= positions[:, None]
    segment = jnp.sum(reached.astype(jnp.int32), axis=1)
    seg_start = jnp.max(jnp.where(reached, bounds[None, :], 0), axis=1)
    edge_rows = conv_in[shard_len - (taps_count - 1) :]
    before = passed_along(edge_rows, "seq", 1)
    extended = jnp.concatenate([before, conv_in], axis=0)
    conv_taps = jnp.concatenate([conv_x, conv_bc.reshape(taps_count, 2 * cols_bc)], axis=1)
    conv_offset = jnp.concatenate([bias_x, bias_bc.reshape(2 * cols_bc)])
    convolved = jnp.zeros((shard_len, conv_taps.shape[1]), jnp.float32) + conv_offset[None, :]
    for lag_index in range(taps_count):
        lagged = extended[
            taps_count - 1 - lag_index : taps_count - 1 - lag_index + shard_len
        ].astype(jnp.float32)
        keep_mask = (positions - lag_index >= seg_start).astype(jnp.float32)
        convolved = convolved + conv_taps[lag_index][None, :] * lagged * keep_mask[:, None]
    activated = jax.nn.silu(convolved).astype(jnp.bfloat16)
    x_conv = activated[:, :width_zx]
    bc_own = activated[:, width_zx:].reshape(shard_len, 2, cols_bc)
    per_group = tensor_size // GROUPS
    steps_count = per_group.bit_length() - 1
    bc_group = group_columns(bc_own, tensor_index, steps_count).astype(jnp.float32)
    state_in_proj = bc_group[:, 0]
    state_out_proj = bc_group[:, 1]
    x_float = x_conv.astype(jnp.float32).reshape(shard_len, heads_dev, head_size)
    log_decay = -decay_rate[None, :] * step_size
    lower = (row_ids[:, None] >= row_ids[None, :]).astype(jnp.float32)
    cumulative = jnp.dot(lower, log_decay, precision=highest)
    cumulative_t = cumulative.T
    valid = (segment[:, None] == segment[None, :]) & (row_ids[:, None] >= row_ids[None, :])
    spread = cumulative_t[:, :, None] - cumulative_t[:, None, :]
    decay_matrix = jnp.where(valid[None], jnp.exp(jnp.where(valid[None], spread, 0.0)), 0.0)
    scores = jnp.dot(state_out_proj, state_in_proj.T, precision=highest)
    mixing = decay_matrix * scores[None] * step_size.T[:, None, :]
    y_local = jnp.einsum("hts,shp->thp", mixing, x_float, precision=highest)
    before_pos = seq_index * shard_len - 1
    seg_before = jnp.sum((bounds <= before_pos).astype(jnp.int32))
    carried = (segment == seg_before).astype(jnp.float32)
    entry_gain = jnp.exp(cumulative) * carried[:, None]
    n_seg = lengths.shape[0]
    end_rows = bounds - 1 - seq_index * shard_len
    inside = (end_rows >= 0) & (end_rows < shard_len)
    target_rows = jnp.concatenate([end_rows, jnp.full((1,), shard_len - 1, jnp.int32)])
    target_seg = jnp.concatenate([jnp.arange(n_seg, dtype=jnp.int32), segment[shard_len - 1 :]])
    target_ok = jnp.concatenate([inside, jnp.ones((1,), bool)])
    picker = (row_ids[None, :] == target_rows[:, None]).astype(jnp.float32)
    cum_end = jnp.dot(picker, cumulative, precision=highest)
    reach = (
        target_ok[:, None]
        & (row_ids[None, :] <= target_rows[:, None])
        & (segment[None, :] == target_seg[:, None])
    )
    gap_end = cum_end[:, :, None] - cumulative_t[None, :, :]
    end_weight = (
        jnp.where(reach[:, None, :], jnp.exp(jnp.where(reach[:, None, :], gap_end, 0.0)), 0.0)
        * step_size.T[None]
    )
    states = jnp.einsum("khs,shp,sn->khpn", end_weight, x_float, state_in_proj, precision=highest)
    end_local = states[:n_seg]
    shard_state = states[n_seg]
    end_gain = jnp.where((target_ok & (target_seg == seg_before))[:, None], jnp.exp(cum_end), 0.0)
    shard_gain = end_gain[n_seg]
    end_gain_seg = end_gain[:n_seg]
    gathered = (
        lax.all_gather(shard_gain[None], "seq", axis=0, tiled=True),
        lax.all_gather(shard_state[None], "seq", axis=0, tiled=True),
        lax.all_gather(end_gain_seg[None], "seq", axis=0, tiled=True),
        lax.all_gather(end_local[None], "seq", axis=0, tiled=True),
    )
    gains_all, states_all, egains_all, elocal_all = gathered

    def fold_step(carry, item):
        gain_now, state_now = item
        return (gain_now[:, None, None] * carry + state_now, carry)

    last_state, incoming = lax.scan(
        fold_step, jnp.zeros(shard_state.shape, jnp.float32), (gains_all, states_all)
    )
    state_entry = lax.dynamic_index_in_dim(incoming, seq_index, 0, keepdims=False)
    final_states = jnp.sum(elocal_all + egains_all[:, :, :, None, None] * incoming[:, None], axis=0)
    y_entry = (
        jnp.einsum("tn,hpn->thp", state_out_proj, state_entry, precision=highest)
        * entry_gain[:, :, None]
    )
    y_total = y_local + y_entry + skip_gain[None, :, None] * x_float
    gate_values = jax.nn.silu(gate_in.astype(jnp.float32)).reshape(shard_len, heads_dev, head_size)
    gated = (y_total * gate_values).reshape(shard_len, width_zx).astype(jnp.bfloat16)
    mixed = lax.psum_scatter(
        jnp.dot(gated, proj_out, preferred_element_type=jnp.float32),
        "tensor",
        scatter_dimension=0,
        tiled=True,
    )
    return (mixed.astype(jnp.bfloat16), final_states)


F32 = jnp.float32
BF16 = jnp.bfloat16
ROWS = 16
LEN = 256
WIDE = 4096
CHAN = 512
STATES = 128
HIGH = lax.Precision.HIGHEST
NT = (((1,), (1,)), ((), ()))
TN = (((0,), (0,)), ((), ()))
CUTS = (1536, 1536, 1024)
ROUND = (1,)
LEAD = 2
SLABS = (768, 256, 512, 512, 512, 512, 512, 512)
BEHIND = 5


def starts(widths):
    return tuple(sum(widths[:i]) for i in range(len(widths)))


CUT_AT = starts(CUTS)
SLAB_AT = starts(SLABS)
NQ = len(CUTS)
NR = len(SLABS)


def remote(src, dst, send, recv, **device):
    return pltpu.make_async_remote_copy(
        src_ref=src,
        dst_ref=dst,
        send_sem=send,
        recv_sem=recv,
        device_id=device,
        device_id_type=pl.DeviceIdType.MESH,
    )


def segment_of(bounds, pos):
    total = jnp.zeros(pos.shape, jnp.int32)
    for bound in bounds:
        total = total + (bound <= pos).astype(jnp.int32)
    return total


def layer_kernel(
    lengths,
    tok_in,
    zx_in,
    bc_in,
    dt_from,
    conv_from,
    bias_from,
    conv_bc,
    bias_bc,
    dt_bias,
    rate_in,
    skip_in,
    out_in,
    mixed,
    finals,
    tok,
    zx_raw,
    w_zx,
    w_bc,
    w_out,
    t_conv,
    t_bias,
    gate,
    ext,
    act,
    steps,
    dt_in,
    conv_x,
    bias_x,
    early,
    okay,
    acc,
    ent_out,
    ent_in,
    keep,
    send_a,
    recv_a,
    send_b,
    recv_b,
    send_c,
    recv_c,
    send_d,
    recv_d,
    send_e,
    recv_e,
    load_sem,
    zx_sem,
    z_s,
    y_s,
    got,
    sib_s,
    sib_r,
    misc_s,
    misc_r,
    ent_s,
    ent_r,
    rsa_s,
    rsa_r,
    rsb_s,
    rsb_r,
    rsc_s,
    rsc_r,
    rsd_s,
    rsd_r,
):
    s = lax.axis_index("seq")
    me = lax.axis_index("tensor")
    z = me // 4
    y = (me // 2) % 2
    c = me % 2
    oy = 1 - y
    oc = 1 - c
    sib = z * 4 + y * 2 + oc
    ypal = z * 4 + oy * 2 + c
    zpal = [((z + d) % 4) * 4 + y * 2 + c for d in range(4)]
    other = 1 - s

    ext[:16] = jnp.zeros((16, CHAN + 256), BF16)
    barrier = pltpu.get_barrier_semaphore()
    for pal in [sib, ypal] + zpal[1:]:
        pl.semaphore_signal(
            barrier, inc=1, device_id={"tensor": pal}, device_id_type=pl.DeviceIdType.MESH
        )
    pl.semaphore_signal(
        barrier, inc=1, device_id={"seq": other}, device_id_type=pl.DeviceIdType.MESH
    )

    own = pltpu.make_async_copy(tok_in, tok.at[z, y, c], load_sem.at[0])
    own.start()
    zx_loads = []
    for q in range(NQ):
        rows = pl.ds(CUT_AT[q], CUTS[q])
        load = pltpu.make_async_copy(zx_in.at[rows], zx_raw.at[rows], zx_sem.at[q])
        load.start()
        zx_loads.append(load)
    bc_load = pltpu.make_async_copy(bc_in, w_bc.at[:, c], load_sem.at[1])
    bc_load.start()
    tap_load = pltpu.make_async_copy(conv_bc, t_conv.at[c], load_sem.at[2])
    tap_load.start()
    off_load = pltpu.make_async_copy(bias_bc, t_bias.at[c], load_sem.at[5])
    off_load.start()
    small_loads = [
        pltpu.make_async_copy(src, dst, load_sem.at[i])
        for i, src, dst in ((4, dt_from, dt_in), (6, conv_from, conv_x), (7, bias_from, bias_x))
    ]
    for load in small_loads:
        load.start()
    out_load = pltpu.make_async_copy(out_in, w_out, load_sem.at[3])
    out_load.start()
    pl.semaphore_wait(barrier, 6)

    started = []

    def go(copy):
        copy.start()
        started.append(copy)
        return copy

    guarded = {}

    def maybe(name, condition, copy):
        pl.when(condition)(copy.start)
        guarded.setdefault(name, (condition, []))[1].append(copy)

    def hop(zz, yy, q, send, device):
        ref = tok.at[zz, yy, c, :, pl.ds(CUT_AT[q], CUTS[q])]
        return remote(ref, ref, send, got.at[zz, yy, q], tensor=device)

    def landed(zz, yy, q):
        hop(zz, yy, q, y_s.at[0, q], ypal).wait_recv()

    mid = (z == 1) | (z == 2)
    ends = (z == 0) | (z == 3)
    first = z + 1 - 2 * (z % 2)
    second = 2 - z // 2
    third = 3 - 3 * (z // 2)
    inner = jnp.where(mid, 3 - z, first)
    line = {k: zz * 4 + y * 2 + c for k, zz in (("first", first), ("inner", inner))}

    def launch(q):
        go(hop(z, y, q, z_s.at[0, q], zpal[2]))
        go(hop(z, y, q, y_s.at[0, q], ypal))
        go(hop(z, y, q, z_s.at[1, q], line["inner"]))
        maybe("mid", mid, hop(z, y, q, z_s.at[2, q], line["first"]))

    def nearby(q):
        @pl.when(mid)
        def _():
            landed(third, y, q)

        maybe("mid", mid, hop(third, y, q, z_s.at[3, q], line["first"]))
        landed(first, y, q)
        if q not in ROUND:
            go(hop(first, y, q, y_s.at[1, q], ypal))
        landed(second, y, q)
        go(hop(second, y, q, y_s.at[2, q], ypal))

    def far(q):
        @pl.when(ends)
        def _():
            landed(third, y, q)

        go(hop(third, y, q, y_s.at[3, q], ypal))

    def across_own(q):
        landed(z, oy, q)
        if q in ROUND:
            go(hop(z, oy, q, y_s.at[1, q], line["first"]))

    def across_near(q):
        landed(first, oy, q)
        landed(second, oy, q)

    def across_far(q):
        landed(third, oy, q)
        go(share(q, c))

    def share(q, core):
        ref = tok.at[:, :, core, :, pl.ds(CUT_AT[q], CUTS[q])]
        return remote(ref, ref, sib_s.at[q], sib_r.at[q], tensor=sib)

    own.wait()
    for q in range(min(LEAD, NQ)):
        launch(q)
    bc_send = go(remote(bc_in, w_bc.at[:, c], misc_s.at[0], misc_r.at[0], tensor=sib))
    tap_send = go(remote(conv_bc, t_conv.at[c], misc_s.at[1], misc_r.at[1], tensor=sib))
    off_send = go(remote(bias_bc, t_bias.at[c], misc_s.at[5], misc_r.at[5], tensor=sib))

    def split(q, part):
        size = CUTS[q] // 4

        def run():
            if part == 0:
                zx_loads[q].wait()

            @pl.loop(0, size // 128)
            def _(j):
                at = pl.multiple_of(CUT_AT[q] + part * size + j * 128, 128)
                rows = pl.ds(at, 128)
                both = pltpu.einshape("abc->bac", zx_raw[rows])
                w_zx[rows, :CHAN] = both[0]
                w_zx[rows, CHAN:] = both[1]

        return run

    def chunk(q):
        at = slice(CUT_AT[q], CUT_AT[q] + CUTS[q])
        return tok[:, :, :, :, at].reshape(LEN, CUTS[q])

    def add_to(q, rows, cols, product):
        if q == 0:
            acc[rows, cols] = product
        else:
            acc[rows, cols] += product

    def dot_zx(q, i):
        def run():
            cols = slice(i * 256, i * 256 + 256)
            at = slice(CUT_AT[q], CUT_AT[q] + CUTS[q])
            add_to(
                q,
                slice(0, LEN),
                cols,
                jnp.dot(chunk(q), w_zx[at, cols], preferred_element_type=F32),
            )

        return run

    def dot_bc(q):
        def run():
            if q == 0:
                for load in (bc_load, tap_load, off_load, *small_loads[1:]):
                    load.wait()
                for sent in (bc_send, tap_send, off_send):
                    sent.wait_recv()
            at = slice(CUT_AT[q], CUT_AT[q] + CUTS[q])
            weights = w_bc[:, :, :, at].reshape(256, CUTS[q])
            add_to(
                q,
                slice(0, LEN),
                slice(1024, 1280),
                lax.dot_general(chunk(q), weights, NT, preferred_element_type=F32),
            )

        return run

    def dot_dt(q):
        def run():
            if q == 0:
                small_loads[0].wait()
            at = slice(CUT_AT[q], CUT_AT[q] + CUTS[q])
            add_to(
                q,
                slice(0, 8),
                slice(1280, 1280 + LEN),
                lax.dot_general(dt_in[:, at], chunk(q), NT, preferred_element_type=F32),
            )

        return run

    n_seg = lengths.shape[0]
    bounds = []
    run_sum = jnp.int32(0)
    for k in range(n_seg):
        run_sum = run_sum + lengths[k]
        bounds.append(run_sum)
    base = s * LEN

    def since(rows):
        pos = lax.broadcasted_iota(jnp.int32, (rows, 128), 0) + base
        seg_start = jnp.zeros((rows, 128), jnp.int32)
        for bound in bounds:
            seg_start = jnp.where(bound <= pos, jnp.maximum(seg_start, bound), seg_start)
        return pos - seg_start

    def ready():
        age = since(LEN)
        row = lax.broadcasted_iota(jnp.int32, (LEN, 128), 0)
        for j in range(1, 4):
            early[j - 1] = ((age >= j) & (row >= j)).astype(F32)
        ri = lax.broadcasted_iota(jnp.int32, (LEN, LEN), 0)
        ci = lax.broadcasted_iota(jnp.int32, (LEN, LEN), 1)
        same = segment_of(bounds, ci + base) == segment_of(bounds, ri + base)
        okay[...] = (same & (ri >= ci)).astype(F32)

    last = NQ - 1
    for t in range(NQ + 3):
        if t + LEAD < NQ:
            launch(t + LEAD)
        todo = []
        if t < NQ:
            todo = [split(t, part) for part in range(4)]
        if t == 0:
            todo.append(ready)
        if t >= 3:
            q = t - 3
            share(q, oc).wait_recv()
            todo += [dot_dt(q), dot_bc(q), dot_zx(q, 2), dot_zx(q, 3)]
            if q != last:
                todo += [dot_zx(q, 0), dot_zx(q, 1)]
        events = [(nearby, t), (far, t - 1), (across_own, t)]
        events += [(across_near, t - 1), (across_far, t - 2)]
        events = [(what, q) for what, q in events if 0 <= q < NQ]
        for i, (what, q) in enumerate(events):
            what(q)
            count = -(-len(todo) // (len(events) - i))
            for work in todo[:count]:
                work()
            todo = todo[count:]
        for work in todo:
            work()

    ext[16:, CHAN:] = acc[:, 1024:1280].astype(BF16)
    ext[16:, :CHAN] = acc[:, 512:1024].astype(BF16)
    halo = go(
        remote(ext.at[pl.ds(256, 16)], ext.at[pl.ds(0, 16)], misc_s.at[2], misc_r.at[2], seq=other)
    )
    head_row = lax.broadcasted_iota(jnp.int32, (8, LEN), 0)

    def by_head(ref, heads):
        values = jnp.zeros(heads.shape, F32)
        for h in range(8):
            values = jnp.where(heads == h, ref[h], values)
        return values

    rate = by_head(rate_in, head_row)
    dt_own = jax.nn.softplus(acc[:8, 1280 : 1280 + LEN] + by_head(dt_bias, head_row))
    steps[s] = dt_own
    step_send = go(remote(steps.at[s], steps.at[s], misc_s.at[3], misc_r.at[3], seq=other))
    upper = (
        lax.broadcasted_iota(jnp.int32, (LEN, LEN), 0)
        <= lax.broadcasted_iota(jnp.int32, (LEN, LEN), 1)
    ).astype(BF16)
    head_of = lax.broadcasted_iota(jnp.int32, (8, CHAN), 1) // 64
    row_of = lax.broadcasted_iota(jnp.int32, (24, CHAN), 0) % 8
    spread = (lax.broadcasted_iota(jnp.int32, (24, CHAN), 1) // 64 == row_of).astype(BF16)

    def terms(v):
        high = v.astype(BF16)
        rest = v - high.astype(F32)
        middle = rest.astype(BF16)
        return [high, middle, (rest - middle.astype(F32)).astype(BF16)]

    def cumulate(dt):
        parts = jnp.concatenate([t.astype(F32) for t in terms(-rate * dt)], axis=0).astype(BF16)
        sums = jnp.dot(parts, upper, preferred_element_type=F32)
        return sums[:8] + sums[8:16] + sums[16:]

    def widen(rows):
        parts = jnp.concatenate([t.astype(F32) for t in terms(rows)], axis=0).astype(BF16)
        return lax.dot_general(parts, spread, TN, preferred_element_type=F32)

    place = lax.broadcasted_iota(jnp.int32, (8, LEN), 1)
    seg_own = segment_of(bounds, place + base)
    seg_last = segment_of(bounds, jnp.full((8, LEN), LEN - 1, jnp.int32) + base)
    cum_r = cumulate(dt_own)
    into = jnp.exp(cum_r[:, LEN - 1 :] - cum_r) * dt_own * (seg_own == seg_last).astype(F32)
    into_wide = widen(into)

    def taps_for(i, row):
        if i < 4:
            cols = slice(i * 128, i * 128 + 128)
            return bias_x[:, cols] if row == 4 else conv_x[row : row + 1, cols]
        k = i - 4
        if row == 4:
            both = [t_bias[e, k : k + 1, :] for e in range(2)]
        else:
            both = [t_conv[e, row, k : k + 1, :] for e in range(2)]
        return jnp.concatenate(both, axis=1)

    def silu(v):
        return v * lax.logistic(v)

    ent_copy = []
    for i in (4, 0, 1, 2, 3, 5):
        cols = slice(i * 128, i * 128 + 128)
        v = ext[16:, cols].astype(F32)
        total = taps_for(i, 4) + taps_for(i, 0) * v
        for j in range(1, 4):
            total = total + taps_for(i, j) * pltpu.roll(v, j, 0) * early[j - 1]
        made = silu(total).astype(BF16)
        act[s, :, cols] = made
        if i < 4:
            x_in = (made.astype(F32) * into_wide[:, cols]).astype(BF16)
            ent_out[i] = lax.dot_general(
                act[s, :, CHAN : CHAN + STATES], x_in, TN, preferred_element_type=F32
            ).astype(BF16)
            ent_copy.append(
                go(remote(ent_out.at[i], ent_in.at[i], ent_s.at[i], ent_r.at[i], seq=other))
            )
    halo.wait_recv()

    @pl.when(s > 0)
    def _():
        age = since(16)
        for i in range(6):
            cols = slice(i * 128, i * 128 + 128)
            v = ext[:32, cols].astype(F32)
            total = taps_for(i, 4) + taps_for(i, 0) * v[16:]
            for j in range(1, 4):
                total = total + taps_for(i, j) * pltpu.roll(v, j, 0)[16:] * (age >= j).astype(F32)
            act[s, :16, cols] = silu(total).astype(BF16)

    seen = act.at[s, :, pl.ds(0, CHAN + STATES)]
    act_send = go(remote(seen, seen, misc_s.at[4], misc_r.at[4], seq=other))

    for i in range(2):
        cols = slice(i * 256, i * 256 + 256)
        at = slice(CUT_AT[last], CUT_AT[last] + CUTS[last])
        gate[:, cols] = (
            acc[:, cols] + jnp.dot(chunk(last), w_zx[at, cols], preferred_element_type=F32)
        ).astype(BF16)

    cum_c = cum_r.T
    b_own = act[s, :, CHAN : CHAN + STATES]
    c_own = act[s, :, CHAN + STATES :]
    lane = lax.broadcasted_iota(jnp.int32, (128, 128), 1)
    for r in range(2):
        rows = slice(r * 128, r * 128 + 128)
        past = slice(0, r * 128 + 128)
        scores = lax.dot_general(c_own[rows], b_own[past], NT, preferred_element_type=F32)
        scores = scores * okay[rows, past]
        for g in range(4):
            cols = slice(g * 128, g * 128 + 128)
            halves = []
            for h in (2 * g, 2 * g + 1):
                gap = jnp.minimum(cum_c[rows, h : h + 1] - cum_r[h : h + 1, past], 0.0)
                mix = jnp.exp(gap) * scores * dt_own[h : h + 1, past]
                halves.append(
                    jnp.dot(mix.astype(BF16), act[s, past, cols], preferred_element_type=F32)
                )
            acc[rows, cols] = jnp.where(lane < 64, halves[0], halves[1])

    seg_before = segment_of(bounds, jnp.full((8, LEN), LEN - 1, jnp.int32))
    carried = ((seg_own == seg_before) & (s > 0)).astype(F32)
    gain = widen(jnp.exp(cum_r) * carried)
    skips = by_head(skip_in, head_of[:1])
    for i in range(4):
        cols = slice(i * 128, i * 128 + 128)
        ent_copy[i].wait_recv()
        y_all = acc[:, cols] + jnp.dot(c_own, ent_in[i], preferred_element_type=F32) * gain[:, cols]
        y_all = y_all + skips[:, cols] * act[s, :, cols].astype(F32)
        gate[:, cols] = (y_all * silu(gate[:, cols].astype(F32))).astype(BF16)
    out_load.wait()

    def part(zz, yy, cc):
        return pl.ds(pl.multiple_of(zz * 64 + yy * 32 + cc * 16, 16), 16)

    a_copy = []
    b_copy = []
    c_copy = []

    def slab(q):
        return slice(SLAB_AT[q], SLAB_AT[q] + SLABS[q]), pl.ds(SLAB_AT[q], SLABS[q])

    def to_sib(q):
        cols, at = slab(q)
        acc[:, cols] = jnp.dot(gate[...], w_out[:, cols], preferred_element_type=F32)
        for zz in range(4):
            for yy in range(2):
                send_a[zz, yy, :, cols] = acc[part(zz, yy, oc), cols].astype(BF16)
        src, dst = send_a.at[:, :, :, at], recv_a.at[:, :, :, at]
        a_copy.append(go(remote(src, dst, rsa_s.at[q], rsa_r.at[q], tensor=sib)))

    d_copy = {}
    cols_0 = slice(0, SLABS[0])

    def line_first():
        def summed(zz, yy):
            return acc[part(zz, yy, c), cols_0] + recv_a[zz, yy, :, cols_0].astype(F32)

        for d in (2, 1, 3):
            for yy in range(2):
                send_d[d, yy] = summed((z + d) % 4, yy).astype(BF16)
            d_copy[d] = go(
                remote(send_d.at[d], recv_d.at[d], rsd_s.at[d], rsd_r.at[d], tensor=zpal[d])
            )
        for yy in range(2):
            keep[yy, :, cols_0] = summed(z, yy)
        b_copy.append(None)

    def turn():
        for d in (2, 1, 3):
            d_copy[d].wait_recv()

        def summed(yy):
            total = keep[yy, :, cols_0]
            for d in (2, 1, 3):
                total = total + recv_d[d, yy].astype(F32)
            return total

        send_e[...] = summed(oy).astype(BF16)
        d_copy[0] = go(remote(send_e, recv_e, rsd_s.at[0], rsd_r.at[0], tensor=ypal))
        keep[2, :, cols_0] = summed(y)

    def to_pal(q):
        cols, at = slab(q)
        a_copy[q].wait_recv()
        if q == 0:
            return line_first()
        for zz in range(4):
            send_b[zz, :, cols] = (
                acc[part(zz, oy, c), cols] + recv_a[zz, oy, :, cols].astype(F32)
            ).astype(BF16)
        src, dst = send_b.at[:, :, at], recv_b.at[:, :, at]
        b_copy.append(go(remote(src, dst, rsb_s.at[q], rsb_r.at[q], tensor=ypal)))
        for zz in range(4):
            keep[zz, :, cols] = acc[part(zz, y, c), cols] + recv_a[zz, y, :, cols].astype(F32)

    def to_line(q):
        cols, at = slab(q)
        b_copy[q].wait_recv()
        for d in (2, 1, 3):
            zz = (z + d) % 4
            send_c[d, :, cols] = (keep[zz, :, cols] + recv_b[zz, :, cols].astype(F32)).astype(BF16)
            src, dst = send_c.at[d, :, at], recv_c.at[d, :, at]
            c_copy.append(
                go(remote(src, dst, rsc_s.at[d, q], rsc_r.at[d, q], tensor=zpal[d]))
            )

    def finals_ready():
        step_send.wait_recv()
        act_send.wait_recv()
        cum_0 = cumulate(steps[0])
        cum_1 = cumulate(steps[1]) + cum_0[:, LEN - 1 :]
        seg_0 = segment_of(bounds, place)
        seg_1 = segment_of(bounds, place + LEN)
        ends_0 = jnp.zeros((8, LEN), F32)
        ends_1 = jnp.zeros((8, LEN), F32)
        for k in range(n_seg):
            spot_0 = (place == bounds[k] - 1).astype(F32) * cum_0
            spot_1 = (place + LEN == bounds[k] - 1).astype(F32) * cum_1
            end = jnp.sum(spot_0 + spot_1, axis=1, keepdims=True)
            ends_0 = jnp.where(seg_0 == k, end, ends_0)
            ends_1 = jnp.where(seg_1 == k, end, ends_1)
        w_0 = widen(jnp.exp(ends_0 - cum_0) * steps[0])
        w_1 = widen(jnp.exp(ends_1 - cum_1) * steps[1])
        xw_0 = (act[0, :, :CHAN].astype(F32) * w_0).astype(BF16)
        xw_1 = (act[1, :, :CHAN].astype(F32) * w_1).astype(BF16)
        b_0 = act[0, :, CHAN : CHAN + STATES]
        b_1 = act[1, :, CHAN : CHAN + STATES]
        spot = lax.broadcasted_iota(jnp.int32, (LEN, STATES), 0)
        col_0 = segment_of(bounds, spot)
        col_1 = segment_of(bounds, spot + LEN)

        def fill(k):
            m_0 = jnp.where(col_0 == k, b_0.astype(F32), 0.0).astype(BF16)
            m_1 = jnp.where(col_1 == k, b_1.astype(F32), 0.0).astype(BF16)
            finals[k] = lax.dot_general(
                xw_0, m_0, TN, preferred_element_type=F32
            ) + lax.dot_general(xw_1, m_1, TN, preferred_element_type=F32)

        return fill

    fill = None
    filled = 0
    for t in range(NR + BEHIND):
        if t < NR:
            to_sib(t)
        if 0 <= t - 1 < NR:
            to_pal(t - 1)
        if t > BEHIND:
            to_line(t - BEHIND)
        if t == BEHIND + 2:
            turn()
        if t == NR:
            fill = finals_ready()
        elif t > NR:
            for k in range(filled, min(n_seg, filled + 2)):
                fill(k)
            filled = min(n_seg, filled + 2)
    for condition, copies in guarded.values():

        @pl.when(condition)
        def _():
            for copy in copies:
                copy.wait_send()

    d_copy[0].wait_recv()
    mixed[:, cols_0] = (keep[2, :, cols_0] + recv_e[...].astype(F32)).astype(BF16)
    for q in range(1, NR):
        cols, _ = slab(q)
        total = keep[z, :, cols] + recv_b[z, :, cols].astype(F32)
        for i, d in enumerate((2, 1, 3)):
            c_copy[(q - 1) * 3 + i].wait_recv()
            total = total + recv_c[d, :, cols].astype(F32)
        mixed[:, cols] = total.astype(BF16)
    for copy in started:
        copy.wait_send()


def settle_kernel(mixed_in, finals_in, mixed, finals, sems):
    copies = [
        pltpu.make_async_copy(finals_in, finals, sems.at[0]),
        pltpu.make_async_copy(mixed_in, mixed, sems.at[1]),
    ]
    for copy in copies:
        copy.start()
    for copy in copies:
        copy.wait()


def fused_body(
    tokens,
    lengths,
    proj_zx,
    proj_bc,
    proj_dt,
    conv_x,
    conv_bc,
    bias_x,
    bias_bc,
    dt_bias,
    decay_rate,
    skip_gain,
    proj_out,
):
    n_seg = lengths.shape[0]
    bc_view = proj_bc.transpose(1, 2, 0)
    dt_view = proj_dt.T
    any_spec = pl.BlockSpec(memory_space=pl.ANY)
    vmem = pl.BlockSpec(memory_space=pltpu.VMEM)
    smem = pl.BlockSpec(memory_space=pltpu.SMEM)
    dma = pltpu.SemaphoreType.DMA
    out_shape = (
        jax.ShapeDtypeStruct((ROWS, WIDE), BF16),
        jax.ShapeDtypeStruct((n_seg, CHAN, STATES), F32),
    )
    mixed, finals = pl.pallas_call(
        layer_kernel,
        out_shape=tuple(pltpu.VMEM(o.shape, o.dtype) for o in out_shape),
        in_specs=[smem, any_spec, any_spec, any_spec, any_spec, any_spec, any_spec]
        + [any_spec, any_spec, smem, smem, smem, any_spec],
        out_specs=(vmem, vmem),
        scratch_shapes=[
            pltpu.VMEM((4, 2, 2, ROWS, WIDE), BF16),
            pltpu.VMEM((WIDE, 2, CHAN), BF16),
            pltpu.VMEM((WIDE, 2 * CHAN), BF16),
            pltpu.VMEM((2, 2, 64, WIDE), BF16),
            pltpu.VMEM((CHAN, WIDE), BF16),
            pltpu.VMEM((2, 4, 2, 64), F32),
            pltpu.VMEM((2, 2, 64), F32),
            pltpu.VMEM((LEN, CHAN), BF16),
            pltpu.VMEM((16 + LEN, CHAN + 256), BF16),
            pltpu.VMEM((2, LEN, CHAN + 256), BF16),
            pltpu.VMEM((2, 8, LEN), F32),
            pltpu.VMEM((8, WIDE), BF16),
            pltpu.VMEM((4, CHAN), F32),
            pltpu.VMEM((1, CHAN), F32),
            pltpu.VMEM((3, LEN, 128), F32),
            pltpu.VMEM((LEN, LEN), F32),
            pltpu.VMEM((LEN, WIDE), F32),
            pltpu.VMEM((4, STATES, 128), BF16),
            pltpu.VMEM((4, STATES, 128), BF16),
            pltpu.VMEM((4, ROWS, WIDE), F32),
            pltpu.VMEM((4, 2, ROWS, WIDE), BF16),
            pltpu.VMEM((4, 2, ROWS, WIDE), BF16),
            pltpu.VMEM((4, ROWS, WIDE), BF16),
            pltpu.VMEM((4, ROWS, WIDE), BF16),
            pltpu.VMEM((4, ROWS, WIDE), BF16),
            pltpu.VMEM((4, ROWS, WIDE), BF16),
            pltpu.VMEM((4, 2, ROWS, SLABS[0]), BF16),
            pltpu.VMEM((4, 2, ROWS, SLABS[0]), BF16),
            pltpu.VMEM((ROWS, SLABS[0]), BF16),
            pltpu.VMEM((ROWS, SLABS[0]), BF16),
        ]
        + [dma((8,)), dma((NQ,)), dma((4, NQ)), dma((4, NQ))]
        + [dma((4, 2, NQ)), dma((NQ,)), dma((NQ,)), dma((6,)), dma((6,)), dma((4,)), dma((4,))]
        + [dma((NR,)), dma((NR,)), dma((NR,)), dma((NR,)), dma((4, NR)), dma((4, NR)), dma((4,)), dma((4,))],
        compiler_params=pltpu.CompilerParams(
            collective_id=0, has_side_effects=True, vmem_limit_bytes=56 << 20
        ),
    )(
        lengths,
        tokens,
        proj_zx,
        bc_view,
        dt_view,
        conv_x,
        bias_x.reshape(1, CHAN),
        conv_bc,
        bias_bc,
        dt_bias,
        decay_rate,
        skip_gain,
        proj_out,
    )
    mixed, finals = pl.pallas_call(
        settle_kernel,
        out_shape=out_shape,
        in_specs=[vmem, vmem],
        out_specs=(any_spec, any_spec),
        scratch_shapes=[dma((2,))],
    )(*(pltpu.with_memory_space_constraint(o, pltpu.VMEM) for o in (mixed, finals)))
    return (mixed, finals.reshape(n_seg, 8, 64, STATES))


def solution(mesh):
    in_specs = (
        P(("seq", "tensor"), None),
        P(),
        P(None, None, "tensor"),
        P(None, None, "tensor"),
        P(None, "tensor"),
        P(None, "tensor"),
        P(None, None, "tensor"),
        P("tensor"),
        P(None, "tensor"),
        P("tensor"),
        P("tensor"),
        P("tensor"),
        P("tensor", None),
    )
    out_specs = (P(("seq", "tensor"), None), P(None, "tensor", None, None))
    small = mesh.shape["seq"] == 2 and mesh.shape["tensor"] == 16
    chosen = fused_body if small else body
    return jax.shard_map(chosen, mesh=mesh, in_specs=in_specs, out_specs=out_specs, check_vma=False)
```

```python
import jax
import jax.numpy as jnp
from jax import lax
from jax.experimental import pallas as pl
from jax.experimental.pallas import tpu as pltpu
from jax.sharding import PartitionSpec as P

GROUPS = 8


def partner_2(value, axis, bit):
    mask = 2**bit
    pairs = [(source, source ^ mask) for source in range(lax.axis_size(axis))]
    return lax.ppermute(value, axis, pairs)


def passed_along(block, axis, distance):
    devices = range(lax.axis_size(axis))
    route = [(i - distance, i) for i in devices if i - distance in devices]
    return lax.ppermute(block, axis, route)


def group_columns(bc_own, tensor_index, steps_count):
    collected = bc_own
    for bit_number in range(steps_count):
        partner = partner_2(collected, "tensor", bit_number)
        upper = tensor_index // 2**bit_number % 2
        low_first = jnp.concatenate([collected, partner], axis=2)
        high_first = jnp.concatenate([partner, collected], axis=2)
        collected = jnp.where(upper == 0, low_first, high_first)
    return collected


def body(
    tokens,
    lengths,
    proj_zx,
    proj_bc,
    proj_dt,
    conv_x,
    conv_bc,
    bias_x,
    bias_bc,
    dt_bias,
    decay_rate,
    skip_gain,
    proj_out,
):
    highest = lax.Precision.HIGHEST
    tensor_size = lax.axis_size("tensor")
    rows_dev = tokens.shape[0]
    shard_len = rows_dev * tensor_size
    seq_index = lax.axis_index("seq")
    tensor_index = lax.axis_index("tensor")
    heads_dev = decay_rate.shape[0]
    width_zx = proj_zx.shape[2]
    head_size = width_zx // heads_dev
    cols_bc = proj_bc.shape[2]
    taps_count = conv_x.shape[0]
    model_width = tokens.shape[1]
    zx_flat = proj_zx.reshape(model_width, 2 * width_zx)
    bc_flat = proj_bc.reshape(model_width, 2 * cols_bc)
    piece = lax.all_gather(tokens, "tensor", axis=0, tiled=True)
    projected = jnp.concatenate(
        [
            jnp.dot(piece, zx_flat, preferred_element_type=jnp.float32),
            jnp.dot(piece, bc_flat, preferred_element_type=jnp.float32),
            jnp.dot(piece, proj_dt, preferred_element_type=jnp.float32),
        ],
        axis=1,
    )
    gate_in = projected[:, :width_zx].astype(jnp.bfloat16)
    conv_in = projected[:, width_zx : 2 * width_zx + 2 * cols_bc].astype(jnp.bfloat16)
    step_size = jax.nn.softplus(projected[:, 2 * width_zx + 2 * cols_bc :] + dt_bias[None, :])
    row_ids = jnp.arange(shard_len, dtype=jnp.int32)
    positions = seq_index * shard_len + row_ids
    later = jnp.arange(lengths.shape[0])
    bounds = jnp.sum(jnp.where(later[None, :] <= later[:, None], lengths[None, :], 0), axis=1)
    reached = bounds[None, :] <= positions[:, None]
    segment = jnp.sum(reached.astype(jnp.int32), axis=1)
    seg_start = jnp.max(jnp.where(reached, bounds[None, :], 0), axis=1)
    edge_rows = conv_in[shard_len - (taps_count - 1) :]
    before = passed_along(edge_rows, "seq", 1)
    extended = jnp.concatenate([before, conv_in], axis=0)
    conv_taps = jnp.concatenate([conv_x, conv_bc.reshape(taps_count, 2 * cols_bc)], axis=1)
    conv_offset = jnp.concatenate([bias_x, bias_bc.reshape(2 * cols_bc)])
    convolved = jnp.zeros((shard_len, conv_taps.shape[1]), jnp.float32) + conv_offset[None, :]
    for lag_index in range(taps_count):
        lagged = extended[
            taps_count - 1 - lag_index : taps_count - 1 - lag_index + shard_len
        ].astype(jnp.float32)
        keep_mask = (positions - lag_index >= seg_start).astype(jnp.float32)
        convolved = convolved + conv_taps[lag_index][None, :] * lagged * keep_mask[:, None]
    activated = jax.nn.silu(convolved).astype(jnp.bfloat16)
    x_conv = activated[:, :width_zx]
    bc_own = activated[:, width_zx:].reshape(shard_len, 2, cols_bc)
    per_group = tensor_size // GROUPS
    steps_count = per_group.bit_length() - 1
    bc_group = group_columns(bc_own, tensor_index, steps_count).astype(jnp.float32)
    state_in_proj = bc_group[:, 0]
    state_out_proj = bc_group[:, 1]
    x_float = x_conv.astype(jnp.float32).reshape(shard_len, heads_dev, head_size)
    log_decay = -decay_rate[None, :] * step_size
    lower = (row_ids[:, None] >= row_ids[None, :]).astype(jnp.float32)
    cumulative = jnp.dot(lower, log_decay, precision=highest)
    cumulative_t = cumulative.T
    valid = (segment[:, None] == segment[None, :]) & (row_ids[:, None] >= row_ids[None, :])
    spread = cumulative_t[:, :, None] - cumulative_t[:, None, :]
    decay_matrix = jnp.where(valid[None], jnp.exp(jnp.where(valid[None], spread, 0.0)), 0.0)
    scores = jnp.dot(state_out_proj, state_in_proj.T, precision=highest)
    mixing = decay_matrix * scores[None] * step_size.T[:, None, :]
    y_local = jnp.einsum("hts,shp->thp", mixing, x_float, precision=highest)
    before_pos = seq_index * shard_len - 1
    seg_before = jnp.sum((bounds <= before_pos).astype(jnp.int32))
    carried = (segment == seg_before).astype(jnp.float32)
    entry_gain = jnp.exp(cumulative) * carried[:, None]
    n_seg = lengths.shape[0]
    end_rows = bounds - 1 - seq_index * shard_len
    inside = (end_rows >= 0) & (end_rows < shard_len)
    target_rows = jnp.concatenate([end_rows, jnp.full((1,), shard_len - 1, jnp.int32)])
    target_seg = jnp.concatenate([jnp.arange(n_seg, dtype=jnp.int32), segment[shard_len - 1 :]])
    target_ok = jnp.concatenate([inside, jnp.ones((1,), bool)])
    picker = (row_ids[None, :] == target_rows[:, None]).astype(jnp.float32)
    cum_end = jnp.dot(picker, cumulative, precision=highest)
    reach = (
        target_ok[:, None]
        & (row_ids[None, :] <= target_rows[:, None])
        & (segment[None, :] == target_seg[:, None])
    )
    gap_end = cum_end[:, :, None] - cumulative_t[None, :, :]
    end_weight = (
        jnp.where(reach[:, None, :], jnp.exp(jnp.where(reach[:, None, :], gap_end, 0.0)), 0.0)
        * step_size.T[None]
    )
    states = jnp.einsum("khs,shp,sn->khpn", end_weight, x_float, state_in_proj, precision=highest)
    end_local = states[:n_seg]
    shard_state = states[n_seg]
    end_gain = jnp.where((target_ok & (target_seg == seg_before))[:, None], jnp.exp(cum_end), 0.0)
    shard_gain = end_gain[n_seg]
    end_gain_seg = end_gain[:n_seg]
    gathered = (
        lax.all_gather(shard_gain[None], "seq", axis=0, tiled=True),
        lax.all_gather(shard_state[None], "seq", axis=0, tiled=True),
        lax.all_gather(end_gain_seg[None], "seq", axis=0, tiled=True),
        lax.all_gather(end_local[None], "seq", axis=0, tiled=True),
    )
    gains_all, states_all, egains_all, elocal_all = gathered

    def fold_step(carry, item):
        gain_now, state_now = item
        return (gain_now[:, None, None] * carry + state_now, carry)

    last_state, incoming = lax.scan(
        fold_step, jnp.zeros(shard_state.shape, jnp.float32), (gains_all, states_all)
    )
    state_entry = lax.dynamic_index_in_dim(incoming, seq_index, 0, keepdims=False)
    final_states = jnp.sum(elocal_all + egains_all[:, :, :, None, None] * incoming[:, None], axis=0)
    y_entry = (
        jnp.einsum("tn,hpn->thp", state_out_proj, state_entry, precision=highest)
        * entry_gain[:, :, None]
    )
    y_total = y_local + y_entry + skip_gain[None, :, None] * x_float
    gate_values = jax.nn.silu(gate_in.astype(jnp.float32)).reshape(shard_len, heads_dev, head_size)
    gated = (y_total * gate_values).reshape(shard_len, width_zx).astype(jnp.bfloat16)
    mixed = lax.psum_scatter(
        jnp.dot(gated, proj_out, preferred_element_type=jnp.float32),
        "tensor",
        scatter_dimension=0,
        tiled=True,
    )
    return (mixed.astype(jnp.bfloat16), final_states)


F32 = jnp.float32
BF16 = jnp.bfloat16
ROWS = 16
LEN = 256
WIDE = 4096
CHAN = 512
STATES = 128
HIGH = lax.Precision.HIGHEST
NT = (((1,), (1,)), ((), ()))
TN = (((0,), (0,)), ((), ()))
CUTS = (1536, 1536, 1024)
ROUND = (1,)
LEAD = 2
SLABS = (768, 256, 512, 512, 512, 512, 512, 256, 256)
BEHIND = 5


def starts(widths):
    return tuple(sum(widths[:i]) for i in range(len(widths)))


CUT_AT = starts(CUTS)
SLAB_AT = starts(SLABS)
NQ = len(CUTS)
NR = len(SLABS)


def remote(src, dst, send, recv, **device):
    return pltpu.make_async_remote_copy(
        src_ref=src,
        dst_ref=dst,
        send_sem=send,
        recv_sem=recv,
        device_id=device,
        device_id_type=pl.DeviceIdType.MESH,
    )


def segment_of(bounds, pos):
    total = jnp.zeros(pos.shape, jnp.int32)
    for bound in bounds:
        total = total + (bound <= pos).astype(jnp.int32)
    return total


def layer_kernel(
    lengths,
    tok_in,
    zx_in,
    bc_in,
    dt_from,
    conv_from,
    bias_from,
    conv_bc,
    bias_bc,
    dt_bias,
    rate_in,
    skip_in,
    out_in,
    mixed,
    finals,
    tok,
    zx_raw,
    w_zx,
    w_bc,
    w_out,
    t_conv,
    t_bias,
    gate,
    ext,
    act,
    steps,
    dt_in,
    conv_x,
    bias_x,
    early,
    okay,
    acc,
    ent_out,
    ent_in,
    keep,
    send_a,
    recv_a,
    send_b,
    recv_b,
    send_c,
    recv_c,
    send_d,
    recv_d,
    send_e,
    recv_e,
    load_sem,
    zx_sem,
    z_s,
    y_s,
    got,
    sib_s,
    sib_r,
    misc_s,
    misc_r,
    ent_s,
    ent_r,
    rsa_s,
    rsa_r,
    rsb_s,
    rsb_r,
    rsc_s,
    rsc_r,
    rsd_s,
    rsd_r,
):
    s = lax.axis_index("seq")
    me = lax.axis_index("tensor")
    z = me // 4
    y = (me // 2) % 2
    c = me % 2
    oy = 1 - y
    oc = 1 - c
    sib = z * 4 + y * 2 + oc
    ypal = z * 4 + oy * 2 + c
    zpal = [((z + d) % 4) * 4 + y * 2 + c for d in range(4)]
    other = 1 - s

    ext[:16] = jnp.zeros((16, CHAN + 256), BF16)
    barrier = pltpu.get_barrier_semaphore()
    for pal in [sib, ypal] + zpal[1:]:
        pl.semaphore_signal(
            barrier, inc=1, device_id={"tensor": pal}, device_id_type=pl.DeviceIdType.MESH
        )
    pl.semaphore_signal(
        barrier, inc=1, device_id={"seq": other}, device_id_type=pl.DeviceIdType.MESH
    )

    own = pltpu.make_async_copy(tok_in, tok.at[z, y, c], load_sem.at[0])
    own.start()
    zx_loads = []
    for q in range(NQ):
        rows = pl.ds(CUT_AT[q], CUTS[q])
        load = pltpu.make_async_copy(zx_in.at[rows], zx_raw.at[rows], zx_sem.at[q])
        load.start()
        zx_loads.append(load)
    bc_load = pltpu.make_async_copy(bc_in, w_bc.at[:, c], load_sem.at[1])
    bc_load.start()
    tap_load = pltpu.make_async_copy(conv_bc, t_conv.at[c], load_sem.at[2])
    tap_load.start()
    off_load = pltpu.make_async_copy(bias_bc, t_bias.at[c], load_sem.at[5])
    off_load.start()
    small_loads = [
        pltpu.make_async_copy(src, dst, load_sem.at[i])
        for i, src, dst in ((4, dt_from, dt_in), (6, conv_from, conv_x), (7, bias_from, bias_x))
    ]
    for load in small_loads:
        load.start()
    out_load = pltpu.make_async_copy(out_in, w_out, load_sem.at[3])
    out_load.start()
    pl.semaphore_wait(barrier, 6)

    started = []

    def go(copy):
        copy.start()
        started.append(copy)
        return copy

    guarded = {}

    def maybe(name, condition, copy):
        pl.when(condition)(copy.start)
        guarded.setdefault(name, (condition, []))[1].append(copy)

    def hop(zz, yy, q, send, device):
        ref = tok.at[zz, yy, c, :, pl.ds(CUT_AT[q], CUTS[q])]
        return remote(ref, ref, send, got.at[zz, yy, q], tensor=device)

    def landed(zz, yy, q):
        hop(zz, yy, q, y_s.at[0, q], ypal).wait_recv()

    mid = (z == 1) | (z == 2)
    ends = (z == 0) | (z == 3)
    first = z + 1 - 2 * (z % 2)
    second = 2 - z // 2
    third = 3 - 3 * (z // 2)
    inner = jnp.where(mid, 3 - z, first)
    line = {k: zz * 4 + y * 2 + c for k, zz in (("first", first), ("inner", inner))}

    def launch(q):
        go(hop(z, y, q, z_s.at[0, q], zpal[2]))
        go(hop(z, y, q, y_s.at[0, q], ypal))
        go(hop(z, y, q, z_s.at[1, q], line["inner"]))
        maybe("mid", mid, hop(z, y, q, z_s.at[2, q], line["first"]))

    def nearby(q):
        @pl.when(mid)
        def _():
            landed(third, y, q)

        maybe("mid", mid, hop(third, y, q, z_s.at[3, q], line["first"]))
        landed(first, y, q)
        if q not in ROUND:
            go(hop(first, y, q, y_s.at[1, q], ypal))
        landed(second, y, q)
        go(hop(second, y, q, y_s.at[2, q], ypal))

    def far(q):
        @pl.when(ends)
        def _():
            landed(third, y, q)

        go(hop(third, y, q, y_s.at[3, q], ypal))

    def across_own(q):
        landed(z, oy, q)
        if q in ROUND:
            go(hop(z, oy, q, y_s.at[1, q], line["first"]))

    def across_near(q):
        landed(first, oy, q)
        landed(second, oy, q)

    def across_far(q):
        landed(third, oy, q)
        go(share(q, c))

    def share(q, core):
        ref = tok.at[:, :, core, :, pl.ds(CUT_AT[q], CUTS[q])]
        return remote(ref, ref, sib_s.at[q], sib_r.at[q], tensor=sib)

    own.wait()
    for q in range(min(LEAD, NQ)):
        launch(q)
    bc_send = go(remote(bc_in, w_bc.at[:, c], misc_s.at[0], misc_r.at[0], tensor=sib))
    tap_send = go(remote(conv_bc, t_conv.at[c], misc_s.at[1], misc_r.at[1], tensor=sib))
    off_send = go(remote(bias_bc, t_bias.at[c], misc_s.at[5], misc_r.at[5], tensor=sib))

    def split(q, part):
        size = CUTS[q] // 4

        def run():
            if part == 0:
                zx_loads[q].wait()

            @pl.loop(0, size // 128)
            def _(j):
                at = pl.multiple_of(CUT_AT[q] + part * size + j * 128, 128)
                rows = pl.ds(at, 128)
                both = pltpu.einshape("abc->bac", zx_raw[rows])
                w_zx[rows, :CHAN] = both[0]
                w_zx[rows, CHAN:] = both[1]

        return run

    def chunk(q):
        at = slice(CUT_AT[q], CUT_AT[q] + CUTS[q])
        return tok[:, :, :, :, at].reshape(LEN, CUTS[q])

    def add_to(q, rows, cols, product):
        if q == 0:
            acc[rows, cols] = product
        else:
            acc[rows, cols] += product

    def dot_zx(q, i):
        def run():
            cols = slice(i * 256, i * 256 + 256)
            at = slice(CUT_AT[q], CUT_AT[q] + CUTS[q])
            add_to(
                q,
                slice(0, LEN),
                cols,
                jnp.dot(chunk(q), w_zx[at, cols], preferred_element_type=F32),
            )

        return run

    def dot_bc(q):
        def run():
            if q == 0:
                for load in (bc_load, tap_load, off_load, *small_loads[1:]):
                    load.wait()
                for sent in (bc_send, tap_send, off_send):
                    sent.wait_recv()
            at = slice(CUT_AT[q], CUT_AT[q] + CUTS[q])
            weights = w_bc[:, :, :, at].reshape(256, CUTS[q])
            add_to(
                q,
                slice(0, LEN),
                slice(1024, 1280),
                lax.dot_general(chunk(q), weights, NT, preferred_element_type=F32),
            )

        return run

    def dot_dt(q):
        def run():
            if q == 0:
                small_loads[0].wait()
            at = slice(CUT_AT[q], CUT_AT[q] + CUTS[q])
            add_to(
                q,
                slice(0, 8),
                slice(1280, 1280 + LEN),
                lax.dot_general(dt_in[:, at], chunk(q), NT, preferred_element_type=F32),
            )

        return run

    n_seg = lengths.shape[0]
    bounds = []
    run_sum = jnp.int32(0)
    for k in range(n_seg):
        run_sum = run_sum + lengths[k]
        bounds.append(run_sum)
    base = s * LEN

    def since(rows):
        pos = lax.broadcasted_iota(jnp.int32, (rows, 128), 0) + base
        seg_start = jnp.zeros((rows, 128), jnp.int32)
        for bound in bounds:
            seg_start = jnp.where(bound <= pos, jnp.maximum(seg_start, bound), seg_start)
        return pos - seg_start

    def ready():
        age = since(LEN)
        row = lax.broadcasted_iota(jnp.int32, (LEN, 128), 0)
        for j in range(1, 4):
            early[j - 1] = ((age >= j) & (row >= j)).astype(F32)
        ri = lax.broadcasted_iota(jnp.int32, (LEN, LEN), 0)
        ci = lax.broadcasted_iota(jnp.int32, (LEN, LEN), 1)
        same = segment_of(bounds, ci + base) == segment_of(bounds, ri + base)
        okay[...] = (same & (ri >= ci)).astype(F32)

    last = NQ - 1
    for t in range(NQ + 3):
        if t + LEAD < NQ:
            launch(t + LEAD)
        todo = []
        if t < NQ:
            todo = [split(t, part) for part in range(4)]
        if t == 0:
            todo.append(ready)
        if t >= 3:
            q = t - 3
            share(q, oc).wait_recv()
            todo += [dot_dt(q), dot_bc(q), dot_zx(q, 2), dot_zx(q, 3)]
            if q != last:
                todo += [dot_zx(q, 0), dot_zx(q, 1)]
        events = [(nearby, t), (far, t - 1), (across_own, t)]
        events += [(across_near, t - 1), (across_far, t - 2)]
        events = [(what, q) for what, q in events if 0 <= q < NQ]
        for i, (what, q) in enumerate(events):
            what(q)
            count = -(-len(todo) // (len(events) - i))
            for work in todo[:count]:
                work()
            todo = todo[count:]
        for work in todo:
            work()

    ext[16:, CHAN:] = acc[:, 1024:1280].astype(BF16)
    ext[16:, :CHAN] = acc[:, 512:1024].astype(BF16)
    halo = go(
        remote(ext.at[pl.ds(256, 16)], ext.at[pl.ds(0, 16)], misc_s.at[2], misc_r.at[2], seq=other)
    )
    head_row = lax.broadcasted_iota(jnp.int32, (8, LEN), 0)

    def by_head(ref, heads):
        values = jnp.zeros(heads.shape, F32)
        for h in range(8):
            values = jnp.where(heads == h, ref[h], values)
        return values

    rate = by_head(rate_in, head_row)
    dt_own = jax.nn.softplus(acc[:8, 1280 : 1280 + LEN] + by_head(dt_bias, head_row))
    steps[s] = dt_own
    step_send = go(remote(steps.at[s], steps.at[s], misc_s.at[3], misc_r.at[3], seq=other))
    upper = (
        lax.broadcasted_iota(jnp.int32, (LEN, LEN), 0)
        <= lax.broadcasted_iota(jnp.int32, (LEN, LEN), 1)
    ).astype(BF16)
    head_of = lax.broadcasted_iota(jnp.int32, (8, CHAN), 1) // 64
    row_of = lax.broadcasted_iota(jnp.int32, (24, CHAN), 0) % 8
    spread = (lax.broadcasted_iota(jnp.int32, (24, CHAN), 1) // 64 == row_of).astype(BF16)

    def terms(v):
        high = v.astype(BF16)
        rest = v - high.astype(F32)
        middle = rest.astype(BF16)
        return [high, middle, (rest - middle.astype(F32)).astype(BF16)]

    def cumulate(dt):
        parts = jnp.concatenate([t.astype(F32) for t in terms(-rate * dt)], axis=0).astype(BF16)
        sums = jnp.dot(parts, upper, preferred_element_type=F32)
        return sums[:8] + sums[8:16] + sums[16:]

    def widen(rows):
        parts = jnp.concatenate([t.astype(F32) for t in terms(rows)], axis=0).astype(BF16)
        return lax.dot_general(parts, spread, TN, preferred_element_type=F32)

    place = lax.broadcasted_iota(jnp.int32, (8, LEN), 1)
    seg_own = segment_of(bounds, place + base)
    seg_last = segment_of(bounds, jnp.full((8, LEN), LEN - 1, jnp.int32) + base)
    cum_r = cumulate(dt_own)
    into = jnp.exp(cum_r[:, LEN - 1 :] - cum_r) * dt_own * (seg_own == seg_last).astype(F32)
    into_wide = widen(into)

    def taps_for(i, row):
        if i < 4:
            cols = slice(i * 128, i * 128 + 128)
            return bias_x[:, cols] if row == 4 else conv_x[row : row + 1, cols]
        k = i - 4
        if row == 4:
            both = [t_bias[e, k : k + 1, :] for e in range(2)]
        else:
            both = [t_conv[e, row, k : k + 1, :] for e in range(2)]
        return jnp.concatenate(both, axis=1)

    def silu(v):
        return v * lax.logistic(v)

    ent_copy = []
    for i in (4, 0, 1, 2, 3, 5):
        cols = slice(i * 128, i * 128 + 128)
        v = ext[16:, cols].astype(F32)
        total = taps_for(i, 4) + taps_for(i, 0) * v
        for j in range(1, 4):
            total = total + taps_for(i, j) * pltpu.roll(v, j, 0) * early[j - 1]
        made = silu(total).astype(BF16)
        act[s, :, cols] = made
        if i < 4:
            x_in = (made.astype(F32) * into_wide[:, cols]).astype(BF16)
            ent_out[i] = lax.dot_general(
                act[s, :, CHAN : CHAN + STATES], x_in, TN, preferred_element_type=F32
            ).astype(BF16)
            ent_copy.append(
                go(remote(ent_out.at[i], ent_in.at[i], ent_s.at[i], ent_r.at[i], seq=other))
            )
    halo.wait_recv()

    @pl.when(s > 0)
    def _():
        age = since(16)
        for i in range(6):
            cols = slice(i * 128, i * 128 + 128)
            v = ext[:32, cols].astype(F32)
            total = taps_for(i, 4) + taps_for(i, 0) * v[16:]
            for j in range(1, 4):
                total = total + taps_for(i, j) * pltpu.roll(v, j, 0)[16:] * (age >= j).astype(F32)
            act[s, :16, cols] = silu(total).astype(BF16)

    seen = act.at[s, :, pl.ds(0, CHAN + STATES)]
    act_send = go(remote(seen, seen, misc_s.at[4], misc_r.at[4], seq=other))

    for i in range(2):
        cols = slice(i * 256, i * 256 + 256)
        at = slice(CUT_AT[last], CUT_AT[last] + CUTS[last])
        gate[:, cols] = (
            acc[:, cols] + jnp.dot(chunk(last), w_zx[at, cols], preferred_element_type=F32)
        ).astype(BF16)

    cum_c = cum_r.T
    b_own = act[s, :, CHAN : CHAN + STATES]
    c_own = act[s, :, CHAN + STATES :]
    lane = lax.broadcasted_iota(jnp.int32, (128, 128), 1)
    for r in range(2):
        rows = slice(r * 128, r * 128 + 128)
        past = slice(0, r * 128 + 128)
        scores = lax.dot_general(c_own[rows], b_own[past], NT, preferred_element_type=F32)
        scores = scores * okay[rows, past]
        for g in range(4):
            cols = slice(g * 128, g * 128 + 128)
            halves = []
            for h in (2 * g, 2 * g + 1):
                gap = jnp.minimum(cum_c[rows, h : h + 1] - cum_r[h : h + 1, past], 0.0)
                mix = jnp.exp(gap) * scores * dt_own[h : h + 1, past]
                halves.append(
                    jnp.dot(mix.astype(BF16), act[s, past, cols], preferred_element_type=F32)
                )
            acc[rows, cols] = jnp.where(lane < 64, halves[0], halves[1])

    seg_before = segment_of(bounds, jnp.full((8, LEN), LEN - 1, jnp.int32))
    carried = ((seg_own == seg_before) & (s > 0)).astype(F32)
    gain = widen(jnp.exp(cum_r) * carried)
    skips = by_head(skip_in, head_of[:1])
    for i in range(4):
        cols = slice(i * 128, i * 128 + 128)
        ent_copy[i].wait_recv()
        y_all = acc[:, cols] + jnp.dot(c_own, ent_in[i], preferred_element_type=F32) * gain[:, cols]
        y_all = y_all + skips[:, cols] * act[s, :, cols].astype(F32)
        gate[:, cols] = (y_all * silu(gate[:, cols].astype(F32))).astype(BF16)
    out_load.wait()

    def part(zz, yy, cc):
        return pl.ds(pl.multiple_of(zz * 64 + yy * 32 + cc * 16, 16), 16)

    a_copy = []
    b_copy = []
    c_copy = []

    def slab(q):
        return slice(SLAB_AT[q], SLAB_AT[q] + SLABS[q]), pl.ds(SLAB_AT[q], SLABS[q])

    def to_sib(q):
        cols, at = slab(q)
        acc[:, cols] = jnp.dot(gate[...], w_out[:, cols], preferred_element_type=F32)
        for zz in range(4):
            for yy in range(2):
                send_a[zz, yy, :, cols] = acc[part(zz, yy, oc), cols].astype(BF16)
        src, dst = send_a.at[:, :, :, at], recv_a.at[:, :, :, at]
        a_copy.append(go(remote(src, dst, rsa_s.at[q], rsa_r.at[q], tensor=sib)))

    d_copy = {}
    cols_0 = slice(0, SLABS[0])

    def line_first():
        def summed(zz, yy):
            return acc[part(zz, yy, c), cols_0] + recv_a[zz, yy, :, cols_0].astype(F32)

        for d in (2, 1, 3):
            for yy in range(2):
                send_d[d, yy] = summed((z + d) % 4, yy).astype(BF16)
            d_copy[d] = go(
                remote(send_d.at[d], recv_d.at[d], rsd_s.at[d], rsd_r.at[d], tensor=zpal[d])
            )
        for yy in range(2):
            keep[yy, :, cols_0] = summed(z, yy)
        b_copy.append(None)

    def turn():
        for d in (2, 1, 3):
            d_copy[d].wait_recv()

        def summed(yy):
            total = keep[yy, :, cols_0]
            for d in (2, 1, 3):
                total = total + recv_d[d, yy].astype(F32)
            return total

        send_e[...] = summed(oy).astype(BF16)
        d_copy[0] = go(remote(send_e, recv_e, rsd_s.at[0], rsd_r.at[0], tensor=ypal))
        keep[2, :, cols_0] = summed(y)

    def to_pal(q):
        cols, at = slab(q)
        a_copy[q].wait_recv()
        if q == 0:
            return line_first()
        for zz in range(4):
            send_b[zz, :, cols] = (
                acc[part(zz, oy, c), cols] + recv_a[zz, oy, :, cols].astype(F32)
            ).astype(BF16)
        src, dst = send_b.at[:, :, at], recv_b.at[:, :, at]
        b_copy.append(go(remote(src, dst, rsb_s.at[q], rsb_r.at[q], tensor=ypal)))
        for zz in range(4):
            keep[zz, :, cols] = acc[part(zz, y, c), cols] + recv_a[zz, y, :, cols].astype(F32)

    def to_line(q):
        cols, at = slab(q)
        b_copy[q].wait_recv()
        for d in (2, 1, 3):
            zz = (z + d) % 4
            send_c[d, :, cols] = (keep[zz, :, cols] + recv_b[zz, :, cols].astype(F32)).astype(BF16)
            src, dst = send_c.at[d, :, at], recv_c.at[d, :, at]
            c_copy.append(
                go(remote(src, dst, rsc_s.at[d, q], rsc_r.at[d, q], tensor=zpal[d]))
            )

    def finals_ready():
        step_send.wait_recv()
        act_send.wait_recv()
        cum_0 = cumulate(steps[0])
        cum_1 = cumulate(steps[1]) + cum_0[:, LEN - 1 :]
        seg_0 = segment_of(bounds, place)
        seg_1 = segment_of(bounds, place + LEN)
        ends_0 = jnp.zeros((8, LEN), F32)
        ends_1 = jnp.zeros((8, LEN), F32)
        for k in range(n_seg):
            spot_0 = (place == bounds[k] - 1).astype(F32) * cum_0
            spot_1 = (place + LEN == bounds[k] - 1).astype(F32) * cum_1
            end = jnp.sum(spot_0 + spot_1, axis=1, keepdims=True)
            ends_0 = jnp.where(seg_0 == k, end, ends_0)
            ends_1 = jnp.where(seg_1 == k, end, ends_1)
        w_0 = widen(jnp.exp(ends_0 - cum_0) * steps[0])
        w_1 = widen(jnp.exp(ends_1 - cum_1) * steps[1])
        xw_0 = (act[0, :, :CHAN].astype(F32) * w_0).astype(BF16)
        xw_1 = (act[1, :, :CHAN].astype(F32) * w_1).astype(BF16)
        b_0 = act[0, :, CHAN : CHAN + STATES]
        b_1 = act[1, :, CHAN : CHAN + STATES]
        spot = lax.broadcasted_iota(jnp.int32, (LEN, STATES), 0)
        col_0 = segment_of(bounds, spot)
        col_1 = segment_of(bounds, spot + LEN)

        def fill(k):
            m_0 = jnp.where(col_0 == k, b_0.astype(F32), 0.0).astype(BF16)
            m_1 = jnp.where(col_1 == k, b_1.astype(F32), 0.0).astype(BF16)
            finals[k] = lax.dot_general(
                xw_0, m_0, TN, preferred_element_type=F32
            ) + lax.dot_general(xw_1, m_1, TN, preferred_element_type=F32)

        return fill

    fill = None
    filled = 0
    for t in range(NR + BEHIND):
        if t < NR:
            to_sib(t)
        if 0 <= t - 1 < NR:
            to_pal(t - 1)
        if t > BEHIND:
            to_line(t - BEHIND)
        if t == BEHIND + 2:
            turn()
        if t == NR:
            fill = finals_ready()
        elif t > NR:
            for k in range(filled, min(n_seg, filled + 2)):
                fill(k)
            filled = min(n_seg, filled + 2)
    for condition, copies in guarded.values():

        @pl.when(condition)
        def _():
            for copy in copies:
                copy.wait_send()

    d_copy[0].wait_recv()
    mixed[:, cols_0] = (keep[2, :, cols_0] + recv_e[...].astype(F32)).astype(BF16)
    for q in range(1, NR):
        cols, _ = slab(q)
        total = keep[z, :, cols] + recv_b[z, :, cols].astype(F32)
        for i, d in enumerate((2, 1, 3)):
            c_copy[(q - 1) * 3 + i].wait_recv()
            total = total + recv_c[d, :, cols].astype(F32)
        mixed[:, cols] = total.astype(BF16)
    for copy in started:
        copy.wait_send()


def settle_kernel(mixed_in, finals_in, mixed, finals, sems):
    copies = [
        pltpu.make_async_copy(finals_in, finals, sems.at[0]),
        pltpu.make_async_copy(mixed_in, mixed, sems.at[1]),
    ]
    for copy in copies:
        copy.start()
    for copy in copies:
        copy.wait()


def fused_body(
    tokens,
    lengths,
    proj_zx,
    proj_bc,
    proj_dt,
    conv_x,
    conv_bc,
    bias_x,
    bias_bc,
    dt_bias,
    decay_rate,
    skip_gain,
    proj_out,
):
    n_seg = lengths.shape[0]
    bc_view = proj_bc.transpose(1, 2, 0)
    dt_view = proj_dt.T
    any_spec = pl.BlockSpec(memory_space=pl.ANY)
    vmem = pl.BlockSpec(memory_space=pltpu.VMEM)
    smem = pl.BlockSpec(memory_space=pltpu.SMEM)
    dma = pltpu.SemaphoreType.DMA
    out_shape = (
        jax.ShapeDtypeStruct((ROWS, WIDE), BF16),
        jax.ShapeDtypeStruct((n_seg, CHAN, STATES), F32),
    )
    mixed, finals = pl.pallas_call(
        layer_kernel,
        out_shape=tuple(pltpu.VMEM(o.shape, o.dtype) for o in out_shape),
        in_specs=[smem, any_spec, any_spec, any_spec, any_spec, any_spec, any_spec]
        + [any_spec, any_spec, smem, smem, smem, any_spec],
        out_specs=(vmem, vmem),
        scratch_shapes=[
            pltpu.VMEM((4, 2, 2, ROWS, WIDE), BF16),
            pltpu.VMEM((WIDE, 2, CHAN), BF16),
            pltpu.VMEM((WIDE, 2 * CHAN), BF16),
            pltpu.VMEM((2, 2, 64, WIDE), BF16),
            pltpu.VMEM((CHAN, WIDE), BF16),
            pltpu.VMEM((2, 4, 2, 64), F32),
            pltpu.VMEM((2, 2, 64), F32),
            pltpu.VMEM((LEN, CHAN), BF16),
            pltpu.VMEM((16 + LEN, CHAN + 256), BF16),
            pltpu.VMEM((2, LEN, CHAN + 256), BF16),
            pltpu.VMEM((2, 8, LEN), F32),
            pltpu.VMEM((8, WIDE), BF16),
            pltpu.VMEM((4, CHAN), F32),
            pltpu.VMEM((1, CHAN), F32),
            pltpu.VMEM((3, LEN, 128), F32),
            pltpu.VMEM((LEN, LEN), F32),
            pltpu.VMEM((LEN, WIDE), F32),
            pltpu.VMEM((4, STATES, 128), BF16),
            pltpu.VMEM((4, STATES, 128), BF16),
            pltpu.VMEM((4, ROWS, WIDE), F32),
            pltpu.VMEM((4, 2, ROWS, WIDE), BF16),
            pltpu.VMEM((4, 2, ROWS, WIDE), BF16),
            pltpu.VMEM((4, ROWS, WIDE), BF16),
            pltpu.VMEM((4, ROWS, WIDE), BF16),
            pltpu.VMEM((4, ROWS, WIDE), BF16),
            pltpu.VMEM((4, ROWS, WIDE), BF16),
            pltpu.VMEM((4, 2, ROWS, SLABS[0]), BF16),
            pltpu.VMEM((4, 2, ROWS, SLABS[0]), BF16),
            pltpu.VMEM((ROWS, SLABS[0]), BF16),
            pltpu.VMEM((ROWS, SLABS[0]), BF16),
        ]
        + [dma((8,)), dma((NQ,)), dma((4, NQ)), dma((4, NQ))]
        + [dma((4, 2, NQ)), dma((NQ,)), dma((NQ,)), dma((6,)), dma((6,)), dma((4,)), dma((4,))]
        + [dma((NR,)), dma((NR,)), dma((NR,)), dma((NR,)), dma((4, NR)), dma((4, NR)), dma((4,)), dma((4,))],
        compiler_params=pltpu.CompilerParams(
            collective_id=0, has_side_effects=True, vmem_limit_bytes=56 << 20
        ),
    )(
        lengths,
        tokens,
        proj_zx,
        bc_view,
        dt_view,
        conv_x,
        bias_x.reshape(1, CHAN),
        conv_bc,
        bias_bc,
        dt_bias,
        decay_rate,
        skip_gain,
        proj_out,
    )
    mixed, finals = pl.pallas_call(
        settle_kernel,
        out_shape=out_shape,
        in_specs=[vmem, vmem],
        out_specs=(any_spec, any_spec),
        scratch_shapes=[dma((2,))],
    )(*(pltpu.with_memory_space_constraint(o, pltpu.VMEM) for o in (mixed, finals)))
    return (mixed, finals.reshape(n_seg, 8, 64, STATES))


def solution(mesh):
    in_specs = (
        P(("seq", "tensor"), None),
        P(),
        P(None, None, "tensor"),
        P(None, None, "tensor"),
        P(None, "tensor"),
        P(None, "tensor"),
        P(None, None, "tensor"),
        P("tensor"),
        P(None, "tensor"),
        P("tensor"),
        P("tensor"),
        P("tensor"),
        P("tensor", None),
    )
    out_specs = (P(("seq", "tensor"), None), P(None, "tensor", None, None))
    small = mesh.shape["seq"] == 2 and mesh.shape["tensor"] == 16
    chosen = fused_body if small else body
    return jax.shard_map(chosen, mesh=mesh, in_specs=in_specs, out_specs=out_specs, check_vma=False)
```
